32 devices in a mesh: dp: 16 (over z, x, core), mp: 2 (over y).
Axes of the slice: x: 2, y: 2, z: 4, core: 2. Of those that a mesh axis runs over, the one named last changes fastest.
Arguments:
- hidden_in: bfloat16 [16384, 1024], P(('dp', 'mp')), may hold values from -6 to 6
- segments: int32 [16, 1024], P('dp'), may hold values from 0 to 7, never falling along the last dimension, each value on 1 to 800 neighbouring positions
- timesteps: int32 [16], P('dp'), may hold values from 0 to 4999
- time_weight: bfloat16 [1024, 1024], P('dp'), may hold values from -0.1875 to 0.1875
- qkv_weight: bfloat16 [3, 1024, 1024], P(None, 'dp', 'mp'), may hold values from -0.1875 to 0.1875
- out_weight: bfloat16 [1024, 1024], P('mp', 'dp'), may hold values from -1 to 1
- in_weight: bfloat16 [1024, 4096], P('dp', 'mp'), may hold values from -0.1875 to 0.1875
- down_weight: bfloat16 [4096, 1024], P('mp', 'dp'), may hold values from -0.09375 to 0.09375
- biases: bfloat16 [7, 1024], P(None, 'dp'), may hold values from -2 to 2
- gains: bfloat16 [2, 1024], P(None, 'dp'), may hold values from 0.099609375 to 1.8984375
- ffn_bias: bfloat16 [4096], P('dp'), may hold values from -2 to 2
- out_grad: bfloat16 [16384, 1024], P(('dp', 'mp')), may hold values from -6 to 6
Outputs:
- layer_out: bfloat16 [16384, 1024], P(('dp', 'mp'))
- input_grad: float32 [16384, 1024], P(('dp', 'mp'))
- time_weight_grad: float32 [1024, 1024], P('dp')
- qkv_weight_grad: float32 [3, 1024, 1024], P(None, 'dp', 'mp')
- out_weight_grad: float32 [1024, 1024], P('mp', 'dp')
- in_weight_grad: float32 [1024, 4096], P('dp', 'mp')
- down_weight_grad: float32 [4096, 1024], P('mp', 'dp')
- bias_grad: float32 [7, 1024], P(None, 'dp')
- gain_grad: float32 [2, 1024], P(None, 'dp')
- ffn_bias_grad: float32 [4096], P('dp')
The draws below stay inside these ranges and needn't reach their ends.
Inputs may be any that keep to these rules, and one draw needn't show every extreme that they name: `segments`: segment numbers never fall along a sequence; each document covers 1 to 800 consecutive tokens of it.
All inputs are finite; a program needn't handle non-finite values.
Results may differ from the reference program's by a relative error of at most 0.028.
Values may be sent and summed in bfloat16 or wider, within the bound.
A program may use at most 192 MiB of HBM per device.

```python
import math
import jax
import jax.numpy as jnp
import numpy as np
from jax import lax

D = 1024
H = 16
HD = 64
FF = 4096
LEN = 1024
SEG_COUNT = 8
SEG_MOST = 800
SEQS = 16
TOKENS = 16384


def plant(entries, own_key, low, largest):
    longest = entries.shape.index(max(entries.shape))
    spots = []
    for shift in (0, 1):
        where = [jax.random.randint(jax.random.fold_in(own_key, axis), (), 0, length) for axis, length in enumerate(entries.shape)]
        where[longest] = (where[longest] + shift) % entries.shape[longest]
        spots.append(tuple(where))
    return entries.at[spots[0]].set(low).at[spots[1]].set(largest)


def shard_levels(own_key, extent, shards, low, high):
    factor_of, own = 1.0, jax.random.fold_in(own_key, 6)
    for dim, parts in shards:
        heights = jnp.exp(jax.random.uniform(jax.random.fold_in(own, dim), (parts,), jnp.float32, low / len(shards), high / len(shards)))
        factor_of = factor_of * jnp.repeat(heights, extent[dim] // parts).reshape([-1 if axis == dim else 1 for axis in range(len(extent))])
    return factor_of


def profile(amount, total, most, lean):
    loads = [(1 << 20) // math.isqrt(rank ** lean) + 1 for rank in range(2, amount + 1)]
    surplus, holding = total - most - (amount - 1), [1] * (amount - 1)
    while surplus > 0:
        movable = [i for i in range(amount - 1) if holding[i] < most]
        mass, left = sum([loads[i] for i in movable]), surplus
        for i in movable:
            extra = min(most - holding[i], max(1, left * loads[i] // mass), surplus)
            holding[i] = holding[i] + extra
            surplus = surplus - extra
    return np.array([most] + holding)


def ragged(stream_key, amount, total, bound, slope):
    if amount == 2:
        one = jax.random.randint(stream_key, (), max(1, total - bound), min(bound, total - 1) + 1)
        return jnp.stack([one, total - one])
    sizes = jnp.asarray(profile(amount, total, bound, slope), jnp.int32)
    couples = (amount - 1) // 2
    donor, taker = sizes[1:1 + 2 * couples:2], sizes[2:2 + 2 * couples:2]
    margin = jnp.minimum(donor - 1, bound - taker)
    shifted = jax.random.randint(jax.random.fold_in(stream_key, 1), (couples,), 0, 1 << 20) % (margin + 1)
    sizes = sizes.at[1:1 + 2 * couples:2].set(donor - shifted).at[2:2 + 2 * couples:2].set(taker + shifted)
    return sizes[jax.random.permutation(jax.random.fold_in(stream_key, 2), amount)]


def bell_draw(own_key, dims, spread, limit, cuts=(), kind=jnp.bfloat16):
    values = spread * jax.random.normal(own_key, dims, jnp.float32)
    if cuts:
        values = values * shard_levels(own_key, dims, cuts, -0.22, 0.18)
    return jnp.clip(values, -limit, limit).astype(kind)


def setup_inputs(seed: int = 0) -> dict:
    keys = jax.random.split(jax.random.key(seed), 13)
    return {
        "hidden_in": bell_draw(keys[0], (TOKENS, D), 1.0, 6.0, ((0, 32),)),
        "segments": jax.vmap(lambda own: jnp.searchsorted(jnp.cumsum(ragged(own, SEG_COUNT, LEN, SEG_MOST, 2)), jnp.arange(LEN), side="right"))(jax.random.split(keys[1], SEQS)).reshape((SEQS, LEN)).astype(jnp.int32),
        "timesteps": plant(jax.random.randint(keys[2], (SEQS,), 0, 5000), jax.random.fold_in(keys[2], 1), 0, 4999).astype(jnp.int32),
        "time_weight": bell_draw(keys[3], (D, D), D ** -0.5, 0.1875, ((0, 16),)),
        "qkv_weight": bell_draw(keys[4], (3, D, D), D ** -0.5, 0.1875, ((1, 16), (2, 2))),
        "out_weight": bell_draw(keys[5], (D, D), (max(D // 32, 8)) ** -0.5, 1.0, ((0, 2), (1, 16))),
        "in_weight": bell_draw(keys[6], (D, FF), D ** -0.5, 0.1875, ((0, 16), (1, 2))),
        "down_weight": bell_draw(keys[7], (FF, D), FF ** -0.5, 0.09375, ((0, 2), (1, 16))),
        "biases": bell_draw(keys[8], (7, D), 0.3, 2.0, ((1, 16),)),
        "gains": jnp.clip(1.0 + 0.18 * jax.random.normal(keys[9], (2, D), jnp.float32), 0.099609375, 1.8984375).astype(jnp.bfloat16),
        "ffn_bias": bell_draw(keys[10], (FF,), 0.3, 2.0, ((0, 16),)),
        "out_grad": bell_draw(keys[11], (TOKENS, D), 1.0, 6.0, ((0, 32),)),
    }


@jax.custom_vjp
def low(v):
    return lax.optimization_barrier(v.astype(jnp.bfloat16)).astype(jnp.float32)

@jax.custom_vjp
def low_back(v):
    return v

def low_keep(v):
    return (low(v), None)

def low_pass(kept, grad):
    return (grad,)

def back_keep(v):
    return (v, None)

def back_low(kept, grad):
    return (low(grad),)
low.defvjp(low_keep, low_pass)
low_back.defvjp(back_keep, back_low)
eps = 1e-05
neg_big = -1000000000.0
highest = lax.Precision.HIGHEST

def product(left, right):
    return jnp.dot(left, right, precision=highest)

def time_features(step_ids, model_width):
    half_width = model_width // 2
    frequency = jnp.exp(jnp.arange(half_width, dtype=jnp.float32) * (-math.log(10000.0) / half_width))
    angles = step_ids.astype(jnp.float32)[:, None] * frequency[None, :]
    return jnp.concatenate([jnp.sin(angles), jnp.cos(angles)], axis=1)

def layer_norm(array_in, gain_row, shift_row):
    row_mean = lax.optimization_barrier(jnp.mean(array_in, axis=-1, keepdims=True))
    centered = array_in - row_mean
    variance = lax.optimization_barrier(jnp.mean(centered * centered, axis=-1, keepdims=True))
    return centered * lax.rsqrt(variance + eps) * gain_row + shift_row

def sequence_layer(weights, inputs, doc_ids, time_row):
    qkv_w, out_w, in_w, down_w, bias_all, gain_all, ffn_b = weights
    embedded = inputs + time_row[None, :]
    embed_low = low(embedded)
    queries = low(low_back(product(embed_low, qkv_w[0])) + bias_all[1])
    key_rows = low(low_back(product(embed_low, qkv_w[1])))
    values = low(low_back(product(embed_low, qkv_w[2])) + bias_all[2])
    same_doc = doc_ids[:, None] == doc_ids[None, :]
    score_scale = 1.0 / math.sqrt(HD)

    def head_attention(packet):
        head_q, head_k, head_v = packet
        raw_score = low_back(product(head_q, head_k.T))
        scores = jnp.where(same_doc, raw_score * score_scale, neg_big)
        row_max = lax.optimization_barrier(jnp.max(scores, axis=-1, keepdims=True))
        exp_score = jnp.exp(scores - row_max)
        attn_prob = exp_score / lax.optimization_barrier(jnp.sum(exp_score, axis=-1, keepdims=True))
        return product(low(attn_prob), head_v)

    def split_heads(array_in):
        return array_in.reshape(LEN, H, HD).transpose(1, 0, 2)
    mixed_heads = lax.map(jax.checkpoint(head_attention), (split_heads(queries), split_heads(key_rows), split_heads(values)))
    mixed_heads = low(low_back(mixed_heads.transpose(1, 0, 2).reshape(LEN, D)))
    attn_total = low_back(product(mixed_heads, out_w)) + bias_all[3]
    middle = layer_norm(embedded + attn_total, gain_all[0], bias_all[4])
    middle_low = low(middle)
    pre_act = low_back(product(middle_low, in_w)) + ffn_b
    hidden_act = low(jax.nn.gelu(pre_act, approximate=False))
    ffn_total = low_back(product(hidden_act, down_w)) + bias_all[5]
    return layer_norm(middle + ffn_total, gain_all[1], bias_all[6])

def reference(hidden_in, segments, timesteps, time_weight, qkv_weight, out_weight, in_weight, down_weight, biases, gains, ffn_bias, out_grad):
    feature = low(time_features(timesteps, D))
    inputs = hidden_in.astype(jnp.float32).reshape(SEQS, LEN, D)
    params = tuple((weight.astype(jnp.float32) for weight in (time_weight, qkv_weight, out_weight, in_weight, down_weight, biases, gains, ffn_bias)))

    def forward(inputs_now, params_now):
        time_w = params_now[0]
        layer_weights = params_now[1:]
        time_rows = product(feature, time_w) + layer_weights[4][0]

        def per_sequence(packet):
            return sequence_layer(layer_weights, packet[0], packet[1], packet[2])
        return lax.map(jax.checkpoint(per_sequence), (inputs_now, segments, time_rows))
    result, pullback = jax.vjp(forward, inputs, params)
    grad_in, grad_params = pullback(out_grad.astype(jnp.float32).reshape(SEQS, LEN, D))
    return (result.reshape(TOKENS, D).astype(jnp.bfloat16), grad_in.reshape(TOKENS, D), grad_params[0], grad_params[1], grad_params[2], grad_params[3], grad_params[4], grad_params[5], grad_params[6], grad_params[7])
```

```python
import functools
import math

import jax
import jax.numpy as jnp
from jax import lax
from jax.experimental import pallas as pl
from jax.experimental.pallas import tpu as pltpu
from jax.sharding import PartitionSpec as P

HD = 64
eps = 1e-05
neg_big = -1000000000.0
MESH = pl.DeviceIdType.MESH
F32, BF16 = jnp.float32, jnp.bfloat16
VMEM_LIMIT = 64000000


def dg(left, right, left_dim, right_dim):
    return lax.dot_general(
        left, right, (((left_dim,), (right_dim,)), ((), ())), preferred_element_type=F32
    )


def place():
    i, y = lax.axis_index("dp"), lax.axis_index("mp")
    return i // 4, (i // 2) % 2, i % 2, y


def z_places(z):
    return [(z // 2) * 2 + 1 - z % 2, (z + 2) % 4, 3 - z]


def peers(z, x, c, y):
    def at(z_, x_, c_, y_):
        return ((z_ * 2 + x_) * 2 + c_, y_)

    return {
        "z": [at(p, x, c, y) for p in z_places(z)],
        "x": at(z, 1 - x, c, y),
        "y": at(z, x, c, 1 - y),
        "c": at(z, x, 1 - c, y),
    }


def enter(near):
    barrier = pltpu.get_barrier_semaphore()
    everyone = near["z"] + [near["x"], near["y"], near["c"]]
    for one in everyone:
        pl.semaphore_signal(barrier, inc=1, device_id=one, device_id_type=MESH)
    pl.semaphore_wait(barrier, len(everyone))


class Wire:
    def __init__(self, send_sems, recv_sems):
        self.send_sems, self.recv_sems, self.used, self.open = send_sems, recv_sems, 0, []

    def send(self, src, dst, to):
        k = self.used
        self.used += 1
        copy = pltpu.make_async_remote_copy(
            src_ref=src,
            dst_ref=dst,
            send_sem=self.send_sems.at[k],
            recv_sem=self.recv_sems.at[k],
            device_id=to,
            device_id_type=MESH,
        )
        copy.start()
        self.open.append(copy)
        return copy

    def close(self):
        assert self.used == self.send_sems.shape[0] == self.recv_sems.shape[0]
        for copy in self.open:
            copy.wait_send()


def gather_dp(wire, near, here, shard, whole):
    z, x, c, y = here
    own = whole.at[z, x, c]
    from_z = [wire.send(shard, own, to) for to in near["z"]]
    late = [wire.send(shard, own, near["c"])]
    yield
    for k in from_z:
        k.wait_recv()
    ref = whole.at[:, x, c]
    from_x = wire.send(ref, ref, near["x"])
    for p in z_places(z):
        ref = whole.at[p, x, c]
        late.append(wire.send(ref, ref, near["c"]))
    yield
    from_x.wait_recv()
    ref = whole.at[:, 1 - x, c]
    late.append(wire.send(ref, ref, near["c"]))
    yield
    for k in late:
        k.wait_recv()


def gather_all(wire, near, here, shard, whole, lo, mid, hi):
    z, x, c, y = here
    a, b, ab = pl.ds(lo, mid - lo), pl.ds(mid, hi - mid), pl.ds(lo, hi - lo)
    own = whole.at[y, z, x, c, :, ab]
    from_z = [wire.send(shard.at[:, ab], own, to) for to in near["z"]]
    late = [wire.send(shard.at[:, ab], own, near["c"])]
    yield
    for k in from_z:
        k.wait_recv()
    ref = whole.at[y, :, x, c, :, a]
    from_x_a = wire.send(ref, ref, near["x"])
    ref = whole.at[y, :, x, c, :, b]
    from_y_b = wire.send(ref, ref, near["y"])
    for p in z_places(z):
        ref = whole.at[y, p, x, c, :, ab]
        late.append(wire.send(ref, ref, near["c"]))
    yield
    from_x_a.wait_recv()
    ref = whole.at[y, :, :, c, :, a]
    from_y_a = wire.send(ref, ref, near["y"])
    from_y_b.wait_recv()
    ref = whole.at[:, :, x, c, :, b]
    from_x_b = wire.send(ref, ref, near["x"])
    for ref in (whole.at[y, :, 1 - x, c, :, a], whole.at[1 - y, :, x, c, :, b]):
        late.append(wire.send(ref, ref, near["c"]))
    yield
    from_y_a.wait_recv()
    from_x_b.wait_recv()
    for ref in (whole.at[1 - y, :, :, c, :, a], whole.at[:, :, 1 - x, c, :, b]):
        late.append(wire.send(ref, ref, near["c"]))
    yield
    for k in late:
        k.wait_recv()


def parts_of(width, parts):
    step = width // parts
    return [(p * step, p * step + step // 2, (p + 1) * step) for p in range(parts)]


def stagger(streams, ahead=0):
    for depth in range(ahead, len(streams) + 6):
        for k, s in enumerate(streams):
            if k <= depth:
                next(s, None)


def gather_kernel(
    v_ref, o_ref, i_ref, d_ref, h_ref, v_all, o_all, i_all, d_all, h_all, send_sems, recv_sems, local_sems
):
    here = place()
    z, x, c, y = here
    near = peers(*here)
    enter(near)
    wire = Wire(send_sems, recv_sems)
    first = gather_dp(wire, near, here, v_ref, v_all)
    next(first)
    from_y = wire.send(h_ref, h_all.at[y], near["y"])
    kept = (
        (v_ref, v_all.at[z, x, c]),
        (o_ref, o_all.at[y, z, x, c]),
        (i_ref, i_all.at[y, z, x, c]),
        (d_ref, d_all.at[y, z, x, c]),
        (h_ref, h_all.at[y]),
    )
    own = [pltpu.make_async_copy(s, d, local_sems.at[k]) for k, (s, d) in enumerate(kept)]
    for k in own:
        k.start()
    streams = [
        gather_all(wire, near, here, shard, whole, *cut)
        for shard, whole, parts in ((o_ref, o_all, 1), (i_ref, i_all, 2), (d_ref, d_all, 2))
        for cut in parts_of(shard.shape[1], parts)
    ]
    for s in streams:
        next(s)
    for k in own:
        k.wait()
    stagger([first] + streams)
    from_y.wait_recv()
    wire.close()


def gather_weights(v, o, i, d, h):
    def whole(a, lead):
        return jax.ShapeDtypeStruct(lead + a.shape, a.dtype)

    dp3 = (4, 2, 2)
    copies = 9 + 15 * 5 + 1
    return pl.pallas_call(
        gather_kernel,
        name="gather_weights",
        out_shape=[
            whole(v, dp3),
            whole(o, (2,) + dp3),
            whole(i, (2,) + dp3),
            whole(d, (2,) + dp3),
            whole(h, (2,)),
        ],
        in_specs=[pl.BlockSpec(memory_space=pltpu.VMEM)] * 5,
        out_specs=[pl.BlockSpec(memory_space=pl.ANY)] * 5,
        scratch_shapes=[
            pltpu.SemaphoreType.DMA((copies,)),
            pltpu.SemaphoreType.DMA((copies,)),
            pltpu.SemaphoreType.DMA((5,)),
        ],
        compiler_params=pltpu.CompilerParams(
            collective_id=0, has_side_effects=True, vmem_limit_bytes=16 * 1024 * 1024
        ),
    )(v, o, i, d, h)


def add_blocks(dst, left, right, lead):
    count = math.prod(lead)

    def one(t, _):
        at = []
        for n in reversed(lead):
            at.append(t % n)
            t = t // n
        at = tuple(reversed(at))
        dst[at] = (left[at].astype(F32) + right[at].astype(F32)).astype(dst.dtype)
        return 0

    lax.fori_loop(0, count, one, 0)


def reduce_dp(wire, near, here, grad, rc, rx, rz, out):
    z, x, c, y = here
    from_c = wire.send(grad.at[:, :, 1 - c], rc, near["c"])
    yield
    from_c.wait_recv()
    add_blocks(rc, grad.at[:, :, c], rc, (4, 2))
    from_x = wire.send(rc.at[:, 1 - x], rx, near["x"])
    yield
    from_x.wait_recv()
    add_blocks(rx, rc.at[:, x], rx, (4,))
    from_z = [wire.send(rx.at[p], rz.at[j], to) for j, (p, to) in enumerate(zip(z_places(z), near["z"]))]
    yield
    for k in from_z:
        k.wait_recv()
    out[...] = ((rx[z].astype(F32) + rz[0].astype(F32)) + rz[1].astype(F32)) + rz[2].astype(F32)


def reduce_all(wire, near, here, grad, rc, ya, xb, xa, yb, rz, out, lo, mid, hi):
    z, x, c, y = here
    a, b, ab = pl.ds(lo, mid - lo), pl.ds(mid, hi - mid), pl.ds(lo, hi - lo)
    half_a, half_b = pl.ds(0, mid - lo), pl.ds(mid - lo, hi - mid)
    from_c = wire.send(grad.at[:, :, :, 1 - c, :, ab], rc, near["c"])
    yield
    from_c.wait_recv()
    add_blocks(rc, grad.at[:, :, :, c, :, ab], rc, (2, 4, 2))
    from_y_a = wire.send(rc.at[1 - y, :, :, :, half_a], ya, near["y"])
    from_x_b = wire.send(rc.at[:, :, 1 - x, :, half_b], xb, near["x"])
    yield
    from_y_a.wait_recv()
    add_blocks(ya, rc.at[y, :, :, :, half_a], ya, (4, 2))
    from_x_a = wire.send(ya.at[:, 1 - x], xa, near["x"])
    from_x_b.wait_recv()
    add_blocks(xb, rc.at[:, :, x, :, half_b], xb, (2, 4))
    from_y_b = wire.send(xb.at[1 - y], yb, near["y"])
    yield
    from_x_a.wait_recv()
    add_blocks(xa, ya.at[:, x], xa, (4,))
    from_y_b.wait_recv()
    add_blocks(yb, xb.at[y], yb, (4,))
    from_z = []
    for j, (p, to) in enumerate(zip(z_places(z), near["z"])):
        from_z.append(wire.send(xa.at[p], rz.at[j, :, half_a], to))
        from_z.append(wire.send(yb.at[p], rz.at[j, :, half_b], to))
    yield
    for k in from_z:
        k.wait_recv()
    for acc, half, cols in ((xa, half_a, a), (yb, half_b, b)):
        out[:, cols] = (
            (acc[z].astype(F32) + rz[0, :, half].astype(F32)) + rz[1, :, half].astype(F32)
        ) + rz[2, :, half].astype(F32)


def reduce_small(wire, near, here, mine, sums, got, out):
    k = wire.send(mine, got.at[0], near["c"])
    yield
    k.wait_recv()
    sums[0] = mine[...] + got[0]
    k = wire.send(sums.at[0], got.at[1], near["x"])
    yield
    k.wait_recv()
    sums[1] = sums[0] + got[1]
    k = wire.send(sums.at[1], got.at[2], near["y"])
    yield
    k.wait_recv()
    sums[2] = sums[1] + got[2]
    last = [wire.send(sums.at[2], got.at[3 + j], to) for j, to in enumerate(near["z"])]
    yield
    for k in last:
        k.wait_recv()
    out[...] = ((sums[2] + got[3]) + got[4]) + got[5]


ALL_CUTS = (1, 2, 2)


def reduce_kernel(v_g, o_g, i_g, d_g, x_part, small, v_out, o_out, i_out, d_out, x_got, s_out, *rest):
    here = place()
    z, x, c, y = here
    near = peers(*here)
    enter(near)
    rest = list(rest)
    send_sems, recv_sems = rest[0], rest[1]
    scratch = iter(rest[2:])
    wire = Wire(send_sems, recv_sems)
    sums, got = next(scratch), next(scratch)
    tiny = reduce_small(wire, near, here, small, sums, got, s_out)
    from_y = wire.send(x_part.at[1 - y], x_got, near["y"])
    streams = []
    for grad, out, parts in ((d_g, d_out, ALL_CUTS[2]), (i_g, i_out, ALL_CUTS[1]), (o_g, o_out, ALL_CUTS[0])):
        for cut in parts_of(out.shape[1], parts):
            bufs = [next(scratch) for _ in range(6)]
            streams.append(reduce_all(wire, near, here, grad, *bufs, out, *cut))
    bufs = [next(scratch) for _ in range(3)]
    streams.append(reduce_dp(wire, near, here, v_g, *bufs, v_out))
    stagger([tiny] + streams)
    from_y.wait_recv()
    wire.close()


def reduce_grads(v_g, o_g, i_g, d_g, x_part, small):
    rows = v_g.shape[-2]
    out = [jax.ShapeDtypeStruct((rows, a.shape[-1]), F32) for a in (v_g, o_g, i_g, d_g)]
    scratch = [pltpu.VMEM((3,) + small.shape, F32), pltpu.VMEM((6,) + small.shape, F32)]
    copies = 6 + 1
    for a, parts in ((d_g, ALL_CUTS[2]), (i_g, ALL_CUTS[1]), (o_g, ALL_CUTS[0])):
        n = a.shape[-1] // parts
        h = n // 2
        for _ in range(parts):
            copies += 11
            scratch += [
                pltpu.VMEM(s, BF16)
                for s in (
                    (2, 4, 2, rows, n),
                    (4, 2, rows, h),
                    (2, 4, rows, h),
                    (4, rows, h),
                    (4, rows, h),
                    (3, rows, n),
                )
            ]
    n = v_g.shape[-1]
    copies += 5
    scratch += [pltpu.VMEM(s, BF16) for s in ((4, 2, rows, n), (4, rows, n), (3, rows, n))]
    vm = pl.BlockSpec(memory_space=pltpu.VMEM)
    hbm = pl.BlockSpec(memory_space=pl.ANY)
    return pl.pallas_call(
        reduce_kernel,
        name="reduce_grads",
        out_shape=out
        + [jax.ShapeDtypeStruct(x_part.shape[1:], x_part.dtype), jax.ShapeDtypeStruct(small.shape, F32)],
        in_specs=[vm] * 4 + [hbm, vm],
        out_specs=[vm] * 4 + [hbm, vm],
        scratch_shapes=[pltpu.SemaphoreType.DMA((copies,)), pltpu.SemaphoreType.DMA((copies,))] + scratch,
        compiler_params=pltpu.CompilerParams(
            collective_id=1, has_side_effects=True, vmem_limit_bytes=VMEM_LIMIT
        ),
    )(v_g, o_g, i_g, d_g, x_part, small)


def attend_kernel(tile, q_ref, k_ref, v_ref, sr_ref, sc_ref, o_ref, l_ref):
    length, width = q_ref.shape

    def step(t, _):
        rows = pl.ds(pl.multiple_of(t * tile, tile), tile)
        same = sc_ref[:, 0:1] == sr_ref[:, rows]
        for h in range(width // HD):
            cols = slice(h * HD, h * HD + HD)
            scores = dg(k_ref[:, cols], q_ref[rows, cols], 1, 1) * (1.0 / math.sqrt(HD))
            scores = jnp.where(same, scores, neg_big)
            row_max = jnp.max(scores, axis=0, keepdims=True)
            prob = jnp.exp(scores - row_max)
            total = jnp.sum(prob, axis=0, keepdims=True)
            mixed = dg(v_ref[:, cols], prob.astype(BF16), 0, 0) / total
            o_ref[rows, cols] = mixed.T.astype(BF16)
            l_ref[0, h : h + 1, rows] = row_max + jnp.log(total)
        return 0

    lax.fori_loop(0, length // tile, step, 0)


def attend_specs(length, heads_pairs):
    def col(k):
        return pl.BlockSpec((length, 2 * HD), lambda i, k=k: (0, k * heads_pairs + i))

    stats = pl.BlockSpec((1, 2, length), lambda i: (i, 0, 0))
    seg_row = pl.BlockSpec((1, length), lambda i: (0, 0))
    seg_col = pl.BlockSpec((length, 128), lambda i: (0, 0))
    return col, stats, seg_row, seg_col


def attend(qkv, segments):
    length = qkv.shape[0]
    pairs = qkv.shape[1] // 3 // (2 * HD)
    col, stats, seg_row, seg_col = attend_specs(length, pairs)
    return pl.pallas_call(
        functools.partial(attend_kernel, min(512, length)),
        name="attend",
        grid=(pairs,),
        in_specs=[col(0), col(1), col(2), seg_row, seg_col],
        out_specs=[col(0), stats],
        out_shape=[
            jax.ShapeDtypeStruct((length, pairs * 2 * HD), BF16),
            jax.ShapeDtypeStruct((pairs, 2, length), F32),
        ],
        cost_estimate=pl.CostEstimate(
            flops=8 * length * length * HD * pairs, bytes_accessed=4 * length * pairs * 256, transcendentals=0
        ),
    )(qkv, qkv, qkv, segments, jnp.broadcast_to(segments.reshape(length, 1), (length, 128)))


def attend_back_kernel(
    tile, q_ref, k_ref, v_ref, d_ref, o_ref, l_ref, sr_ref, sc_ref, dq_ref, dk_ref, dv_ref
):
    length, width = q_ref.shape
    scale = 1.0 / math.sqrt(HD)
    dk_ref[...] = jnp.zeros_like(dk_ref)
    dv_ref[...] = jnp.zeros_like(dv_ref)

    def step(t, _):
        rows = pl.ds(pl.multiple_of(t * tile, tile), tile)
        same = sc_ref[:, 0:1] == sr_ref[:, rows]
        for h in range(width // HD):
            cols = slice(h * HD, h * HD + HD)
            keys, q_rows, d_rows = k_ref[:, cols], q_ref[rows, cols], d_ref[rows, cols]
            delta = jnp.sum(
                (d_rows.astype(F32) * o_ref[rows, cols].astype(F32)).T, axis=0, keepdims=True
            )
            scores = dg(keys, q_rows, 1, 1) * scale
            prob = jnp.where(same, jnp.exp(scores - l_ref[0, h : h + 1, rows]), 0.0)
            d_prob = dg(v_ref[:, cols], d_rows, 1, 1)
            d_score = (prob * (d_prob - delta) * scale).astype(BF16)
            dv_ref[:, cols] += dg(prob.astype(BF16), d_rows, 1, 0)
            dk_ref[:, cols] += dg(d_score, q_rows, 1, 0)
            dq_ref[rows, cols] = dg(d_score, keys, 0, 0)
        return 0

    lax.fori_loop(0, length // tile, step, 0)


def attend_back(qkv, d_mixed, mixed, stats_in, segments):
    length = qkv.shape[0]
    pairs = qkv.shape[1] // 3 // (2 * HD)
    col, stats, seg_row, seg_col = attend_specs(length, pairs)
    return pl.pallas_call(
        functools.partial(attend_back_kernel, min(512, length)),
        name="attend_back",
        grid=(pairs,),
        in_specs=[col(0), col(1), col(2), col(0), col(0), stats, seg_row, seg_col],
        out_specs=[col(0)] * 3,
        out_shape=[jax.ShapeDtypeStruct((length, pairs * 2 * HD), F32)] * 3,
        cost_estimate=pl.CostEstimate(
            flops=20 * length * length * HD * pairs, bytes_accessed=8 * length * pairs * 256, transcendentals=0
        ),
    )(qkv, qkv, qkv, d_mixed, mixed, stats_in, segments, jnp.broadcast_to(segments.reshape(length, 1), (length, 128)))


def time_features(step_ids, model_width):
    half_width = model_width // 2
    frequency = jnp.exp(
        jnp.arange(half_width, dtype=F32) * (-math.log(10000.0) / half_width)
    )
    angles = step_ids.astype(F32)[:, None] * frequency[None, :]
    return jnp.concatenate([jnp.sin(angles), jnp.cos(angles)], axis=1)


def normalize(array_in):
    row_mean = jnp.mean(array_in, axis=-1, keepdims=True)
    centered = array_in - row_mean
    variance = jnp.mean(centered * centered, axis=-1, keepdims=True)
    inv_std = lax.rsqrt(variance + eps)
    return (centered * inv_std, inv_std)


def norm_back(grad_rows, unit_rows, inv_std, gain_row):
    d_unit = grad_rows * gain_row
    return inv_std * (
        d_unit
        - jnp.mean(d_unit, axis=-1, keepdims=True)
        - unit_rows * jnp.mean(d_unit * unit_rows, axis=-1, keepdims=True)
    )


def exact_gelu(array_in):
    return jax.nn.gelu(array_in, approximate=False)


def ein(spec, left, right):
    return jnp.einsum(spec, left, right, preferred_element_type=F32)


def on_device(
    hidden_in,
    segments,
    timesteps,
    time_weight,
    qkv_weight,
    out_weight,
    in_weight,
    down_weight,
    biases,
    gains,
    ffn_bias,
    out_grad,
    *,
    dp,
    mp,
):
    own_rows, width = hidden_in.shape
    length = segments.shape[1]
    rows = time_weight.shape[0]
    cols = qkv_weight.shape[2]
    hidden = in_weight.shape[1]
    dp_index, mp_index = lax.axis_index("dp"), lax.axis_index("mp")
    fast = (dp, mp) == (16, 2)

    bias_count = biases.shape[0] + gains.shape[0] + ffn_bias.shape[0] // rows
    v_shard = jnp.concatenate(
        [
            qkv_weight[0],
            qkv_weight[1],
            qkv_weight[2],
            time_weight,
            biases.T,
            gains.T,
            ffn_bias.reshape(rows, -1),
            jnp.broadcast_to(jnp.stack([timesteps // 64, timesteps % 64], axis=1), (rows, 2)).astype(BF16),
            jnp.zeros((rows, 126 - bias_count), BF16),
        ],
        axis=1,
    )
    shards = (v_shard, out_weight.T, in_weight, down_weight.T, hidden_in)
    if fast:
        v_all, o_all, i_all, d_all, h_all = gather_weights(*shards)
    else:
        v_all = lax.all_gather(shards[0], "dp", axis=0)
        o_all, i_all, d_all = (
            lax.all_gather(lax.all_gather(a, "dp", axis=0), "mp", axis=0) for a in shards[1:4]
        )
        h_all = lax.all_gather(hidden_in, "mp", axis=0)
    v_all = v_all.reshape(width, -1)
    o_all, i_all, d_all = (a.reshape(mp, width, -1) for a in (o_all, i_all, d_all))
    h_all = h_all.reshape(length, width)

    qkv_w = v_all[:, : 3 * cols]
    time_w = v_all[:, 3 * cols : 3 * cols + width]
    params = v_all[:, 3 * cols + width :].astype(F32)
    bias_all = params[:, :7].T
    gain_all = params[:, 7:9].T
    ffn_b = params[:, 9 : 9 + ffn_bias.shape[0] // rows].reshape(mp, hidden)

    feature = time_features(timesteps, width).astype(BF16)
    time_row = jnp.dot(feature, time_w, preferred_element_type=F32) + bias_all[0]
    embedded = hidden_in.astype(F32) + time_row
    embed_low = (h_all.astype(F32) + time_row).astype(BF16)
    column = mp_index * cols
    bias_qkv = jnp.concatenate(
        [
            lax.dynamic_slice_in_dim(bias_all[1], column, cols),
            jnp.zeros((cols,), F32),
            lax.dynamic_slice_in_dim(bias_all[2], column, cols),
        ]
    )
    qkv = (jnp.dot(embed_low, qkv_w, preferred_element_type=F32) + bias_qkv).astype(BF16)
    mixed_heads, stats = attend(qkv, segments)

    def heads_to_rows(array_in):
        cut = array_in.reshape(mp, own_rows, cols)
        return trade(cut)

    def rows_to_heads(array_in):
        return trade(array_in).reshape(length, cols)

    def trade(cut):
        if mp == 2:
            far = lax.ppermute(
                lax.dynamic_index_in_dim(cut, 1 - mp_index, 0, False), "mp", [(0, 1), (1, 0)]
            )
            own = jnp.arange(2)[:, None, None] == mp_index
            return jnp.where(own, cut, far[None])
        return lax.all_to_all(cut, "mp", 0, 0, tiled=True)

    mixed = heads_to_rows(mixed_heads)
    attn_total = ein("yrk,ynk->rn", mixed, o_all)
    unit_one, inv_one = normalize(embedded + attn_total + bias_all[3])
    middle = unit_one * gain_all[0] + bias_all[4]
    middle_low = middle.astype(BF16)
    pre_act = ein("rd,ydf->yrf", middle_low, i_all) + ffn_b[:, None, :]
    hidden_act = exact_gelu(pre_act).astype(BF16)
    ffn_total = ein("yrf,ynf->rn", hidden_act, d_all)
    unit_two, inv_two = normalize(middle + ffn_total + bias_all[5])
    layer_out = (unit_two * gain_all[1] + bias_all[6]).astype(BF16)

    grad_out = out_grad.astype(F32)
    gain_two_part = jnp.sum(grad_out * unit_two, axis=0)
    shift_two_part = jnp.sum(grad_out, axis=0)
    d_pre_two = norm_back(grad_out, unit_two, inv_two, gain_all[1])
    bias_five_part = jnp.sum(d_pre_two, axis=0)
    d_ffn = d_pre_two.astype(BF16)
    down_grad = ein("rn,yrf->ynf", d_ffn, hidden_act).astype(BF16)
    d_act = ein("rn,ynf->yrf", d_ffn, d_all)
    d_pre_act = jax.vjp(exact_gelu, pre_act)[1](d_act)[0]
    ffn_bias_part = jnp.sum(d_pre_act, axis=1).reshape(-1, width)
    d_pre_low = d_pre_act.astype(BF16)
    in_grad = ein("rd,yrf->ydf", middle_low, d_pre_low).astype(BF16)
    d_middle = d_pre_two + ein("yrf,ydf->rd", d_pre_low, i_all)
    gain_one_part = jnp.sum(d_middle * unit_one, axis=0)
    shift_one_part = jnp.sum(d_middle, axis=0)
    d_pre_one = norm_back(d_middle, unit_one, inv_one, gain_all[0])
    bias_three_part = jnp.sum(d_pre_one, axis=0)
    d_attn = d_pre_one.astype(BF16)
    out_grad_t = ein("rn,yrk->ynk", d_attn, mixed).astype(BF16)
    d_mixed = rows_to_heads(ein("rn,ynk->yrk", d_attn, o_all).astype(BF16))
    d_q, d_k, d_v = attend_back(qkv, d_mixed, mixed_heads, stats, segments)
    d_qkv = jnp.concatenate([d_q, d_k, d_v], axis=1).astype(BF16)
    v_grad = dg(embed_low, d_qkv, 0, 0).astype(BF16)
    d_embed = dg(d_qkv, qkv_w, 1, 1)
    time_part = bias_three_part + jnp.sum(d_embed, axis=0)
    d_embed = d_embed.astype(BF16).reshape(mp, own_rows, width)

    zero_row = jnp.zeros((width,), F32)
    seq_rows = jnp.where(jnp.arange(dp)[:, None] == dp_index, time_part[None, :], 0.0)
    small = jnp.concatenate(
        [
            seq_rows,
            jnp.stack(
                [
                    lax.dynamic_update_slice_in_dim(zero_row, jnp.sum(d_q, axis=0), column, 0),
                    lax.dynamic_update_slice_in_dim(zero_row, jnp.sum(d_v, axis=0), column, 0),
                    bias_three_part,
                    shift_one_part,
                    bias_five_part,
                    shift_two_part,
                    gain_one_part,
                    gain_two_part,
                ]
            ),
            ffn_bias_part,
        ],
        axis=0,
    )
    small = jnp.pad(small, ((0, -small.shape[0] % 8), (0, 0)))

    if fast:
        shape = (2, 4, 2, 2, rows, -1)
        v_sum, o_sum, i_sum, d_sum, d_far, small = reduce_grads(
            v_grad.reshape(shape[1:]),
            out_grad_t.reshape(shape),
            in_grad.reshape(shape),
            down_grad.reshape(shape),
            d_embed,
            small,
        )
        d_own = lax.dynamic_index_in_dim(d_embed, mp_index, 0, False).astype(F32) + d_far.astype(F32)
    else:
        v_sum = lax.psum_scatter(v_grad, "dp", scatter_dimension=0, tiled=True).astype(F32)

        def both(a):
            a = lax.psum_scatter(a, "mp", scatter_dimension=0)
            return lax.psum_scatter(a, "dp", scatter_dimension=0, tiled=True).astype(F32)

        o_sum, i_sum, d_sum = both(out_grad_t), both(in_grad), both(down_grad)
        d_own = lax.psum_scatter(d_embed, "mp", scatter_dimension=0).astype(F32)
        small = lax.psum(small, ("dp", "mp"))

    input_grad = d_pre_one + d_own
    d_time = small[:dp]
    start = dp_index * rows
    step_parts = params[::rows, bias_count : bias_count + 2]
    step_ids = 64.0 * step_parts[:, 0] + step_parts[:, 1]
    features = time_features(step_ids, width).astype(BF16).astype(F32)
    features = lax.dynamic_slice_in_dim(features, start, rows, axis=1)
    time_grad = lax.dot_general(
        features, d_time, (((0,), (0,)), ((), ())), precision=lax.Precision.HIGHEST
    )
    tail = small[dp:]
    bias_rows = jnp.concatenate([jnp.sum(d_time, axis=0)[None], tail[:6]], axis=0)
    bias_grad = lax.dynamic_slice_in_dim(bias_rows, start, rows, axis=1)
    gain_grad = lax.dynamic_slice_in_dim(tail[6:8], start, rows, axis=1)
    ffn_rows = ffn_bias.shape[0]
    ffn_all = tail[8:].reshape(-1)
    ffn_bias_grad = lax.dynamic_slice_in_dim(ffn_all, dp_index * ffn_rows, ffn_rows)
    qkv_grad = v_sum.reshape(rows, 3, cols).transpose(1, 0, 2)
    return (
        layer_out,
        input_grad,
        time_grad,
        qkv_grad,
        o_sum.T,
        i_sum,
        d_sum.T,
        bias_grad,
        gain_grad,
        ffn_bias_grad,
    )


def solution(mesh):
    dp, mp = mesh.shape["dp"], mesh.shape["mp"]
    placed = (
        P(("dp", "mp"), None),
        P("dp", None),
        P("dp"),
        P("dp", None),
        P(None, "dp", "mp"),
        P("mp", "dp"),
        P("dp", "mp"),
        P("mp", "dp"),
        P(None, "dp"),
        P(None, "dp"),
        P("dp"),
        P(("dp", "mp"), None),
    )
    return jax.shard_map(
        functools.partial(on_device, dp=dp, mp=mp),
        mesh=mesh,
        in_specs=placed,
        out_specs=(
            P(("dp", "mp"), None),
            P(("dp", "mp"), None),
            P("dp", None),
            P(None, "dp", "mp"),
            P("mp", "dp"),
            P("dp", "mp"),
            P("mp", "dp"),
            P(None, "dp"),
            P(None, "dp"),
            P("dp"),
        ),
        check_vma=False,
    )
```

```python
import functools
import math

import jax
import jax.numpy as jnp
from jax import lax
from jax.experimental import pallas as pl
from jax.experimental.pallas import tpu as pltpu
from jax.sharding import PartitionSpec as P

HD = 64
eps = 1e-05
neg_big = -1000000000.0
MESH = pl.DeviceIdType.MESH
F32, BF16 = jnp.float32, jnp.bfloat16
VMEM_LIMIT = 64000000


def dg(left, right, left_dim, right_dim):
    return lax.dot_general(
        left, right, (((left_dim,), (right_dim,)), ((), ())), preferred_element_type=F32
    )


class Place:
    def __init__(self):
        i, y = lax.axis_index("dp"), lax.axis_index("mp")
        z, x, c = i // 4, (i // 2) % 2, i % 2
        self.i, self.z, self.x, self.c, self.y = i, z, x, c, y
        self.nx, self.nc, self.ny, self.zero = 1 - x, 1 - c, 1 - y, 0 * i
        low, high = z % 2, z // 2
        flipped = [(1 - 2 * bit) * v + bit for v, bit in ((low, 1), (high, 1))]
        self.zs = [high * 2 + flipped[0], flipped[1] * 2 + low, flipped[1] * 2 + flipped[0]]
        self.to_z = [((p * 2 + x) * 2 + c, y) for p in self.zs]
        self.to_x = ((z * 2 + self.nx) * 2 + c, y)
        self.to_y = (i, self.ny)
        self.to_c = ((z * 2 + x) * 2 + self.nc, y)
        self.dp = [
            (pz * 2 + px) * 2 + pc
            for pz in [z] + self.zs
            for px in (x, self.nx)
            for pc in (c, self.nc)
        ][1:]

    def enter(self, all_dp):
        barrier = pltpu.get_barrier_semaphore()
        near = [self.to_y]
        near += [(p, self.y) for p in self.dp] if all_dp else self.to_z + [self.to_x, self.to_c]
        for one in near:
            pl.semaphore_signal(barrier, inc=1, device_id=one, device_id_type=MESH)
        pl.semaphore_wait(barrier, len(near))


class Wire:
    def __init__(self, at, send_sems, recv_sems):
        self.sems = [(send_sems.at[at.zero + k], recv_sems.at[at.zero + k]) for k in range(send_sems.shape[0])]
        self.used, self.open = 0, []

    def send(self, src, dst, to):
        k = self.used
        self.used += 1
        copy = pltpu.make_async_remote_copy(
            src_ref=src,
            dst_ref=dst,
            send_sem=self.sems[k][0],
            recv_sem=self.sems[k][1],
            device_id=to,
            device_id_type=MESH,
        )
        copy.start()
        self.open.append(copy)
        return copy

    def close(self):
        assert self.used == len(self.sems), self.used
        for copy in self.open:
            copy.wait_send()


class Local:
    def __init__(self, sems):
        self.sems, self.used, self.open = sems, 0, []

    def copy(self, src, dst):
        one = pltpu.make_async_copy(src, dst, self.sems.at[self.used])
        self.used += 1
        one.start()
        self.open.append(one)
        return one

    def close(self):
        assert self.used == self.sems.shape[0], self.used
        for one in self.open:
            one.wait()


def parts_of(width, parts):
    step = width // parts
    return [(p * step, p * step + step // 2, (p + 1) * step) for p in range(parts)]


def stagger(streams, ahead=0):
    for depth in range(ahead, len(streams) + 6):
        for k, s in enumerate(streams):
            if k <= depth:
                next(s, None)


def gather_dp(wire, at, shard, whole, lo, hi):
    n = pl.ds(lo, hi - lo)
    own = whole.at[at.z, at.x, at.c, :, n]
    from_z = [wire.send(shard.at[:, n], own, to) for to in at.to_z]
    late = [wire.send(shard.at[:, n], own, at.to_c)]
    yield
    for k in from_z:
        k.wait_recv()
    ref = whole.at[:, at.x, at.c, :, n]
    from_x = wire.send(ref, ref, at.to_x)
    for p in at.zs:
        ref = whole.at[p, at.x, at.c, :, n]
        late.append(wire.send(ref, ref, at.to_c))
    yield
    from_x.wait_recv()
    ref = whole.at[:, at.nx, at.c, :, n]
    late.append(wire.send(ref, ref, at.to_c))
    yield
    for k in late:
        k.wait_recv()


def gather_all(wire, at, shard, whole, lo, mid, hi):
    a, b, ab = pl.ds(lo, mid - lo), pl.ds(mid, hi - mid), pl.ds(lo, hi - lo)
    y, z, x, c = at.y, at.z, at.x, at.c
    own = whole.at[y, z, x, c, :, ab]
    from_z = [wire.send(shard.at[:, ab], own, to) for to in at.to_z]
    late = [wire.send(shard.at[:, ab], own, at.to_c)]
    yield
    for k in from_z:
        k.wait_recv()
    ref = whole.at[y, :, x, c, :, a]
    from_x_a = wire.send(ref, ref, at.to_x)
    ref = whole.at[y, :, x, c, :, b]
    from_y_b = wire.send(ref, ref, at.to_y)
    for p in at.zs:
        ref = whole.at[y, p, x, c, :, ab]
        late.append(wire.send(ref, ref, at.to_c))
    yield
    from_x_a.wait_recv()
    ref = whole.at[y, :, :, c, :, a]
    from_y_a = wire.send(ref, ref, at.to_y)
    from_y_b.wait_recv()
    ref = whole.at[:, :, x, c, :, b]
    from_x_b = wire.send(ref, ref, at.to_x)
    for ref in (whole.at[y, :, at.nx, c, :, a], whole.at[at.ny, :, x, c, :, b]):
        late.append(wire.send(ref, ref, at.to_c))
    yield
    from_y_a.wait_recv()
    from_x_b.wait_recv()
    for ref in (whole.at[at.ny, :, :, c, :, a], whole.at[:, :, at.nx, c, :, b]):
        late.append(wire.send(ref, ref, at.to_c))
    yield
    for k in late:
        k.wait_recv()


def one_hot_rows(count, width, start):
    down = lax.broadcasted_iota(jnp.int32, (count, width), 0)
    across = lax.broadcasted_iota(jnp.int32, (count, width), 1)
    return jnp.where(down == across + start, 1.0, 0.0).astype(BF16)


def forward_kernel(
    v_ref, t_ref, f_ref, b_ref, o_ref, i_ref, d_ref, h_ref, sr_ref, sc_ref,
    v_out, o_out, i_out, d_all, few_out, par_out, time_out, embed_out, qkv_out, mine_out, far_out,
    stats_out, unit_out, inv_out, mid_out, act_out, slope_out,
    v_all, o_all, i_all, few, part, got, h_far, par, ffn_b, embed, qkv, mine, far, stats, unit, inv,
    mid, act, slope, send_sems, recv_sems, local_sems, tile_sems,
):
    at = Place()
    y, z, x, c = at.y, at.z, at.x, at.c
    at.enter(True)
    wire, local = Wire(at, send_sems, recv_sems), Local(local_sems)
    width = h_ref.shape[1]
    own_rows = h_ref.shape[0]
    rows = v_ref.shape[0]
    cols = o_ref.shape[1]
    hidden = i_ref.shape[1]
    length = 2 * own_rows

    from_few = [wire.send(f_ref, few.at[at.i], (p, y)) for p in at.dp]
    from_h = wire.send(h_ref, h_far, at.to_y)
    v_mid = 7 * 128
    v0 = gather_dp(wire, at, v_ref, v_all, 0, v_mid)
    v1 = gather_dp(wire, at, v_ref, v_all, v_mid, v_ref.shape[1])
    out_w = gather_all(wire, at, o_ref, o_all, *parts_of(cols, 1)[0])
    in_w = [gather_all(wire, at, i_ref, i_all, *cut) for cut in parts_of(hidden, 2)]
    down_w = [gather_all(wire, at, d_ref, d_all, *cut) for cut in parts_of(hidden, 2)]
    next(v0)
    kept = [
        local.copy(v_ref, v_all.at[z, x, c]),
        local.copy(o_ref, o_all.at[y, z, x, c]),
        local.copy(i_ref, i_all.at[y, z, x, c]),
        local.copy(d_ref, d_all.at[y, z, x, c]),
    ]
    few[at.i] = f_ref[...]
    for k in from_few:
        k.wait_recv()
    seqs = few.shape[0]
    table = jnp.concatenate([few[s] for s in range(seqs)], axis=0)
    pick = one_hot_rows(width, rows, at.i * rows)
    feats = dg(table[:, :width].astype(BF16), pick, 1, 0).astype(BF16)
    partial = dg(feats, t_ref[...], 1, 0) + dg(b_ref[...], pick, 1, 1)
    for s in range(seqs):
        part[s] = partial[s : s + 1]
    ffn_b[...] = jnp.concatenate([few[s][:, width:] for s in range(seqs)], axis=1)
    local.copy(few, few_out)
    from_part = [wire.send(part.at[p], got.at[j], (p, y)) for j, p in enumerate(at.dp)]
    next(v1)
    next(out_w)
    next(in_w[0])
    for k in kept:
        k.wait()
        local.open.remove(k)
    next(v0)
    next(v1)
    next(in_w[1])
    next(down_w[0])
    next(down_w[1])
    for k in from_part:
        k.wait_recv()
    total = part[at.i]
    for j in range(seqs - 1):
        total = total + got[j]
    time_out[...] = total

    from_h.wait_recv()
    step = 128

    def embed_rows(t, _):
        r = pl.ds(pl.multiple_of(t * step, step), step)
        embed[y, r] = (h_ref[r].astype(F32) + total).astype(BF16)
        embed[at.ny, r] = (h_far[r].astype(F32) + total).astype(BF16)
        return 0

    lax.fori_loop(0, own_rows // step, embed_rows, 0)
    local.copy(embed, embed_out)
    next(v0)
    next(out_w)
    next(v1)
    next(in_w[0])
    next(v0, None)
    next(v1, None)
    local.copy(v_all, v_out)
    par[...] = v_all[:, :, :, :, 3 * cols :].reshape(width, 128).astype(F32).T
    local.copy(par, par_out)
    heads = pl.ds(pl.multiple_of(y * cols, cols), cols)
    bias_q, bias_v = par[1:2, heads], par[2:3, heads]

    step_q = 256

    def project(t, _):
        half, r = t // (own_rows // step_q), pl.ds(pl.multiple_of((t % (own_rows // step_q)) * step_q, step_q), step_q)
        whole_r = pl.ds(pl.multiple_of(t * step_q, step_q), step_q)
        left = embed[half, r]
        for j, bias in enumerate((bias_q, None, bias_v)):
            n = slice(j * cols, (j + 1) * cols)
            made = dg(left, v_all[:, :, :, :, n].reshape(width, cols), 1, 0)
            qkv[whole_r, n] = (made if bias is None else made + bias).astype(BF16)
        return 0

    lax.fori_loop(0, length // step_q, project, 0)
    local.copy(qkv, qkv_out)
    next(out_w)
    next(in_w[1])

    pair, tile = 2 * HD, own_rows
    from_far = []

    def give(p):
        n = pl.ds(p * pair, pair)
        from_far.append(wire.send(mine.at[at.ny, :, n], far.at[:, n], at.to_y))

    ticks = {
        0: lambda: next(in_w[0]),
        1: lambda: (give(0), next(out_w)),
        2: lambda: next(down_w[0]),
        3: lambda: (give(1), next(in_w[0])),
        4: lambda: next(in_w[1]),
        5: lambda: (give(2), next(down_w[1])),
        6: lambda: next(down_w[0]),
        7: lambda: (give(3), next(out_w, None), next(in_w[0], None)),
    }

    def attend_step(t, _):
        p, half = t // 2, t % 2
        r = pl.ds(pl.multiple_of(half * tile, tile), tile)
        n = pl.multiple_of(p * pair, pair)
        queries = qkv[r, pl.ds(n, pair)]
        keys = qkv[:, pl.ds(cols + n, pair)]
        values = qkv[:, pl.ds(2 * cols + n, pair)]
        same = sc_ref[:, 0:1] == sr_ref[:, r]
        made = []
        for h in range(2):
            k = slice(h * HD, h * HD + HD)
            scores = dg(keys[:, k], queries[:, k], 1, 1) * (1.0 / math.sqrt(HD))
            scores = jnp.where(same, scores, neg_big)
            row_max = jnp.max(scores, axis=0, keepdims=True)
            prob = jnp.exp(scores - row_max)
            row_total = jnp.sum(prob, axis=0, keepdims=True)
            made.append((dg(values[:, k], prob.astype(BF16), 0, 0) / row_total).T)
            stats[p, h : h + 1, r] = row_max + jnp.log(row_total)
        mine[half, :, pl.ds(n, pair)] = jnp.concatenate(made, axis=1).astype(BF16)
        for k, tick in ticks.items():
            pl.when(t == k)(lambda tick=tick: (tick(), None)[1])
        return 0

    lax.fori_loop(0, 2 * (cols // pair), attend_step, 0)
    local.copy(mine, mine_out)
    local.copy(stats, stats_out)
    local.copy(o_all, o_out)

    for k in from_far:
        k.wait_recv()
    local.copy(far, far_out)

    def project_out(t, _):
        r = pl.ds(pl.multiple_of(t * step_q, step_q), step_q)
        total_r = dg(mine[y, r], o_all[y].reshape(width, cols), 1, 1)
        total_r += dg(far[r], o_all[at.ny].reshape(width, cols), 1, 1)
        total_r += h_ref[r].astype(F32) + total + par[3:4]
        made, inv_std = normalize(total_r)
        unit[r] = made
        inv[r] = jnp.broadcast_to(inv_std, (step_q, 128))
        mid[r] = (made * par[7:8] + par[4:5]).astype(BF16)
        return 0

    lax.fori_loop(0, own_rows // step_q, project_out, 0)
    local.copy(unit, unit_out)
    local.copy(inv, inv_out)
    local.copy(mid, mid_out)

    chunk = 512
    per = hidden // 2 // chunk
    later = {
        0: lambda: next(in_w[1]),
        1: lambda: next(down_w[1]),
        3: lambda: next(in_w[1], None),
        4: lambda: next(down_w[0]),
        6: lambda: next(down_w[1]),
    }

    def feed_step(t, _):
        side = (t // per) % 2
        n = pl.multiple_of((t // (2 * per)) * (hidden // 2) + (t % per) * chunk, chunk)
        made = dg(mid[...], i_all[side, :, :, :, :, pl.ds(n, chunk)].reshape(width, chunk), 1, 0)
        made = made + ffn_b[:, pl.ds(pl.multiple_of(side * hidden, hidden) + n, chunk)]
        below = 0.5 + 0.5 * lax.erf(made * math.sqrt(0.5))
        act[side, :, pl.ds(n, chunk)] = (made * below).astype(BF16)
        bell = jnp.exp(-0.5 * made * made) * (1.0 / math.sqrt(2.0 * math.pi))
        slope[side, :, pl.ds(n, chunk)] = (below + made * bell).astype(BF16)
        pltpu.make_async_copy(
            act.at[side, :, pl.ds(n, chunk)], act_out.at[side, :, pl.ds(n, chunk)], tile_sems.at[0, t]
        ).start()
        pltpu.make_async_copy(
            slope.at[side, :, pl.ds(n, chunk)], slope_out.at[side, :, pl.ds(n, chunk)], tile_sems.at[1, t]
        ).start()
        for k, tick in later.items():
            pl.when(t == k)(lambda tick=tick: (tick(), None)[1])
        return 0

    tiles = 4 * per
    lax.fori_loop(0, tiles, feed_step, 0)
    local.copy(i_all, i_out)
    next(down_w[0], None)
    next(down_w[1], None)
    for t in range(tiles):
        n = pl.ds(0, chunk)
        pltpu.make_async_copy(act.at[0, :, n], act_out.at[0, :, n], tile_sems.at[0, t]).wait()
        pltpu.make_async_copy(slope.at[0, :, n], slope_out.at[0, :, n], tile_sems.at[1, t]).wait()
    local.close()
    wire.close()


def forward(v, t, few_row, bias_zero, o, i, d, h, seg_row, seg_col):
    rows, cols, hidden = v.shape[0], o.shape[1], i.shape[1]
    own_rows, width = h.shape
    length = 2 * own_rows
    pairs = cols // (2 * HD)
    S = jax.ShapeDtypeStruct
    dp3 = (4, 2, 2)
    v_all, o_all, i_all = S(dp3 + v.shape, BF16), S((2,) + dp3 + o.shape, BF16), S((2,) + dp3 + i.shape, BF16)
    few = S((16,) + few_row.shape, F32)
    par, time_row = S((128, width), F32), S((1, width), F32)
    embed, qkv = S((2, own_rows, width), BF16), S((length, 3 * cols), BF16)
    mine, far = S((2, own_rows, cols), BF16), S((own_rows, cols), BF16)
    stats = S((pairs, 2, length), F32)
    unit, inv, mid = S((own_rows, width), F32), S((own_rows, 128), F32), S((own_rows, width), BF16)
    act = S((2, own_rows, hidden), BF16)
    outs = [v_all, o_all, i_all, i_all, few, par, time_row, embed, qkv, mine, far, stats, unit, inv, mid, act, act]
    vm, hbm = pl.BlockSpec(memory_space=pltpu.VMEM), pl.BlockSpec(memory_space=pl.ANY)
    out_specs = [hbm] * len(outs)
    out_specs[6] = vm
    part, got = S((16, 1, width), F32), S((15, 1, width), F32)
    h_far, ffn_b = S(h.shape, BF16), S((1, 2 * hidden), F32)
    scratch = [v_all, o_all, i_all, few, part, got, h_far, par, ffn_b, embed, qkv, mine, far, stats, unit, inv, mid, act, act]
    copies = 15 + 15 + 1 + 2 * 9 + 5 * 15 + pairs
    return pl.pallas_call(
        forward_kernel,
        name="forward",
        out_shape=outs,
        in_specs=[vm] * 10,
        out_specs=out_specs,
        scratch_shapes=[pltpu.VMEM(a.shape, a.dtype) for a in scratch]
        + [
            pltpu.SemaphoreType.DMA((copies,)),
            pltpu.SemaphoreType.DMA((copies,)),
            pltpu.SemaphoreType.DMA((FORWARD_LOCAL,)),
            pltpu.SemaphoreType.DMA((2, 2 * hidden // 512)),
        ],
        compiler_params=pltpu.CompilerParams(
            collective_id=0, has_side_effects=True, vmem_limit_bytes=VMEM_LIMIT
        ),
    )(v, t, few_row, bias_zero, o, i, d, h, seg_row, seg_col)


FORWARD_LOCAL = 17


def add_blocks(dst, left, right, lead):
    count = math.prod(lead)

    def one(t, _):
        at = []
        for n in reversed(lead):
            at.append(t % n)
            t = t // n
        at = tuple(reversed(at))
        dst[at] = (left[at].astype(F32) + right[at].astype(F32)).astype(dst.dtype)
        return 0

    lax.fori_loop(0, count, one, 0)


def reduce_dp(wire, at, grad, rc, rx, rz, out):
    z, x, c, y = at.z, at.x, at.c, at.y
    from_c = wire.send(grad.at[:, :, at.nc], rc, at.to_c)
    yield
    from_c.wait_recv()
    add_blocks(rc, grad.at[:, :, c], rc, (4, 2))
    from_x = wire.send(rc.at[:, at.nx], rx, at.to_x)
    yield
    from_x.wait_recv()
    add_blocks(rx, rc.at[:, x], rx, (4,))
    from_z = [wire.send(rx.at[p], rz.at[j], to) for j, (p, to) in enumerate(zip(at.zs, at.to_z))]
    yield
    for k in from_z:
        k.wait_recv()
    out[...] = ((rx[z].astype(F32) + rz[0].astype(F32)) + rz[1].astype(F32)) + rz[2].astype(F32)


def reduce_all(wire, at, grad, rc, ya, xb, xa, yb, rz, out, lo, mid, hi):
    z, x, c, y = at.z, at.x, at.c, at.y
    a, b, ab = pl.ds(lo, mid - lo), pl.ds(mid, hi - mid), pl.ds(lo, hi - lo)
    half_a, half_b = pl.ds(0, mid - lo), pl.ds(mid - lo, hi - mid)
    from_c = wire.send(grad.at[:, :, :, at.nc, :, ab], rc, at.to_c)
    yield
    from_c.wait_recv()
    add_blocks(rc, grad.at[:, :, :, c, :, ab], rc, (2, 4, 2))
    from_y_a = wire.send(rc.at[at.ny, :, :, :, half_a], ya, at.to_y)
    from_x_b = wire.send(rc.at[:, :, at.nx, :, half_b], xb, at.to_x)
    yield
    from_y_a.wait_recv()
    add_blocks(ya, rc.at[y, :, :, :, half_a], ya, (4, 2))
    from_x_a = wire.send(ya.at[:, at.nx], xa, at.to_x)
    from_x_b.wait_recv()
    add_blocks(xb, rc.at[:, :, x, :, half_b], xb, (2, 4))
    from_y_b = wire.send(xb.at[at.ny], yb, at.to_y)
    yield
    from_x_a.wait_recv()
    add_blocks(xa, ya.at[:, x], xa, (4,))
    from_y_b.wait_recv()
    add_blocks(yb, xb.at[y], yb, (4,))
    from_z = []
    for j, (p, to) in enumerate(zip(at.zs, at.to_z)):
        from_z.append(wire.send(xa.at[p], rz.at[j, :, half_a], to))
        from_z.append(wire.send(yb.at[p], rz.at[j, :, half_b], to))
    yield
    for k in from_z:
        k.wait_recv()
    for acc, half, cols in ((xa, half_a, a), (yb, half_b, b)):
        out[:, cols] = (
            (acc[z].astype(F32) + rz[0, :, half].astype(F32)) + rz[1, :, half].astype(F32)
        ) + rz[2, :, half].astype(F32)


def reduce_small(wire, at, mine, sums, got, out):
    k = wire.send(mine, got.at[0], at.to_c)
    yield
    k.wait_recv()
    sums[0] = mine[...] + got[0]
    k = wire.send(sums.at[0], got.at[1], at.to_x)
    yield
    k.wait_recv()
    sums[1] = sums[0] + got[1]
    k = wire.send(sums.at[1], got.at[2], at.to_y)
    yield
    k.wait_recv()
    sums[2] = sums[1] + got[2]
    last = [wire.send(sums.at[2], got.at[3 + j], to) for j, to in enumerate(at.to_z)]
    yield
    for k in last:
        k.wait_recv()
    out[...] = ((sums[2] + got[3]) + got[4]) + got[5]


ALL_CUTS = (1, 2, 2)


def reduce_kernel(v_g, o_g, i_g, d_g, x_part, small, v_out, o_out, i_out, d_out, x_got, s_out, *rest):
    at = Place()
    at.enter(False)
    rest = list(rest)
    send_sems, recv_sems = rest[0], rest[1]
    scratch = iter(rest[2:])
    wire = Wire(at, send_sems, recv_sems)
    sums, got = next(scratch), next(scratch)
    tiny = reduce_small(wire, at, small, sums, got, s_out)
    from_y = wire.send(x_part.at[at.ny], x_got, at.to_y)
    streams = []
    for grad, out, parts in ((d_g, d_out, ALL_CUTS[2]), (i_g, i_out, ALL_CUTS[1]), (o_g, o_out, ALL_CUTS[0])):
        for cut in parts_of(out.shape[1], parts):
            bufs = [next(scratch) for _ in range(6)]
            streams.append(reduce_all(wire, at, grad, *bufs, out, *cut))
    bufs = [next(scratch) for _ in range(3)]
    streams.append(reduce_dp(wire, at, v_g, *bufs, v_out))
    stagger([tiny] + streams)
    from_y.wait_recv()
    wire.close()


def reduce_grads(v_g, o_g, i_g, d_g, x_part, small):
    rows = v_g.shape[-2]
    out = [jax.ShapeDtypeStruct((rows, a.shape[-1]), F32) for a in (v_g, o_g, i_g, d_g)]
    scratch = [pltpu.VMEM((3,) + small.shape, F32), pltpu.VMEM((6,) + small.shape, F32)]
    copies = 6 + 1
    for a, parts in ((d_g, ALL_CUTS[2]), (i_g, ALL_CUTS[1]), (o_g, ALL_CUTS[0])):
        n = a.shape[-1] // parts
        h = n // 2
        for _ in range(parts):
            copies += 11
            scratch += [
                pltpu.VMEM(s, BF16)
                for s in (
                    (2, 4, 2, rows, n),
                    (4, 2, rows, h),
                    (2, 4, rows, h),
                    (4, rows, h),
                    (4, rows, h),
                    (3, rows, n),
                )
            ]
    n = v_g.shape[-1]
    copies += 5
    scratch += [pltpu.VMEM(s, BF16) for s in ((4, 2, rows, n), (4, rows, n), (3, rows, n))]
    vm = pl.BlockSpec(memory_space=pltpu.VMEM)
    hbm = pl.BlockSpec(memory_space=pl.ANY)
    return pl.pallas_call(
        reduce_kernel,
        name="reduce_grads",
        out_shape=out
        + [jax.ShapeDtypeStruct(x_part.shape[1:], x_part.dtype), jax.ShapeDtypeStruct(small.shape, F32)],
        in_specs=[vm] * 4 + [hbm, vm],
        out_specs=[vm] * 4 + [hbm, vm],
        scratch_shapes=[pltpu.SemaphoreType.DMA((copies,)), pltpu.SemaphoreType.DMA((copies,))] + scratch,
        compiler_params=pltpu.CompilerParams(
            collective_id=1, has_side_effects=True, vmem_limit_bytes=VMEM_LIMIT
        ),
    )(v_g, o_g, i_g, d_g, x_part, small)


def attend_kernel(tile, q_ref, k_ref, v_ref, sr_ref, sc_ref, o_ref, l_ref):
    length, width = q_ref.shape

    def step(t, _):
        rows = pl.ds(pl.multiple_of(t * tile, tile), tile)
        same = sc_ref[:, 0:1] == sr_ref[:, rows]
        for h in range(width // HD):
            cols = slice(h * HD, h * HD + HD)
            scores = dg(k_ref[:, cols], q_ref[rows, cols], 1, 1) * (1.0 / math.sqrt(HD))
            scores = jnp.where(same, scores, neg_big)
            row_max = jnp.max(scores, axis=0, keepdims=True)
            prob = jnp.exp(scores - row_max)
            total = jnp.sum(prob, axis=0, keepdims=True)
            mixed = dg(v_ref[:, cols], prob.astype(BF16), 0, 0) / total
            o_ref[rows, cols] = mixed.T.astype(BF16)
            l_ref[0, h : h + 1, rows] = row_max + jnp.log(total)
        return 0

    lax.fori_loop(0, length // tile, step, 0)


def attend_specs(length, heads_pairs):
    def col(k):
        return pl.BlockSpec((length, 2 * HD), lambda i, k=k: (0, k * heads_pairs + i))

    stats = pl.BlockSpec((1, 2, length), lambda i: (i, 0, 0))
    seg_row = pl.BlockSpec((1, length), lambda i: (0, 0))
    seg_col = pl.BlockSpec((length, 128), lambda i: (0, 0))
    return col, stats, seg_row, seg_col


def attend(qkv, segments):
    length = qkv.shape[0]
    pairs = qkv.shape[1] // 3 // (2 * HD)
    col, stats, seg_row, seg_col = attend_specs(length, pairs)
    return pl.pallas_call(
        functools.partial(attend_kernel, min(512, length)),
        name="attend",
        grid=(pairs,),
        in_specs=[col(0), col(1), col(2), seg_row, seg_col],
        out_specs=[col(0), stats],
        out_shape=[
            jax.ShapeDtypeStruct((length, pairs * 2 * HD), BF16),
            jax.ShapeDtypeStruct((pairs, 2, length), F32),
        ],
        cost_estimate=pl.CostEstimate(
            flops=8 * length * length * HD * pairs, bytes_accessed=4 * length * pairs * 256, transcendentals=0
        ),
    )(qkv, qkv, qkv, segments, jnp.broadcast_to(segments.reshape(length, 1), (length, 128)))


def attend_back_kernel(
    tile, q_ref, k_ref, v_ref, d_ref, o_ref, l_ref, sr_ref, sc_ref, dq_ref, dk_ref, dv_ref
):
    length, width = q_ref.shape
    scale = 1.0 / math.sqrt(HD)
    dk_ref[...] = jnp.zeros_like(dk_ref)
    dv_ref[...] = jnp.zeros_like(dv_ref)

    def step(t, _):
        rows = pl.ds(pl.multiple_of(t * tile, tile), tile)
        same = sc_ref[:, 0:1] == sr_ref[:, rows]
        for h in range(width // HD):
            cols = slice(h * HD, h * HD + HD)
            keys, q_rows, d_rows = k_ref[:, cols], q_ref[rows, cols], d_ref[rows, cols]
            delta = jnp.sum(
                (d_rows.astype(F32) * o_ref[rows, cols].astype(F32)).T, axis=0, keepdims=True
            )
            scores = dg(keys, q_rows, 1, 1) * scale
            prob = jnp.where(same, jnp.exp(scores - l_ref[0, h : h + 1, rows]), 0.0)
            d_prob = dg(v_ref[:, cols], d_rows, 1, 1)
            d_score = (prob * (d_prob - delta) * scale).astype(BF16)
            dv_ref[:, cols] += dg(prob.astype(BF16), d_rows, 1, 0)
            dk_ref[:, cols] += dg(d_score, q_rows, 1, 0)
            dq_ref[rows, cols] = dg(d_score, keys, 0, 0)
        return 0

    lax.fori_loop(0, length // tile, step, 0)


def attend_back(qkv, d_mixed, mixed, stats_in, segments):
    length = qkv.shape[0]
    pairs = qkv.shape[1] // 3 // (2 * HD)
    col, stats, seg_row, seg_col = attend_specs(length, pairs)
    return pl.pallas_call(
        functools.partial(attend_back_kernel, min(512, length)),
        name="attend_back",
        grid=(pairs,),
        in_specs=[col(0), col(1), col(2), col(0), col(0), stats, seg_row, seg_col],
        out_specs=[col(0)] * 3,
        out_shape=[jax.ShapeDtypeStruct((length, pairs * 2 * HD), F32)] * 3,
        cost_estimate=pl.CostEstimate(
            flops=20 * length * length * HD * pairs, bytes_accessed=8 * length * pairs * 256, transcendentals=0
        ),
    )(qkv, qkv, qkv, d_mixed, mixed, stats_in, segments, jnp.broadcast_to(segments.reshape(length, 1), (length, 128)))


def time_features(step_ids, model_width):
    half_width = model_width // 2
    frequency = jnp.exp(
        jnp.arange(half_width, dtype=F32) * (-math.log(10000.0) / half_width)
    )
    angles = step_ids.astype(F32)[:, None] * frequency[None, :]
    return jnp.concatenate([jnp.sin(angles), jnp.cos(angles)], axis=1)


def normalize(array_in):
    row_mean = jnp.mean(array_in, axis=-1, keepdims=True)
    centered = array_in - row_mean
    variance = jnp.mean(centered * centered, axis=-1, keepdims=True)
    inv_std = lax.rsqrt(variance + eps)
    return (centered * inv_std, inv_std)


def norm_back(grad_rows, unit_rows, inv_std, gain_row):
    d_unit = grad_rows * gain_row
    return inv_std * (
        d_unit
        - jnp.mean(d_unit, axis=-1, keepdims=True)
        - unit_rows * jnp.mean(d_unit * unit_rows, axis=-1, keepdims=True)
    )


def ein(spec, left, right):
    return jnp.einsum(spec, left, right, preferred_element_type=F32)


def on_device(
    hidden_in,
    segments,
    timesteps,
    time_weight,
    qkv_weight,
    out_weight,
    in_weight,
    down_weight,
    biases,
    gains,
    ffn_bias,
    out_grad,
    *,
    dp,
    mp,
):
    own_rows, width = hidden_in.shape
    length = segments.shape[1]
    rows = time_weight.shape[0]
    cols = qkv_weight.shape[2]
    hidden = in_weight.shape[1]
    dp_index, mp_index = lax.axis_index("dp"), lax.axis_index("mp")
    fast = (dp, mp) == (16, 2)

    bias_count = biases.shape[0] + gains.shape[0]
    v_shard = jnp.concatenate(
        [qkv_weight[0], qkv_weight[1], qkv_weight[2], biases.T, gains.T, jnp.zeros((rows, 128 - bias_count), BF16)],
        axis=1,
    )
    feature = time_features(timesteps, width).astype(BF16)
    few_row = jnp.concatenate([feature.astype(F32), ffn_bias.astype(F32)[None]], axis=1)
    seg_col = jnp.broadcast_to(segments.reshape(length, 1), (length, 128))
    if fast:
        (
            v_all, o_all, i_all, d_all, few, par, time_row, embed_low, qkv, mixed_heads, mixed_far,
            stats, unit_one, inv_one, middle_low, hidden_act, slope,
        ) = forward(
            v_shard, time_weight, few_row, biases[:1], out_weight.T, in_weight, down_weight.T,
            hidden_in, segments, seg_col,
        )
        few = few.reshape(dp, -1)
        inv_one = inv_one[:, :1]
        own = jnp.arange(2)[:, None, None] == mp_index
        mixed = jnp.where(own, mixed_heads, mixed_far[None])
    else:
        v_all = lax.all_gather(v_shard, "dp", axis=0)
        o_all, i_all, d_all = (
            lax.all_gather(lax.all_gather(a, "dp", axis=0), "mp", axis=0)
            for a in (out_weight.T, in_weight, down_weight.T)
        )
        few = lax.all_gather(few_row, "dp", axis=0, tiled=True)
        time_w = lax.all_gather(time_weight, "dp", axis=0, tiled=True)
    v_all = v_all.reshape(width, -1)
    o_all, i_all, d_all = (a.reshape(mp, width, -1) for a in (o_all, i_all, d_all))
    qkv_w = v_all[:, : 3 * cols]
    column = mp_index * cols
    if fast:
        bias_all, gain_all = par[:7], par[7:9]
        middle = unit_one * gain_all[0] + bias_all[4]
    else:
        params = v_all[:, 3 * cols :].astype(F32).T
        bias_all, gain_all = params[:7], params[7:9]
        time_row = jnp.dot(feature, time_w, preferred_element_type=F32) + bias_all[0]
        h_all = lax.all_gather(hidden_in, "mp", axis=0, tiled=True)
        embedded = hidden_in.astype(F32) + time_row
        embed_low = (h_all.astype(F32) + time_row).astype(BF16)
        bias_qkv = jnp.concatenate(
            [
                lax.dynamic_slice_in_dim(bias_all[1], column, cols),
                jnp.zeros((cols,), F32),
                lax.dynamic_slice_in_dim(bias_all[2], column, cols),
            ]
        )
        qkv = (jnp.dot(embed_low, qkv_w, preferred_element_type=F32) + bias_qkv).astype(BF16)
        mixed_heads, stats = attend(qkv, segments)
        mixed = lax.all_to_all(mixed_heads.reshape(mp, own_rows, cols), "mp", 0, 0, tiled=True)
        attn_total = ein("yrk,ynk->rn", mixed, o_all)
        unit_one, inv_one = normalize(embedded + attn_total + bias_all[3])
        middle = unit_one * gain_all[0] + bias_all[4]
        middle_low = middle.astype(BF16)
        ffn_b = few[:, width:].reshape(mp, hidden)
        pre_act = ein("rd,ydf->yrf", middle_low, i_all) + ffn_b[:, None, :]
        below = 0.5 + 0.5 * lax.erf(pre_act * math.sqrt(0.5))
        hidden_act = (pre_act * below).astype(BF16)
        slope = below + pre_act * jnp.exp(-0.5 * pre_act * pre_act) * (1.0 / math.sqrt(2.0 * math.pi))
    embed_low = embed_low.reshape(length, width)
    mixed_heads = mixed_heads.reshape(length, cols)

    def rows_to_heads(cut):
        if mp == 2:
            far = lax.ppermute(
                lax.dynamic_index_in_dim(cut, 1 - mp_index, 0, False), "mp", [(0, 1), (1, 0)]
            )
            return jnp.where(own, cut, far[None]).reshape(length, cols)
        return lax.all_to_all(cut, "mp", 0, 0, tiled=True).reshape(length, cols)

    ffn_total = ein("yrf,ynf->rn", hidden_act, d_all)
    unit_two, inv_two = normalize(middle + ffn_total + bias_all[5])
    layer_out = (unit_two * gain_all[1] + bias_all[6]).astype(BF16)

    grad_out = out_grad.astype(F32)
    gain_two_part = jnp.sum(grad_out * unit_two, axis=0)
    shift_two_part = jnp.sum(grad_out, axis=0)
    d_pre_two = norm_back(grad_out, unit_two, inv_two, gain_all[1])
    bias_five_part = jnp.sum(d_pre_two, axis=0)
    d_ffn = d_pre_two.astype(BF16)
    down_grad = ein("rn,yrf->ynf", d_ffn, hidden_act).astype(BF16)
    d_act = ein("rn,ynf->yrf", d_ffn, d_all)
    d_pre_act = d_act * slope.astype(F32)
    ffn_bias_part = jnp.sum(d_pre_act, axis=1).reshape(-1, width)
    d_pre_low = d_pre_act.astype(BF16)
    in_grad = ein("rd,yrf->ydf", middle_low, d_pre_low).astype(BF16)
    d_middle = d_pre_two + ein("yrf,ydf->rd", d_pre_low, i_all)
    gain_one_part = jnp.sum(d_middle * unit_one, axis=0)
    shift_one_part = jnp.sum(d_middle, axis=0)
    d_pre_one = norm_back(d_middle, unit_one, inv_one, gain_all[0])
    bias_three_part = jnp.sum(d_pre_one, axis=0)
    d_attn = d_pre_one.astype(BF16)
    out_grad_t = ein("rn,yrk->ynk", d_attn, mixed).astype(BF16)
    d_mixed = rows_to_heads(ein("rn,ynk->yrk", d_attn, o_all).astype(BF16))
    d_q, d_k, d_v = attend_back(qkv, d_mixed, mixed_heads, stats, segments)
    d_qkv = jnp.concatenate([d_q, d_k, d_v], axis=1).astype(BF16)
    v_grad = dg(embed_low, d_qkv, 0, 0).astype(BF16)
    d_embed = dg(d_qkv, qkv_w, 1, 1)
    time_part = bias_three_part + jnp.sum(d_embed, axis=0)
    d_embed = d_embed.astype(BF16).reshape(mp, own_rows, width)

    zero_row = jnp.zeros((width,), F32)
    seq_rows = jnp.where(jnp.arange(dp)[:, None] == dp_index, time_part[None, :], 0.0)
    small = jnp.concatenate(
        [
            seq_rows,
            jnp.stack(
                [
                    lax.dynamic_update_slice_in_dim(zero_row, jnp.sum(d_q, axis=0), column, 0),
                    lax.dynamic_update_slice_in_dim(zero_row, jnp.sum(d_v, axis=0), column, 0),
                    bias_three_part,
                    shift_one_part,
                    bias_five_part,
                    shift_two_part,
                    gain_one_part,
                    gain_two_part,
                ]
            ),
            ffn_bias_part,
        ],
        axis=0,
    )
    small = jnp.pad(small, ((0, -small.shape[0] % 8), (0, 0)))

    if fast:
        shape = (2, 4, 2, 2, rows, -1)
        v_sum, o_sum, i_sum, d_sum, d_far, small = reduce_grads(
            v_grad.reshape(shape[1:]),
            out_grad_t.reshape(shape),
            in_grad.reshape(shape),
            down_grad.reshape(shape),
            d_embed,
            small,
        )
        d_own = lax.dynamic_index_in_dim(d_embed, mp_index, 0, False).astype(F32) + d_far.astype(F32)
    else:
        v_sum = lax.psum_scatter(v_grad, "dp", scatter_dimension=0, tiled=True).astype(F32)

        def both(a):
            a = lax.psum_scatter(a, "mp", scatter_dimension=0)
            return lax.psum_scatter(a, "dp", scatter_dimension=0, tiled=True).astype(F32)

        o_sum, i_sum, d_sum = both(out_grad_t), both(in_grad), both(down_grad)
        d_own = lax.psum_scatter(d_embed, "mp", scatter_dimension=0).astype(F32)
        small = lax.psum(small, ("dp", "mp"))

    input_grad = d_pre_one + d_own
    d_time = small[:dp]
    start = dp_index * rows
    features = few[:, :width]
    features = lax.dynamic_slice_in_dim(features, start, rows, axis=1)
    time_grad = lax.dot_general(
        features, d_time, (((0,), (0,)), ((), ())), precision=lax.Precision.HIGHEST
    )
    tail = small[dp:]
    bias_rows = jnp.concatenate([jnp.sum(d_time, axis=0)[None], tail[:6]], axis=0)
    bias_grad = lax.dynamic_slice_in_dim(bias_rows, start, rows, axis=1)
    gain_grad = lax.dynamic_slice_in_dim(tail[6:8], start, rows, axis=1)
    ffn_rows = ffn_bias.shape[0]
    ffn_all = tail[8:].reshape(-1)
    ffn_bias_grad = lax.dynamic_slice_in_dim(ffn_all, dp_index * ffn_rows, ffn_rows)
    qkv_grad = v_sum.reshape(rows, 3, cols).transpose(1, 0, 2)
    return (
        layer_out,
        input_grad,
        time_grad,
        qkv_grad,
        o_sum.T,
        i_sum,
        d_sum.T,
        bias_grad,
        gain_grad,
        ffn_bias_grad,
    )


def solution(mesh):
    dp, mp = mesh.shape["dp"], mesh.shape["mp"]
    placed = (
        P(("dp", "mp"), None),
        P("dp", None),
        P("dp"),
        P("dp", None),
        P(None, "dp", "mp"),
        P("mp", "dp"),
        P("dp", "mp"),
        P("mp", "dp"),
        P(None, "dp"),
        P(None, "dp"),
        P("dp"),
        P(("dp", "mp"), None),
    )
    return jax.shard_map(
        functools.partial(on_device, dp=dp, mp=mp),
        mesh=mesh,
        in_specs=placed,
        out_specs=(
            P(("dp", "mp"), None),
            P(("dp", "mp"), None),
            P("dp", None),
            P(None, "dp", "mp"),
            P("mp", "dp"),
            P("dp", "mp"),
            P("mp", "dp"),
            P(None, "dp"),
            P(None, "dp"),
            P("dp"),
        ),
        check_vma=False,
    )
```

```python
import functools
import math

import jax
import jax.numpy as jnp
from jax import lax
from jax.experimental import pallas as pl
from jax.experimental.pallas import tpu as pltpu
from jax.sharding import PartitionSpec as P

HD = 64
eps = 1e-05
neg_big = -1000000000.0
MESH = pl.DeviceIdType.MESH
F32, BF16 = jnp.float32, jnp.bfloat16
VMEM_LIMIT, VMEM_ALL = 64000000, 67043328


def dg(left, right, left_dim, right_dim):
    return lax.dot_general(
        left, right, (((left_dim,), (right_dim,)), ((), ())), preferred_element_type=F32
    )


class Place:
    def __init__(self):
        i, y = lax.axis_index("dp"), lax.axis_index("mp")
        z, x, c = i // 4, (i // 2) % 2, i % 2
        self.i, self.z, self.x, self.c, self.y = i, z, x, c, y
        self.nx, self.nc, self.ny, self.zero = 1 - x, 1 - c, 1 - y, 0 * i
        low, high = z % 2, z // 2
        flipped = [(1 - 2 * bit) * v + bit for v, bit in ((low, 1), (high, 1))]
        self.zs = [high * 2 + flipped[0], flipped[1] * 2 + low, flipped[1] * 2 + flipped[0]]
        self.to_z = [((p * 2 + x) * 2 + c, y) for p in self.zs]
        self.to_x = ((z * 2 + self.nx) * 2 + c, y)
        self.to_y = (i, self.ny)
        self.to_c = ((z * 2 + x) * 2 + self.nc, y)
        self.count = [self.zero + j for j in range(3)]
        self.dp = [
            (pz * 2 + px) * 2 + pc
            for pz in [z] + self.zs
            for px in (x, self.nx)
            for pc in (c, self.nc)
        ][1:]

    def enter(self, all_dp):
        barrier = pltpu.get_barrier_semaphore()
        near = [self.to_y]
        near += [(p, self.y) for p in self.dp] if all_dp else self.to_z + [self.to_x, self.to_c]
        for one in near:
            pl.semaphore_signal(barrier, inc=1, device_id=one, device_id_type=MESH)
        pl.semaphore_wait(barrier, len(near))


class Wire:
    def __init__(self, at, send_sems, recv_sems):
        self.sems = [(send_sems.at[at.zero + k], recv_sems.at[at.zero + k]) for k in range(send_sems.shape[0])]
        self.used, self.open = 0, []

    def send(self, src, dst, to):
        k = self.used
        self.used += 1
        copy = pltpu.make_async_remote_copy(
            src_ref=src,
            dst_ref=dst,
            send_sem=self.sems[k][0],
            recv_sem=self.sems[k][1],
            device_id=to,
            device_id_type=MESH,
        )
        copy.start()
        self.open.append(copy)
        return copy

    def both(self, copy):
        copy.wait_send()
        self.open = [one for one in self.open if one is not copy]
        copy.wait_recv()

    def close(self):
        assert self.used == len(self.sems), self.used
        for copy in self.open:
            copy.wait_send()


class Local:
    def __init__(self, sems):
        self.sems, self.used, self.open = sems, 0, []

    def copy(self, src, dst):
        one = pltpu.make_async_copy(src, dst, self.sems.at[self.used])
        self.used += 1
        one.start()
        self.open.append(one)
        return one

    def close(self):
        assert self.used == self.sems.shape[0], self.used
        for one in self.open:
            one.wait()


def parts_of(width, parts):
    step = width // parts
    return [(p * step, p * step + step // 2, (p + 1) * step) for p in range(parts)]


def stagger(streams, ahead=0):
    for depth in range(ahead, len(streams) + 6):
        for k, s in enumerate(streams):
            if k <= depth:
                next(s, None)


def gather_dp(wire, at, shard, whole, lo, hi):
    n = pl.ds(lo, hi - lo)
    own = whole.at[at.z, at.x, at.c, :, n]
    from_z = [wire.send(shard.at[:, n], own, to) for to in at.to_z]
    late = [wire.send(shard.at[:, n], own, at.to_c)]
    yield
    for k in from_z:
        k.wait_recv()
    ref = whole.at[:, at.x, at.c, :, n]
    from_x = wire.send(ref, ref, at.to_x)
    for p in at.zs:
        ref = whole.at[p, at.x, at.c, :, n]
        late.append(wire.send(ref, ref, at.to_c))
    yield
    from_x.wait_recv()
    ref = whole.at[:, at.nx, at.c, :, n]
    late.append(wire.send(ref, ref, at.to_c))
    yield
    for k in late:
        k.wait_recv()


def gather_all(wire, at, shard, whole, lo, mid, hi):
    a, b, ab = pl.ds(lo, mid - lo), pl.ds(mid, hi - mid), pl.ds(lo, hi - lo)
    y, z, x, c = at.y, at.z, at.x, at.c
    own = whole.at[y, z, x, c, :, ab]
    from_z = [wire.send(shard.at[:, ab], own, to) for to in at.to_z]
    late = [wire.send(shard.at[:, ab], own, at.to_c)]
    yield
    for k in from_z:
        k.wait_recv()
    ref = whole.at[y, :, x, c, :, a]
    from_x_a = wire.send(ref, ref, at.to_x)
    ref = whole.at[y, :, x, c, :, b]
    from_y_b = wire.send(ref, ref, at.to_y)
    for p in at.zs:
        ref = whole.at[y, p, x, c, :, ab]
        late.append(wire.send(ref, ref, at.to_c))
    yield
    from_x_a.wait_recv()
    ref = whole.at[y, :, :, c, :, a]
    from_y_a = wire.send(ref, ref, at.to_y)
    from_y_b.wait_recv()
    ref = whole.at[:, :, x, c, :, b]
    from_x_b = wire.send(ref, ref, at.to_x)
    for ref in (whole.at[y, :, at.nx, c, :, a], whole.at[at.ny, :, x, c, :, b]):
        late.append(wire.send(ref, ref, at.to_c))
    yield
    from_y_a.wait_recv()
    from_x_b.wait_recv()
    for ref in (whole.at[at.ny, :, :, c, :, a], whole.at[:, :, at.nx, c, :, b]):
        late.append(wire.send(ref, ref, at.to_c))
    yield
    for k in late:
        k.wait_recv()


def one_hot_rows(count, width, start):
    down = lax.broadcasted_iota(jnp.int32, (count, width), 0)
    across = lax.broadcasted_iota(jnp.int32, (count, width), 1)
    return jnp.where(down == across + start, 1.0, 0.0).astype(BF16)


def forward_kernel(
    v_ref, t_ref, f_ref, b_ref, o_ref, i_ref, d_ref, h_ref, sr_ref, sc_ref,
    v_out, o_out, i_out, d_all, few_out, par_out, time_out, embed_out, qkv_out, mine_out, far_out,
    stats_out, unit_out, inv_out, mid_out, act_out, slope_out,
    v_all, o_all, i_all, few, part, got, h_far, par, ffn_b, embed, qkv, mine, far, stats, unit, inv,
    mid, act, slope, send_sems, recv_sems, local_sems, tile_sems,
):
    at = Place()
    y, z, x, c = at.y, at.z, at.x, at.c
    at.enter(True)
    wire, local = Wire(at, send_sems, recv_sems), Local(local_sems)
    width = h_ref.shape[1]
    own_rows = h_ref.shape[0]
    rows = v_ref.shape[0]
    cols = o_ref.shape[1]
    hidden = i_ref.shape[1]
    length = 2 * own_rows

    from_few = [wire.send(f_ref, few.at[at.i], (p, y)) for p in at.dp]
    from_h = wire.send(h_ref, h_far, at.to_y)
    v_mid = 7 * 128
    v0 = gather_dp(wire, at, v_ref, v_all, 0, v_mid)
    v1 = gather_dp(wire, at, v_ref, v_all, v_mid, v_ref.shape[1])
    out_w = gather_all(wire, at, o_ref, o_all, *parts_of(cols, 1)[0])
    in_w = [gather_all(wire, at, i_ref, i_all, *cut) for cut in parts_of(hidden, 2)]
    down_w = [gather_all(wire, at, d_ref, d_all, *cut) for cut in parts_of(hidden, 2)]
    next(v0)
    kept = [
        local.copy(v_ref, v_all.at[z, x, c]),
        local.copy(o_ref, o_all.at[y, z, x, c]),
        local.copy(i_ref, i_all.at[y, z, x, c]),
        local.copy(d_ref, d_all.at[y, z, x, c]),
    ]
    few[at.i] = f_ref[...]
    for k in from_few:
        k.wait_recv()
    seqs = few.shape[0]
    table = jnp.concatenate([few[s] for s in range(seqs)], axis=0)
    pick = one_hot_rows(width, rows, at.i * rows)
    feats = dg(table[:, :width].astype(BF16), pick, 1, 0).astype(BF16)
    partial = dg(feats, t_ref[...], 1, 0) + dg(b_ref[...], pick, 1, 1)
    for s in range(seqs):
        part[s] = partial[s : s + 1]
    ffn_b[...] = jnp.concatenate([few[s][:, width:] for s in range(seqs)], axis=1)
    local.copy(few, few_out)
    from_part = [wire.send(part.at[p], got.at[j], (p, y)) for j, p in enumerate(at.dp)]
    next(v1)
    next(out_w)
    next(in_w[0])
    for k in kept:
        k.wait()
        local.open.remove(k)
    next(v0)
    next(v1)
    next(in_w[1])
    next(down_w[0])
    next(down_w[1])
    for k in from_part:
        k.wait_recv()
    total = part[at.i]
    for j in range(seqs - 1):
        total = total + got[j]
    time_out[...] = total

    from_h.wait_recv()
    step = 128

    def embed_rows(t, _):
        r = pl.ds(pl.multiple_of(t * step, step), step)
        embed[y, r] = (h_ref[r].astype(F32) + total).astype(BF16)
        embed[at.ny, r] = (h_far[r].astype(F32) + total).astype(BF16)
        return 0

    lax.fori_loop(0, own_rows // step, embed_rows, 0)
    local.copy(embed, embed_out)
    next(v0)
    next(out_w)
    next(v1)
    next(in_w[0])
    next(v0, None)
    next(v1, None)
    local.copy(v_all, v_out)
    par[...] = v_all[:, :, :, :, 3 * cols :].reshape(width, 128).astype(F32).T
    local.copy(par, par_out)
    heads = pl.ds(pl.multiple_of(y * cols, cols), cols)
    bias_q, bias_v = par[1:2, heads], par[2:3, heads]

    step_q = 256

    def project(t, _):
        half, r = t // (own_rows // step_q), pl.ds(pl.multiple_of((t % (own_rows // step_q)) * step_q, step_q), step_q)
        whole_r = pl.ds(pl.multiple_of(t * step_q, step_q), step_q)
        left = embed[half, r]
        for j, bias in enumerate((bias_q, None, bias_v)):
            n = slice(j * cols, (j + 1) * cols)
            made = dg(left, v_all[:, :, :, :, n].reshape(width, cols), 1, 0)
            qkv[whole_r, n] = (made if bias is None else made + bias).astype(BF16)
        return 0

    lax.fori_loop(0, length // step_q, project, 0)
    local.copy(qkv, qkv_out)
    next(out_w)
    next(in_w[1])

    pair, tile = 2 * HD, own_rows
    from_far = []

    def give(p):
        n = pl.ds(p * pair, pair)
        from_far.append(wire.send(mine.at[at.ny, :, n], far.at[:, n], at.to_y))

    ticks = {
        0: lambda: next(in_w[0]),
        1: lambda: (give(0), next(out_w)),
        2: lambda: next(down_w[0]),
        3: lambda: (give(1), next(in_w[0])),
        4: lambda: next(in_w[1]),
        5: lambda: (give(2), next(down_w[1])),
        6: lambda: next(down_w[0]),
        7: lambda: (give(3), next(out_w, None), next(in_w[0], None)),
    }

    def attend_step(t, _):
        p, half = t // 2, t % 2
        r = pl.ds(pl.multiple_of(half * tile, tile), tile)
        n = pl.multiple_of(p * pair, pair)
        queries = qkv[r, pl.ds(n, pair)]
        keys = qkv[:, pl.ds(cols + n, pair)]
        values = qkv[:, pl.ds(2 * cols + n, pair)]
        same = sc_ref[:, 0:1] == sr_ref[:, r]
        made = []
        for h in range(2):
            k = slice(h * HD, h * HD + HD)
            scores = dg(keys[:, k], queries[:, k], 1, 1) * (1.0 / math.sqrt(HD))
            scores = jnp.where(same, scores, neg_big)
            row_max = jnp.max(scores, axis=0, keepdims=True)
            prob = jnp.exp(scores - row_max)
            row_total = jnp.sum(prob, axis=0, keepdims=True)
            made.append((dg(values[:, k], prob.astype(BF16), 0, 0) / row_total).T)
            stats[p, h : h + 1, r] = row_max + jnp.log(row_total)
        mine[half, :, pl.ds(n, pair)] = jnp.concatenate(made, axis=1).astype(BF16)
        for k, tick in ticks.items():
            pl.when(t == k)(lambda tick=tick: (tick(), None)[1])
        return 0

    lax.fori_loop(0, 2 * (cols // pair), attend_step, 0)
    local.copy(mine, mine_out)
    local.copy(stats, stats_out)
    local.copy(o_all, o_out)

    for k in from_far:
        k.wait_recv()
    local.copy(far, far_out)

    def project_out(t, _):
        r = pl.ds(pl.multiple_of(t * step_q, step_q), step_q)
        total_r = dg(mine[y, r], o_all[y].reshape(width, cols), 1, 1)
        total_r += dg(far[r], o_all[at.ny].reshape(width, cols), 1, 1)
        total_r += h_ref[r].astype(F32) + total + par[3:4]
        made, inv_std = normalize(total_r)
        unit[r] = made
        inv[r] = jnp.broadcast_to(inv_std, (step_q, 128))
        mid[r] = (made * par[7:8] + par[4:5]).astype(BF16)
        return 0

    lax.fori_loop(0, own_rows // step_q, project_out, 0)
    local.copy(unit, unit_out)
    local.copy(inv, inv_out)
    local.copy(mid, mid_out)

    chunk = 512
    per = hidden // 2 // chunk
    later = {
        0: lambda: next(in_w[1]),
        1: lambda: next(down_w[1]),
        3: lambda: next(in_w[1], None),
        4: lambda: next(down_w[0]),
        6: lambda: next(down_w[1]),
    }

    def feed_step(t, _):
        side = (t // per) % 2
        n = pl.multiple_of((t // (2 * per)) * (hidden // 2) + (t % per) * chunk, chunk)
        made = dg(mid[...], i_all[side, :, :, :, :, pl.ds(n, chunk)].reshape(width, chunk), 1, 0)
        made = made + ffn_b[:, pl.ds(pl.multiple_of(side * hidden, hidden) + n, chunk)]
        below = 0.5 + 0.5 * lax.erf(made * math.sqrt(0.5))
        act[side, :, pl.ds(n, chunk)] = (made * below).astype(BF16)
        bell = jnp.exp(-0.5 * made * made) * (1.0 / math.sqrt(2.0 * math.pi))
        slope[side, :, pl.ds(n, chunk)] = (below + made * bell).astype(BF16)
        pltpu.make_async_copy(
            act.at[side, :, pl.ds(n, chunk)], act_out.at[side, :, pl.ds(n, chunk)], tile_sems.at[0, t]
        ).start()
        pltpu.make_async_copy(
            slope.at[side, :, pl.ds(n, chunk)], slope_out.at[side, :, pl.ds(n, chunk)], tile_sems.at[1, t]
        ).start()
        for k, tick in later.items():
            pl.when(t == k)(lambda tick=tick: (tick(), None)[1])
        return 0

    tiles = 4 * per
    lax.fori_loop(0, tiles, feed_step, 0)
    local.copy(i_all, i_out)
    next(down_w[0], None)
    next(down_w[1], None)
    for t in range(tiles):
        n = pl.ds(0, chunk)
        pltpu.make_async_copy(act.at[0, :, n], act_out.at[0, :, n], tile_sems.at[0, t]).wait()
        pltpu.make_async_copy(slope.at[0, :, n], slope_out.at[0, :, n], tile_sems.at[1, t]).wait()
    local.close()
    wire.close()


def forward(v, t, few_row, bias_zero, o, i, d, h, seg_row, seg_col):
    rows, cols, hidden = v.shape[0], o.shape[1], i.shape[1]
    own_rows, width = h.shape
    length = 2 * own_rows
    pairs = cols // (2 * HD)
    S = jax.ShapeDtypeStruct
    dp3 = (4, 2, 2)
    v_all, o_all, i_all = S(dp3 + v.shape, BF16), S((2,) + dp3 + o.shape, BF16), S((2,) + dp3 + i.shape, BF16)
    few = S((16,) + few_row.shape, F32)
    par, time_row = S((128, width), F32), S((1, width), F32)
    embed, qkv = S((2, own_rows, width), BF16), S((length, 3 * cols), BF16)
    mine, far = S((2, own_rows, cols), BF16), S((own_rows, cols), BF16)
    stats = S((pairs, 2, length), F32)
    unit, inv, mid = S((own_rows, width), F32), S((own_rows, 128), F32), S((own_rows, width), BF16)
    act = S((2, own_rows, hidden), BF16)
    outs = [v_all, o_all, i_all, i_all, few, par, time_row, embed, qkv, mine, far, stats, unit, inv, mid, act, act]
    vm, hbm = pl.BlockSpec(memory_space=pltpu.VMEM), pl.BlockSpec(memory_space=pl.ANY)
    out_specs = [hbm] * len(outs)
    out_specs[6] = vm
    part, got = S((16, 1, width), F32), S((15, 1, width), F32)
    h_far, ffn_b = S(h.shape, BF16), S((1, 2 * hidden), F32)
    scratch = [v_all, o_all, i_all, few, part, got, h_far, par, ffn_b, embed, qkv, mine, far, stats, unit, inv, mid, act, act]
    copies = 15 + 15 + 1 + 2 * 9 + 5 * 15 + pairs
    return pl.pallas_call(
        forward_kernel,
        name="forward",
        out_shape=outs,
        in_specs=[vm] * 10,
        out_specs=out_specs,
        scratch_shapes=[pltpu.VMEM(a.shape, a.dtype) for a in scratch]
        + [
            pltpu.SemaphoreType.DMA((copies,)),
            pltpu.SemaphoreType.DMA((copies,)),
            pltpu.SemaphoreType.DMA((FORWARD_LOCAL,)),
            pltpu.SemaphoreType.DMA((2, 2 * hidden // 512)),
        ],
        compiler_params=pltpu.CompilerParams(
            collective_id=0, has_side_effects=True, vmem_limit_bytes=VMEM_LIMIT
        ),
    )(v, t, few_row, bias_zero, o, i, d, h, seg_row, seg_col)


FORWARD_LOCAL = 17


def add_blocks(dst, left, right, lead):
    count = math.prod(lead)

    def one(t, _):
        at = []
        for n in reversed(lead):
            at.append(t % n)
            t = t // n
        at = tuple(reversed(at))
        dst[at] = (left[at].astype(F32) + right[at].astype(F32)).astype(dst.dtype)
        return 0

    lax.fori_loop(0, count, one, 0)


def reduce_dp(wire, at, grad, rc, rx, rz, out):
    z, x, c, y = at.z, at.x, at.c, at.y
    from_c = wire.send(grad.at[:, :, at.nc], rc, at.to_c)
    yield
    wire.both(from_c)
    add_blocks(rc, grad.at[:, :, c], rc, (4, 2))
    from_x = wire.send(rc.at[:, at.nx], rx, at.to_x)
    yield
    from_x.wait_recv()
    add_blocks(rx, rc.at[:, x], rx, (4,))
    from_z = [wire.send(rx.at[p], rz.at[at.count[j]], to) for j, (p, to) in enumerate(zip(at.zs, at.to_z))]
    yield
    for k in from_z:
        k.wait_recv()
    out[...] = ((rx[z].astype(F32) + rz[0].astype(F32)) + rz[1].astype(F32)) + rz[2].astype(F32)


def reduce_all(wire, at, grad, rc, ya, xb, xa, yb, rz, out, lo, mid, hi):
    z, x, c, y = at.z, at.x, at.c, at.y
    a, b, ab = pl.ds(lo, mid - lo), pl.ds(mid, hi - mid), pl.ds(lo, hi - lo)
    half_a, half_b = pl.ds(0, mid - lo), pl.ds(mid - lo, hi - mid)
    from_c = wire.send(grad.at[:, :, :, at.nc, :, ab], rc, at.to_c)
    yield
    wire.both(from_c)
    add_blocks(rc, grad.at[:, :, :, c, :, ab], rc, (2, 4, 2))
    from_y_a = wire.send(rc.at[at.ny, :, :, :, half_a], ya, at.to_y)
    from_x_b = wire.send(rc.at[:, :, at.nx, :, half_b], xb, at.to_x)
    yield
    from_y_a.wait_recv()
    add_blocks(ya, rc.at[y, :, :, :, half_a], ya, (4, 2))
    from_x_a = wire.send(ya.at[:, at.nx], xa, at.to_x)
    from_x_b.wait_recv()
    add_blocks(xb, rc.at[:, :, x, :, half_b], xb, (2, 4))
    from_y_b = wire.send(xb.at[at.ny], yb, at.to_y)
    yield
    from_x_a.wait_recv()
    add_blocks(xa, ya.at[:, x], xa, (4,))
    from_y_b.wait_recv()
    add_blocks(yb, xb.at[y], yb, (4,))
    from_z = []
    for j, (p, to) in enumerate(zip(at.zs, at.to_z)):
        from_z.append(wire.send(xa.at[p], rz.at[at.count[j], :, half_a], to))
        from_z.append(wire.send(yb.at[p], rz.at[at.count[j], :, half_b], to))
    yield
    for k in from_z:
        k.wait_recv()
    for acc, half, cols in ((xa, half_a, a), (yb, half_b, b)):
        out[:, cols] = (
            (acc[z].astype(F32) + rz[0, :, half].astype(F32)) + rz[1, :, half].astype(F32)
        ) + rz[2, :, half].astype(F32)


def reduce_small(wire, at, mine, sums, got, out):
    k = wire.send(mine, got.at[0], at.to_c)
    yield
    k.wait_recv()
    sums[0] = mine[...] + got[0]
    k = wire.send(sums.at[0], got.at[1], at.to_x)
    yield
    k.wait_recv()
    sums[1] = sums[0] + got[1]
    k = wire.send(sums.at[1], got.at[2], at.to_y)
    yield
    k.wait_recv()
    sums[2] = sums[1] + got[2]
    last = [wire.send(sums.at[2], got.at[3 + j], to) for j, to in enumerate(at.to_z)]
    yield
    for k in last:
        k.wait_recv()
    out[...] = ((sums[2] + got[3]) + got[4]) + got[5]


def turn_rows(src, dst):
    def one(t, _):
        r = pl.ds(pl.multiple_of(t * 128, 128), 128)
        dst[r, :] = src[:, r].astype(F32).T.astype(BF16)
        return 0

    lax.fori_loop(0, src.shape[1] // 128, one, 0)


def backward_kernel(
    ffn_ref, mid_ref, attn_ref, act_ref, pre_ref, mix_ref, qkv_ref, embed_ref, v_ref,
    far_ref, mine_ref, stats_ref, sr_ref, sc_ref, small_ref,
    v_out, o_out, i_out, d_out, x_own, x_got, s_out, *rest,
):
    at = Place()
    y = at.y
    at.enter(False)
    rest = iter(rest)
    wire, local = Wire(at, next(rest), next(rest)), Local(next(rest))
    raw, tr, big, d_heads, d_g, i_g, o_g, v_g, acc_k, acc_v, table, sums, got = (next(rest) for _ in range(13))
    own_rows, width = raw.shape
    hidden, cols, length = big.shape[2], d_heads.shape[2], 2 * own_rows

    def stream(grad, out, cut):
        return reduce_all(wire, at, grad, *(next(rest) for _ in range(6)), out, *cut)

    d_s = [stream(d_g, d_out, cut) for cut in parts_of(hidden, 2)]
    i_s = [stream(i_g, i_out, cut) for cut in parts_of(hidden, 2)]
    o_s = stream(o_g, o_out, parts_of(cols, 1)[0])
    v_s = [reduce_dp(wire, at, v_g.at[k], *(next(rest) for _ in range(3)), v_out.at[k]) for k in range(2)]
    tiny = reduce_small(wire, at, table, sums, got, s_out)

    def done(one):
        one.wait()
        local.open = [other for other in local.open if other is not one]

    from_mix = wire.send(mix_ref.at[at.ny], d_heads.at[y], at.to_y)
    halves = [pl.ds(lo, hi - lo) for lo, _, hi in parts_of(hidden, 2)]
    raw_in = local.copy(ffn_ref, raw)
    big_in = [local.copy(act_ref.at[:, :, cut], big.at[:, :, cut]) for cut in halves]
    mix_in = local.copy(mix_ref.at[y], d_heads.at[y])
    table[...] = small_ref[...]
    done(raw_in)
    turn_rows(raw, tr.at[0])
    raw_in = local.copy(mid_ref, raw)

    chunk = 512
    per = hidden // 2 // chunk

    def products(left, grad, part):
        def one(t, _):
            side = t // per
            n = pl.ds(pl.multiple_of(part * (hidden // 2) + (t % per) * chunk, chunk), chunk)
            made = dg(left[...], big[side, :, n], 1, 0).astype(BF16)
            grad[side, :, :, :, :, n] = made.reshape(grad.shape[1:5] + (chunk,))
            return 0

        lax.fori_loop(0, 2 * per, one, 0)

    for part in range(2):
        done(big_in[part])
        products(tr.at[0], d_g, part)
        next(d_s[part])
        big_in[part] = local.copy(pre_ref.at[:, :, halves[part]], big.at[:, :, halves[part]])
    done(raw_in)
    turn_rows(raw, tr.at[1])
    raw_in = local.copy(attn_ref, raw)
    done(big_in[0])
    products(tr.at[1], i_g, 0)
    next(i_s[0])
    next(d_s[0])
    done(big_in[1])
    products(tr.at[1], i_g, 1)
    next(i_s[1])
    qkv_in = local.copy(qkv_ref, big.at[:, :, 0 : 3 * cols])
    done(raw_in)
    turn_rows(raw, tr.at[0])
    for side, right in ((y, mine_ref.at[y]), (at.ny, far_ref)):
        made = dg(tr[0], right[...], 1, 0).astype(BF16)
        o_g[side] = made.reshape(o_g.shape[1:])
    next(o_s)
    next(d_s[1])

    embed_in = local.copy(embed_ref, d_g.at[0, :, :, :, :, 0:width])
    v_in = local.copy(v_ref, d_g.at[1, :, :, :, :, 0 : v_ref.shape[4]])
    done(embed_in)

    def turn_embed(t, _):
        n = pl.ds(pl.multiple_of(t * 128, 128), 128)
        block = d_g[0, :, :, :, :, n].reshape(length, 128)
        d_g[0, t // 2, t % 2, :, :, width : 2 * width] = (
            block.astype(F32).T.astype(BF16).reshape(d_g.shape[3:5] + (length,))
        )
        return 0

    lax.fori_loop(0, width // 128, turn_embed, 0)
    done(v_in)
    done(qkv_in)
    done(mix_in)
    from_mix.wait_recv()

    part_cols = cols // 2

    def project_grad(k):
        def one(j, _):
            n = pl.ds(pl.multiple_of(j * cols + k * part_cols, part_cols), part_cols)
            made = dg(
                d_g[0, :, :, :, :, width : 2 * width].reshape(width, length),
                big[:, :, n].reshape(length, part_cols), 1, 0,
            ).astype(BF16)
            v_g[k, :, :, :, :, pl.ds(pl.multiple_of(j * part_cols, part_cols), part_cols)] = made.reshape(
                v_g.shape[1:5] + (part_cols,)
            )
            return 0

        lax.fori_loop(0, 3, one, 0)

    pair = 2 * HD
    scale = 1.0 / math.sqrt(HD)
    ticks = {
        0: lambda: next(d_s[0]),
        1: lambda: next(i_s[0]),
        2: lambda: next(i_s[1]),
        3: lambda: (project_grad(0), next(v_s[0]), next(d_s[0])),
        4: lambda: (next(d_s[1]), next(o_s)),
        5: lambda: next(v_s[0]),
        6: lambda: next(i_s[0]),
        7: lambda: (next(d_s[0], None), next(d_s[1])),
    }

    def attend_step(t, _):
        p, half = t // 2, t % 2
        n = pl.multiple_of(p * pair, pair)
        r = pl.ds(pl.multiple_of(half * own_rows, own_rows), own_rows)
        cq, ck, cv = pl.ds(n, pair), pl.ds(cols + n, pair), pl.ds(2 * cols + n, pair)
        same = sc_ref[:, 0:1] == sr_ref[:, r]
        queries = big[half, :, cq]
        keys, values = big[:, :, ck].reshape(length, pair), big[:, :, cv].reshape(length, pair)
        d_rows, o_rows = d_heads[half, :, cq], mine_ref[half, :, cq]
        here = pl.ds(pl.multiple_of(y * cols + n, pair), pair)
        d_q, d_k, d_v = [], [], []
        for h in range(2):
            k = slice(h * HD, h * HD + HD)
            delta = jnp.sum((d_rows[:, k].astype(F32) * o_rows[:, k].astype(F32)).T, axis=0, keepdims=True)
            scores = dg(keys[:, k], queries[:, k], 1, 1) * scale
            prob = jnp.where(same, jnp.exp(scores - stats_ref[p, h : h + 1, r]), 0.0)
            d_prob = dg(values[:, k], d_rows[:, k], 1, 1)
            d_score = (prob * (d_prob - delta) * scale).astype(BF16)
            d_v.append(dg(prob.astype(BF16), d_rows[:, k], 1, 0))
            d_k.append(dg(d_score, queries[:, k], 1, 0))
            d_q.append(dg(d_score, keys[:, k], 0, 0))
        d_q, d_k, d_v = (jnp.concatenate(a, axis=1) for a in (d_q, d_k, d_v))
        big[half, :, cq] = d_q.astype(BF16)
        table[16:17, here] += jnp.sum(d_q, axis=0, keepdims=True)
        table[17:18, here] += jnp.sum(d_v, axis=0, keepdims=True)

        @pl.when(half == 0)
        def _():
            acc_k[...] = d_k
            acc_v[...] = d_v

        @pl.when(half == 1)
        def _():
            big[:, :, ck] = (acc_k[...] + d_k).astype(BF16).reshape(2, own_rows, pair)
            big[:, :, cv] = (acc_v[...] + d_v).astype(BF16).reshape(2, own_rows, pair)

        for k, tick in ticks.items():
            pl.when(t == k)(lambda tick=tick: (tick(), None)[1])
        return 0

    lax.fori_loop(0, 2 * (cols // pair), attend_step, 0)
    project_grad(1)
    next(v_s[1])

    step = 256
    total = table[18:19]
    for half in (at.ny, y):

        def embed_grad(t, acc, half=half):
            r = pl.ds(pl.multiple_of(t * step, step), step)
            made = dg(
                big[half, r, 0 : 3 * cols],
                d_g[1, :, :, :, :, 0 : 3 * cols].reshape(width, 3 * cols), 1, 1,
            )
            i_g[0, 2 * half + t, :, :, :, 0:width] = made.astype(BF16).reshape(i_g.shape[2:5] + (width,))
            return acc + jnp.sum(made, axis=0, keepdims=True)

        total = lax.fori_loop(0, own_rows // step, embed_grad, total)
        if half is y:
            local.copy(i_g.at[0, pl.ds(2 * half, 2), :, :, :, 0:width], x_own)
        else:
            from_x = wire.send(i_g.at[0, pl.ds(2 * half, 2), :, :, :, 0:width], x_got, at.to_y)
    down = lax.broadcasted_iota(jnp.int32, (16, width), 0)
    table[0:16] = jnp.where(down == at.i, total, 0.0)
    left = [tiny, i_s[1], v_s[1], o_s, v_s[0], i_s[0], d_s[1]]
    for _ in range(7):
        for one in left:
            next(one, None)
    from_x.wait_recv()
    local.close()
    wire.close()


def backward(d_ffn, mid, d_attn, act, d_pre, d_mix, qkv, embed, v_all, far, mine, stats, seg_row, seg_col, small):
    own_rows, width = mid.shape
    hidden, cols, rows = act.shape[2], far.shape[1], v_all.shape[3]
    dp3 = (4, 2, 2)
    S = jax.ShapeDtypeStruct
    x_part = S((2, 2, 2, rows, width), BF16)
    outs = [
        S((2, rows, 3 * cols // 2), F32), S((rows, cols), F32), S((rows, hidden), F32), S((rows, hidden), F32),
        x_part, x_part, S(small.shape, F32),
    ]
    wide = S((2,) + dp3 + (rows, hidden), BF16)
    acc = S((2 * own_rows, 2 * HD), F32)
    scratch = [
        S((own_rows, width), BF16), S((2, width, own_rows), BF16), S((2, own_rows, hidden), BF16),
        S((2, own_rows, cols), BF16), wide, wide, S((2,) + dp3 + (rows, cols), BF16),
        S((2,) + dp3 + (rows, 3 * cols // 2), BF16), acc, acc,
        S(small.shape, F32), S((3,) + small.shape, F32), S((6,) + small.shape, F32),
    ]
    copies = 1 + 1 + 6
    for n in [hidden // 2] * 4 + [cols]:
        h = n // 2
        copies += 11
        scratch += [
            S(s, BF16)
            for s in ((2, 4, 2, rows, n), (4, 2, rows, h), (2, 4, rows, h), (4, rows, h), (4, rows, h), (3, rows, n))
        ]
    for n in [3 * cols // 2] * 2:
        copies += 5
        scratch += [S(s, BF16) for s in ((4, 2, rows, n), (4, rows, n), (3, rows, n))]
    vm, hbm = pl.BlockSpec(memory_space=pltpu.VMEM), pl.BlockSpec(memory_space=pl.ANY)
    return pl.pallas_call(
        backward_kernel,
        name="backward",
        out_shape=outs,
        in_specs=[hbm] * 9 + [vm] * 6,
        out_specs=[vm] * 4 + [hbm] * 2 + [vm],
        scratch_shapes=[
            pltpu.SemaphoreType.DMA((copies,)), pltpu.SemaphoreType.DMA((copies,)),
            pltpu.SemaphoreType.DMA((BACKWARD_LOCAL,)),
        ]
        + [pltpu.VMEM(a.shape, a.dtype) for a in scratch],
        compiler_params=pltpu.CompilerParams(
            collective_id=1, has_side_effects=True, vmem_limit_bytes=VMEM_ALL
        ),
    )(d_ffn, mid, d_attn, act, d_pre, d_mix, qkv, embed, v_all, far, mine, stats, seg_row, seg_col, small)


BACKWARD_LOCAL = 12


def attend_kernel(tile, q_ref, k_ref, v_ref, sr_ref, sc_ref, o_ref, l_ref):
    length, width = q_ref.shape

    def step(t, _):
        rows = pl.ds(pl.multiple_of(t * tile, tile), tile)
        same = sc_ref[:, 0:1] == sr_ref[:, rows]
        for h in range(width // HD):
            cols = slice(h * HD, h * HD + HD)
            scores = dg(k_ref[:, cols], q_ref[rows, cols], 1, 1) * (1.0 / math.sqrt(HD))
            scores = jnp.where(same, scores, neg_big)
            row_max = jnp.max(scores, axis=0, keepdims=True)
            prob = jnp.exp(scores - row_max)
            total = jnp.sum(prob, axis=0, keepdims=True)
            mixed = dg(v_ref[:, cols], prob.astype(BF16), 0, 0) / total
            o_ref[rows, cols] = mixed.T.astype(BF16)
            l_ref[0, h : h + 1, rows] = row_max + jnp.log(total)
        return 0

    lax.fori_loop(0, length // tile, step, 0)


def attend_specs(length, heads_pairs):
    def col(k):
        return pl.BlockSpec((length, 2 * HD), lambda i, k=k: (0, k * heads_pairs + i))

    stats = pl.BlockSpec((1, 2, length), lambda i: (i, 0, 0))
    seg_row = pl.BlockSpec((1, length), lambda i: (0, 0))
    seg_col = pl.BlockSpec((length, 128), lambda i: (0, 0))
    return col, stats, seg_row, seg_col


def attend(qkv, segments):
    length = qkv.shape[0]
    pairs = qkv.shape[1] // 3 // (2 * HD)
    col, stats, seg_row, seg_col = attend_specs(length, pairs)
    return pl.pallas_call(
        functools.partial(attend_kernel, min(512, length)),
        name="attend",
        grid=(pairs,),
        in_specs=[col(0), col(1), col(2), seg_row, seg_col],
        out_specs=[col(0), stats],
        out_shape=[
            jax.ShapeDtypeStruct((length, pairs * 2 * HD), BF16),
            jax.ShapeDtypeStruct((pairs, 2, length), F32),
        ],
        cost_estimate=pl.CostEstimate(
            flops=8 * length * length * HD * pairs, bytes_accessed=4 * length * pairs * 256, transcendentals=0
        ),
    )(qkv, qkv, qkv, segments, jnp.broadcast_to(segments.reshape(length, 1), (length, 128)))


def attend_back_kernel(
    tile, q_ref, k_ref, v_ref, d_ref, o_ref, l_ref, sr_ref, sc_ref, dq_ref, dk_ref, dv_ref
):
    length, width = q_ref.shape
    scale = 1.0 / math.sqrt(HD)
    dk_ref[...] = jnp.zeros_like(dk_ref)
    dv_ref[...] = jnp.zeros_like(dv_ref)

    def step(t, _):
        rows = pl.ds(pl.multiple_of(t * tile, tile), tile)
        same = sc_ref[:, 0:1] == sr_ref[:, rows]
        for h in range(width // HD):
            cols = slice(h * HD, h * HD + HD)
            keys, q_rows, d_rows = k_ref[:, cols], q_ref[rows, cols], d_ref[rows, cols]
            delta = jnp.sum(
                (d_rows.astype(F32) * o_ref[rows, cols].astype(F32)).T, axis=0, keepdims=True
            )
            scores = dg(keys, q_rows, 1, 1) * scale
            prob = jnp.where(same, jnp.exp(scores - l_ref[0, h : h + 1, rows]), 0.0)
            d_prob = dg(v_ref[:, cols], d_rows, 1, 1)
            d_score = (prob * (d_prob - delta) * scale).astype(BF16)
            dv_ref[:, cols] += dg(prob.astype(BF16), d_rows, 1, 0)
            dk_ref[:, cols] += dg(d_score, q_rows, 1, 0)
            dq_ref[rows, cols] = dg(d_score, keys, 0, 0)
        return 0

    lax.fori_loop(0, length // tile, step, 0)


def attend_back(qkv, d_mixed, mixed, stats_in, segments):
    length = qkv.shape[0]
    pairs = qkv.shape[1] // 3 // (2 * HD)
    col, stats, seg_row, seg_col = attend_specs(length, pairs)
    return pl.pallas_call(
        functools.partial(attend_back_kernel, min(512, length)),
        name="attend_back",
        grid=(pairs,),
        in_specs=[col(0), col(1), col(2), col(0), col(0), stats, seg_row, seg_col],
        out_specs=[col(0)] * 3,
        out_shape=[jax.ShapeDtypeStruct((length, pairs * 2 * HD), F32)] * 3,
        cost_estimate=pl.CostEstimate(
            flops=20 * length * length * HD * pairs, bytes_accessed=8 * length * pairs * 256, transcendentals=0
        ),
    )(qkv, qkv, qkv, d_mixed, mixed, stats_in, segments, jnp.broadcast_to(segments.reshape(length, 1), (length, 128)))


def time_features(step_ids, model_width):
    half_width = model_width // 2
    frequency = jnp.exp(
        jnp.arange(half_width, dtype=F32) * (-math.log(10000.0) / half_width)
    )
    angles = step_ids.astype(F32)[:, None] * frequency[None, :]
    return jnp.concatenate([jnp.sin(angles), jnp.cos(angles)], axis=1)


def normalize(array_in):
    row_mean = jnp.mean(array_in, axis=-1, keepdims=True)
    centered = array_in - row_mean
    variance = jnp.mean(centered * centered, axis=-1, keepdims=True)
    inv_std = lax.rsqrt(variance + eps)
    return (centered * inv_std, inv_std)


def norm_back(grad_rows, unit_rows, inv_std, gain_row):
    d_unit = grad_rows * gain_row
    return inv_std * (
        d_unit
        - jnp.mean(d_unit, axis=-1, keepdims=True)
        - unit_rows * jnp.mean(d_unit * unit_rows, axis=-1, keepdims=True)
    )


def ein(spec, left, right):
    return jnp.einsum(spec, left, right, preferred_element_type=F32)


def on_device(
    hidden_in,
    segments,
    timesteps,
    time_weight,
    qkv_weight,
    out_weight,
    in_weight,
    down_weight,
    biases,
    gains,
    ffn_bias,
    out_grad,
    *,
    dp,
    mp,
):
    own_rows, width = hidden_in.shape
    length = segments.shape[1]
    rows = time_weight.shape[0]
    cols = qkv_weight.shape[2]
    hidden = in_weight.shape[1]
    dp_index, mp_index = lax.axis_index("dp"), lax.axis_index("mp")
    fast = (dp, mp) == (16, 2)

    bias_count = biases.shape[0] + gains.shape[0]
    v_shard = jnp.concatenate(
        [qkv_weight[0], qkv_weight[1], qkv_weight[2], biases.T, gains.T, jnp.zeros((rows, 128 - bias_count), BF16)],
        axis=1,
    )
    feature = time_features(timesteps, width).astype(BF16)
    few_row = jnp.concatenate([feature.astype(F32), ffn_bias.astype(F32)[None]], axis=1)
    seg_col = jnp.broadcast_to(segments.reshape(length, 1), (length, 128))
    if fast:
        (
            v_all, o_all, i_all, d_all, few, par, time_row, embed_low, qkv, mixed_heads, mixed_far,
            stats, unit_one, inv_one, middle_low, hidden_act, slope,
        ) = forward(
            v_shard, time_weight, few_row, biases[:1], out_weight.T, in_weight, down_weight.T,
            hidden_in, segments, seg_col,
        )
        few = few.reshape(dp, -1)
        inv_one = inv_one[:, :1]
    else:
        v_all = lax.all_gather(v_shard, "dp", axis=0)
        o_all, i_all, d_all = (
            lax.all_gather(lax.all_gather(a, "dp", axis=0), "mp", axis=0)
            for a in (out_weight.T, in_weight, down_weight.T)
        )
        few = lax.all_gather(few_row, "dp", axis=0, tiled=True)
        time_w = lax.all_gather(time_weight, "dp", axis=0, tiled=True)
    v_raw, v_all = v_all, v_all.reshape(width, -1)
    o_all, i_all, d_all = (a.reshape(mp, width, -1) for a in (o_all, i_all, d_all))
    qkv_w = v_all[:, : 3 * cols]
    column = mp_index * cols
    if fast:
        bias_all, gain_all = par[:7], par[7:9]
        middle = unit_one * gain_all[0] + bias_all[4]
    else:
        params = v_all[:, 3 * cols :].astype(F32).T
        bias_all, gain_all = params[:7], params[7:9]
        time_row = jnp.dot(feature, time_w, preferred_element_type=F32) + bias_all[0]
        h_all = lax.all_gather(hidden_in, "mp", axis=0, tiled=True)
        embedded = hidden_in.astype(F32) + time_row
        embed_low = (h_all.astype(F32) + time_row).astype(BF16)
        bias_qkv = jnp.concatenate(
            [
                lax.dynamic_slice_in_dim(bias_all[1], column, cols),
                jnp.zeros((cols,), F32),
                lax.dynamic_slice_in_dim(bias_all[2], column, cols),
            ]
        )
        qkv = (jnp.dot(embed_low, qkv_w, preferred_element_type=F32) + bias_qkv).astype(BF16)
        mixed_heads, stats = attend(qkv, segments)
        mixed = lax.all_to_all(mixed_heads.reshape(mp, own_rows, cols), "mp", 0, 0, tiled=True)
        attn_total = ein("yrk,ynk->rn", mixed, o_all)
        unit_one, inv_one = normalize(embedded + attn_total + bias_all[3])
        middle = unit_one * gain_all[0] + bias_all[4]
        middle_low = middle.astype(BF16)
        ffn_b = few[:, width:].reshape(mp, hidden)
        pre_act = ein("rd,ydf->yrf", middle_low, i_all) + ffn_b[:, None, :]
        below = 0.5 + 0.5 * lax.erf(pre_act * math.sqrt(0.5))
        hidden_act = (pre_act * below).astype(BF16)
        slope = below + pre_act * jnp.exp(-0.5 * pre_act * pre_act) * (1.0 / math.sqrt(2.0 * math.pi))

    ffn_total = ein("yrf,ynf->rn", hidden_act, d_all)
    unit_two, inv_two = normalize(middle + ffn_total + bias_all[5])
    layer_out = (unit_two * gain_all[1] + bias_all[6]).astype(BF16)

    grad_out = out_grad.astype(F32)
    gain_two_part = jnp.sum(grad_out * unit_two, axis=0)
    shift_two_part = jnp.sum(grad_out, axis=0)
    d_pre_two = norm_back(grad_out, unit_two, inv_two, gain_all[1])
    bias_five_part = jnp.sum(d_pre_two, axis=0)
    d_ffn = d_pre_two.astype(BF16)
    d_act = ein("rn,ynf->yrf", d_ffn, d_all)
    d_pre_act = d_act * slope.astype(F32)
    ffn_bias_part = jnp.sum(d_pre_act, axis=1).reshape(-1, width)
    d_pre_low = d_pre_act.astype(BF16)
    d_middle = d_pre_two + ein("yrf,ydf->rd", d_pre_low, i_all)
    gain_one_part = jnp.sum(d_middle * unit_one, axis=0)
    shift_one_part = jnp.sum(d_middle, axis=0)
    d_pre_one = norm_back(d_middle, unit_one, inv_one, gain_all[0])
    bias_three_part = jnp.sum(d_pre_one, axis=0)
    d_attn = d_pre_one.astype(BF16)
    d_mix = ein("rn,ynk->yrk", d_attn, o_all).astype(BF16)
    zero_row = jnp.zeros((width,), F32)
    sums = [bias_three_part, shift_one_part, bias_five_part, shift_two_part, gain_one_part, gain_two_part]

    def pad_rows(a):
        return jnp.pad(a, ((0, -a.shape[0] % 8), (0, 0)))

    if fast:
        small = jnp.concatenate([jnp.zeros((dp + 2, width), F32), jnp.stack(sums), ffn_bias_part], axis=0)
        v_sum, o_sum, i_sum, d_sum, d_near, d_far, small = backward(
            d_ffn, middle_low, d_attn, hidden_act, d_pre_low, d_mix, qkv.reshape(mp, own_rows, -1),
            embed_low.reshape(v_raw.shape[:4] + (width,)), v_raw, mixed_far, mixed_heads, stats, segments, seg_col,
            pad_rows(small),
        )
        d_own = (d_near.astype(F32) + d_far.astype(F32)).reshape(own_rows, width)
        qkv_grad = v_sum.reshape(2, rows, 3, -1).transpose(2, 1, 0, 3).reshape(3, rows, cols)
    else:
        embed_low = embed_low.reshape(length, width)
        mixed_heads = mixed_heads.reshape(length, cols)
        down_grad = ein("rn,yrf->ynf", d_ffn, hidden_act).astype(BF16)
        in_grad = ein("rd,yrf->ydf", middle_low, d_pre_low).astype(BF16)
        out_grad_t = ein("rn,yrk->ynk", d_attn, mixed).astype(BF16)
        d_mixed = lax.all_to_all(d_mix, "mp", 0, 0, tiled=True).reshape(length, cols)
        d_q, d_k, d_v = attend_back(qkv, d_mixed, mixed_heads, stats, segments)
        d_qkv = jnp.concatenate([d_q, d_k, d_v], axis=1).astype(BF16)
        v_grad = dg(embed_low, d_qkv, 0, 0).astype(BF16)
        d_embed = dg(d_qkv, qkv_w, 1, 1)
        time_part = bias_three_part + jnp.sum(d_embed, axis=0)
        d_embed = d_embed.astype(BF16).reshape(mp, own_rows, width)
        seq_rows = jnp.where(jnp.arange(dp)[:, None] == dp_index, time_part[None, :], 0.0)
        spread = [lax.dynamic_update_slice_in_dim(zero_row, jnp.sum(a, axis=0), column, 0) for a in (d_q, d_v)]
        small = pad_rows(jnp.concatenate([seq_rows, jnp.stack(spread + sums), ffn_bias_part], axis=0))
        v_sum = lax.psum_scatter(v_grad, "dp", scatter_dimension=0, tiled=True).astype(F32)

        def both(a):
            a = lax.psum_scatter(a, "mp", scatter_dimension=0)
            return lax.psum_scatter(a, "dp", scatter_dimension=0, tiled=True).astype(F32)

        o_sum, i_sum, d_sum = both(out_grad_t), both(in_grad), both(down_grad)
        d_own = lax.psum_scatter(d_embed, "mp", scatter_dimension=0).astype(F32)
        small = lax.psum(small, ("dp", "mp"))
        qkv_grad = v_sum.reshape(rows, 3, cols).transpose(1, 0, 2)

    input_grad = d_pre_one + d_own
    d_time = small[:dp]
    start = dp_index * rows
    features = few[:, :width]
    features = lax.dynamic_slice_in_dim(features, start, rows, axis=1)
    time_grad = lax.dot_general(
        features, d_time, (((0,), (0,)), ((), ())), precision=lax.Precision.HIGHEST
    )
    tail = small[dp:]
    bias_rows = jnp.concatenate([jnp.sum(d_time, axis=0)[None], tail[:6]], axis=0)
    bias_grad = lax.dynamic_slice_in_dim(bias_rows, start, rows, axis=1)
    gain_grad = lax.dynamic_slice_in_dim(tail[6:8], start, rows, axis=1)
    ffn_rows = ffn_bias.shape[0]
    ffn_all = tail[8:].reshape(-1)
    ffn_bias_grad = lax.dynamic_slice_in_dim(ffn_all, dp_index * ffn_rows, ffn_rows)
    return (
        layer_out,
        input_grad,
        time_grad,
        qkv_grad,
        o_sum.T,
        i_sum,
        d_sum.T,
        bias_grad,
        gain_grad,
        ffn_bias_grad,
    )


def solution(mesh):
    dp, mp = mesh.shape["dp"], mesh.shape["mp"]
    placed = (
        P(("dp", "mp"), None),
        P("dp", None),
        P("dp"),
        P("dp", None),
        P(None, "dp", "mp"),
        P("mp", "dp"),
        P("dp", "mp"),
        P("mp", "dp"),
        P(None, "dp"),
        P(None, "dp"),
        P("dp"),
        P(("dp", "mp"), None),
    )
    return jax.shard_map(
        functools.partial(on_device, dp=dp, mp=mp),
        mesh=mesh,
        in_specs=placed,
        out_specs=(
            P(("dp", "mp"), None),
            P(("dp", "mp"), None),
            P("dp", None),
            P(None, "dp", "mp"),
            P("mp", "dp"),
            P("dp", "mp"),
            P("mp", "dp"),
            P(None, "dp"),
            P(None, "dp"),
            P("dp"),
        ),
        check_vma=False,
    )
```

```python
import functools
import math

import jax
import jax.numpy as jnp
from jax import lax
from jax.experimental import pallas as pl
from jax.experimental.pallas import tpu as pltpu
from jax.sharding import PartitionSpec as P

HD = 64
eps = 1e-05
neg_big = -1000000000.0
MESH = pl.DeviceIdType.MESH
F32, BF16 = jnp.float32, jnp.bfloat16
VMEM_LIMIT, VMEM_ALL = 64000000, 67043328


def dg(left, right, left_dim, right_dim):
    return lax.dot_general(
        left, right, (((left_dim,), (right_dim,)), ((), ())), preferred_element_type=F32
    )


class Place:
    def __init__(self):
        i, y = lax.axis_index("dp"), lax.axis_index("mp")
        z, x, c = i // 4, (i // 2) % 2, i % 2
        self.i, self.z, self.x, self.c, self.y = i, z, x, c, y
        self.nx, self.nc, self.ny, self.zero = 1 - x, 1 - c, 1 - y, 0 * i
        low, high = z % 2, z // 2
        flipped = [(1 - 2 * bit) * v + bit for v, bit in ((low, 1), (high, 1))]
        self.zs = [high * 2 + flipped[0], flipped[1] * 2 + low, flipped[1] * 2 + flipped[0]]
        self.to_z = [((p * 2 + x) * 2 + c, y) for p in self.zs]
        self.to_x = ((z * 2 + self.nx) * 2 + c, y)
        self.to_y = (i, self.ny)
        self.to_c = ((z * 2 + x) * 2 + self.nc, y)
        self.count = [self.zero + j for j in range(3)]
        self.dp = [
            (pz * 2 + px) * 2 + pc
            for pz in [z] + self.zs
            for px in (x, self.nx)
            for pc in (c, self.nc)
        ][1:]

    def enter(self, all_dp):
        barrier = pltpu.get_barrier_semaphore()
        near = [self.to_y]
        near += [(p, self.y) for p in self.dp] if all_dp else self.to_z + [self.to_x, self.to_c]
        for one in near:
            pl.semaphore_signal(barrier, inc=1, device_id=one, device_id_type=MESH)
        pl.semaphore_wait(barrier, len(near))


class Wire:
    def __init__(self, at, send_sems, recv_sems):
        self.sems = [(send_sems.at[at.zero + k], recv_sems.at[at.zero + k]) for k in range(send_sems.shape[0])]
        self.used, self.open = 0, []

    def send(self, src, dst, to):
        k = self.used
        self.used += 1
        copy = pltpu.make_async_remote_copy(
            src_ref=src,
            dst_ref=dst,
            send_sem=self.sems[k][0],
            recv_sem=self.sems[k][1],
            device_id=to,
            device_id_type=MESH,
        )
        copy.start()
        self.open.append(copy)
        return copy

    def both(self, copy):
        copy.wait_send()
        self.open = [one for one in self.open if one is not copy]
        copy.wait_recv()

    def close(self):
        assert self.used == len(self.sems), self.used
        for copy in self.open:
            copy.wait_send()


class Local:
    def __init__(self, sems):
        self.sems, self.used, self.open = sems, 0, []

    def copy(self, src, dst):
        one = pltpu.make_async_copy(src, dst, self.sems.at[self.used])
        self.used += 1
        one.start()
        self.open.append(one)
        return one

    def close(self):
        assert self.used == self.sems.shape[0], self.used
        for one in self.open:
            one.wait()


def parts_of(width, parts, first=0.5):
    step = width // parts
    return [(p * step, p * step + int(step * first), (p + 1) * step) for p in range(parts)]


def stagger(streams, ahead=0):
    for depth in range(ahead, len(streams) + 6):
        for k, s in enumerate(streams):
            if k <= depth:
                next(s, None)


def gather_dp(wire, at, shard, whole, lo, hi):
    n = pl.ds(lo, hi - lo)
    own = whole.at[at.z, at.x, at.c, :, n]
    from_z = [wire.send(shard.at[:, n], own, to) for to in at.to_z]
    late = [wire.send(shard.at[:, n], own, at.to_c)]
    yield
    for k in from_z:
        k.wait_recv()
    ref = whole.at[:, at.x, at.c, :, n]
    from_x = wire.send(ref, ref, at.to_x)
    for p in at.zs:
        ref = whole.at[p, at.x, at.c, :, n]
        late.append(wire.send(ref, ref, at.to_c))
    yield
    from_x.wait_recv()
    ref = whole.at[:, at.nx, at.c, :, n]
    late.append(wire.send(ref, ref, at.to_c))
    yield
    for k in late:
        k.wait_recv()


def gather_all(wire, at, shard, whole, lo, mid, hi):
    a, b, ab = pl.ds(lo, mid - lo), pl.ds(mid, hi - mid), pl.ds(lo, hi - lo)
    y, z, x, c = at.y, at.z, at.x, at.c
    from_z_a = [wire.send(shard.at[:, a], whole.at[y, z, x, c, :, a], to) for to in at.to_z]
    from_y_b = wire.send(shard.at[:, b], whole.at[y, z, x, c, :, b], at.to_y)
    late = [wire.send(shard.at[:, ab], whole.at[y, z, x, c, :, ab], at.to_c)]

    def to_core(*refs):
        for ref in refs:
            late.append(wire.send(ref, ref, at.to_c))

    yield
    from_y_b.wait_recv()
    ref = whole.at[:, z, x, c, :, b]
    from_z_b = [wire.send(ref, ref, to) for to in at.to_z]
    to_core(whole.at[at.ny, z, x, c, :, b])
    yield
    for k in from_z_a:
        k.wait_recv()
    ref = whole.at[y, :, x, c, :, a]
    from_x_a = wire.send(ref, ref, at.to_x)
    to_core(*(whole.at[y, p, x, c, :, a] for p in at.zs))
    yield
    from_x_a.wait_recv()
    ref = whole.at[y, :, :, c, :, a]
    from_y_a = wire.send(ref, ref, at.to_y)
    to_core(whole.at[y, :, at.nx, c, :, a])
    yield
    for k in from_z_b:
        k.wait_recv()
    ref = whole.at[:, :, x, c, :, b]
    from_x_b = wire.send(ref, ref, at.to_x)
    to_core(*(whole.at[:, p, x, c, :, b] for p in at.zs))
    yield
    from_y_a.wait_recv()
    from_x_b.wait_recv()
    to_core(whole.at[at.ny, :, :, c, :, a], whole.at[:, :, at.nx, c, :, b])
    yield
    for k in late:
        k.wait_recv()


def one_hot_rows(count, width, start):
    down = lax.broadcasted_iota(jnp.int32, (count, width), 0)
    across = lax.broadcasted_iota(jnp.int32, (count, width), 1)
    return jnp.where(down == across + start, 1.0, 0.0).astype(BF16)


def forward_kernel(
    v_ref, t_ref, f_ref, b_ref, o_ref, i_ref, d_ref, h_ref, sr_ref, sc_ref,
    v_out, o_out, i_out, d_all, few_out, par_out, time_out, embed_out, qkv_out, mine_out, far_out,
    stats_out, unit_out, inv_out, mid_out, act_out, slope_out,
    v_all, o_all, i_all, few, part, got, h_far, par, ffn_b, embed, qkv, mine, far, stats, unit, inv,
    mid, act, slope, send_sems, recv_sems, local_sems, tile_sems,
):
    at = Place()
    y, z, x, c = at.y, at.z, at.x, at.c
    at.enter(True)
    wire, local = Wire(at, send_sems, recv_sems), Local(local_sems)
    width = h_ref.shape[1]
    own_rows = h_ref.shape[0]
    rows = v_ref.shape[0]
    cols = o_ref.shape[1]
    hidden = i_ref.shape[1]
    length = 2 * own_rows

    from_few = [wire.send(f_ref, few.at[at.i], (p, y)) for p in at.dp]
    from_h = wire.send(h_ref, h_far, at.to_y)
    v_mid = 7 * 128
    v0 = gather_dp(wire, at, v_ref, v_all, 0, v_mid)
    v1 = gather_dp(wire, at, v_ref, v_all, v_mid, v_ref.shape[1])
    out_w = gather_all(wire, at, o_ref, o_all, *parts_of(cols, 1)[0])
    in_w = [gather_all(wire, at, i_ref, i_all, *cut) for cut in parts_of(hidden, 2, 0.625)]
    down_w = [gather_all(wire, at, d_ref, d_all, *cut) for cut in parts_of(hidden, 2, 0.625)]
    kept = [
        local.copy(v_ref, v_all.at[z, x, c]),
        local.copy(o_ref, o_all.at[y, z, x, c]),
        local.copy(i_ref, i_all.at[y, z, x, c]),
        local.copy(d_ref, d_all.at[y, z, x, c]),
    ]
    next(v0)
    next(v1)
    next(out_w)
    next(in_w[0])
    few[at.i] = f_ref[...]
    for k in from_few:
        k.wait_recv()
    seqs = few.shape[0]
    table = jnp.concatenate([few[s] for s in range(seqs)], axis=0)
    pick = one_hot_rows(width, rows, at.i * rows)
    feats = dg(table[:, :width].astype(BF16), pick, 1, 0).astype(BF16)
    partial = dg(feats, t_ref[...], 1, 0) + dg(b_ref[...], pick, 1, 1)
    for s in range(seqs):
        part[s] = partial[s : s + 1]
    ffn_b[...] = jnp.concatenate([few[s][:, width:] for s in range(seqs)], axis=1)
    local.copy(few, few_out)
    from_part = [wire.send(part.at[p], got.at[j], (p, y)) for j, p in enumerate(at.dp)]
    for k in kept:
        k.wait()
        local.open.remove(k)
    next(v0)
    next(v1)
    next(out_w)
    next(in_w[1])
    next(down_w[0])
    next(v0)
    next(out_w)
    for k in from_part:
        k.wait_recv()
    total = part[at.i]
    for j in range(seqs - 1):
        total = total + got[j]
    time_out[...] = total
    next(in_w[0])
    next(v1)
    next(in_w[0])
    next(v0, None)

    from_h.wait_recv()
    step = 128

    def embed_rows(t, _):
        r = pl.ds(pl.multiple_of(t * step, step), step)
        embed[y, r] = (h_ref[r].astype(F32) + total).astype(BF16)
        embed[at.ny, r] = (h_far[r].astype(F32) + total).astype(BF16)
        return 0

    lax.fori_loop(0, own_rows // step, embed_rows, 0)
    local.copy(embed, embed_out)
    next(v1, None)
    next(in_w[1])
    next(out_w)
    next(down_w[1])
    local.copy(v_all, v_out)
    par[...] = v_all[:, :, :, :, 3 * cols :].reshape(width, 128).astype(F32).T
    local.copy(par, par_out)
    heads = pl.ds(pl.multiple_of(y * cols, cols), cols)
    bias_q, bias_v = par[1:2, heads], par[2:3, heads]

    step_q = 256

    def project(t, _):
        half, r = t // (own_rows // step_q), pl.ds(pl.multiple_of((t % (own_rows // step_q)) * step_q, step_q), step_q)
        whole_r = pl.ds(pl.multiple_of(t * step_q, step_q), step_q)
        left = embed[half, r]
        for j, bias in enumerate((bias_q, None, bias_v)):
            n = slice(j * cols, (j + 1) * cols)
            made = dg(left, v_all[:, :, :, :, n].reshape(width, cols), 1, 0)
            qkv[whole_r, n] = (made if bias is None else made + bias).astype(BF16)
        return 0

    lax.fori_loop(0, length // step_q, project, 0)
    local.copy(qkv, qkv_out)
    next(in_w[0])
    next(out_w)

    pair, tile = 2 * HD, own_rows
    from_far = []

    def give(p):
        n = pl.ds(p * pair, pair)
        from_far.append(wire.send(mine.at[at.ny, :, n], far.at[:, n], at.to_y))

    ticks = {
        1: lambda: (give(0), next(down_w[0]), next(down_w[1]), next(in_w[1]),),
        3: lambda: (give(1), next(in_w[1]), next(down_w[0]), next(in_w[0]),),
        5: lambda: (give(2),),
        6: lambda: (next(in_w[1]), next(out_w),),
        7: lambda: (give(3), next(in_w[0]), next(down_w[0]), next(out_w, None), next(in_w[1]), next(down_w[1]), next(in_w[0], None), next(down_w[0]),),
    }

    def attend_step(t, _):
        p, half = t // 2, t % 2
        r = pl.ds(pl.multiple_of(half * tile, tile), tile)
        n = pl.multiple_of(p * pair, pair)
        queries = qkv[r, pl.ds(n, pair)]
        keys = qkv[:, pl.ds(cols + n, pair)]
        values = qkv[:, pl.ds(2 * cols + n, pair)]
        same = sc_ref[:, 0:1] == sr_ref[:, r]
        made = []
        for h in range(2):
            k = slice(h * HD, h * HD + HD)
            scores = dg(keys[:, k], queries[:, k], 1, 1) * (1.0 / math.sqrt(HD))
            scores = jnp.where(same, scores, neg_big)
            row_max = jnp.max(scores, axis=0, keepdims=True)
            prob = jnp.exp(scores - row_max)
            row_total = jnp.sum(prob, axis=0, keepdims=True)
            made.append((dg(values[:, k], prob.astype(BF16), 0, 0) / row_total).T)
            stats[p, h : h + 1, r] = row_max + jnp.log(row_total)
        mine[half, :, pl.ds(n, pair)] = jnp.concatenate(made, axis=1).astype(BF16)
        for k, tick in ticks.items():
            pl.when(t == k)(lambda tick=tick: (tick(), None)[1])
        return 0

    lax.fori_loop(0, 2 * (cols // pair), attend_step, 0)
    local.copy(mine, mine_out)
    local.copy(stats, stats_out)
    local.copy(o_all, o_out)

    for k in from_far:
        k.wait_recv()
    local.copy(far, far_out)

    def project_out(t, _):
        r = pl.ds(pl.multiple_of(t * step_q, step_q), step_q)
        total_r = dg(mine[y, r], o_all[y].reshape(width, cols), 1, 1)
        total_r += dg(far[r], o_all[at.ny].reshape(width, cols), 1, 1)
        total_r += h_ref[r].astype(F32) + total + par[3:4]
        made, inv_std = normalize(total_r)
        unit[r] = made
        inv[r] = jnp.broadcast_to(inv_std, (step_q, 128))
        mid[r] = (made * par[7:8] + par[4:5]).astype(BF16)
        return 0

    lax.fori_loop(0, own_rows // step_q, project_out, 0)
    local.copy(unit, unit_out)
    local.copy(inv, inv_out)
    local.copy(mid, mid_out)


    chunk = 512
    per = hidden // 2 // chunk
    later = {
        0: lambda: (next(down_w[1]),),
        2: lambda: (next(in_w[1], None), next(down_w[1]),),
        4: lambda: (next(down_w[0]),),
        6: lambda: (next(down_w[1]),),
    }

    def feed_step(t, _):
        side = (t // per) % 2
        n = pl.multiple_of((t // (2 * per)) * (hidden // 2) + (t % per) * chunk, chunk)
        made = dg(mid[...], i_all[side, :, :, :, :, pl.ds(n, chunk)].reshape(width, chunk), 1, 0)
        made = made + ffn_b[:, pl.ds(pl.multiple_of(side * hidden, hidden) + n, chunk)]
        below = 0.5 + 0.5 * lax.erf(made * math.sqrt(0.5))
        act[side, :, pl.ds(n, chunk)] = (made * below).astype(BF16)
        bell = jnp.exp(-0.5 * made * made) * (1.0 / math.sqrt(2.0 * math.pi))
        slope[side, :, pl.ds(n, chunk)] = (below + made * bell).astype(BF16)
        pltpu.make_async_copy(
            act.at[side, :, pl.ds(n, chunk)], act_out.at[side, :, pl.ds(n, chunk)], tile_sems.at[0, t]
        ).start()
        pltpu.make_async_copy(
            slope.at[side, :, pl.ds(n, chunk)], slope_out.at[side, :, pl.ds(n, chunk)], tile_sems.at[1, t]
        ).start()
        for k, tick in later.items():
            pl.when(t == k)(lambda tick=tick: (tick(), None)[1])
        return 0

    tiles = 4 * per
    lax.fori_loop(0, tiles, feed_step, 0)
    local.copy(i_all, i_out)
    next(down_w[0], None)
    next(down_w[1], None)
    for t in range(tiles):
        n = pl.ds(0, chunk)
        pltpu.make_async_copy(act.at[0, :, n], act_out.at[0, :, n], tile_sems.at[0, t]).wait()
        pltpu.make_async_copy(slope.at[0, :, n], slope_out.at[0, :, n], tile_sems.at[1, t]).wait()
    local.close()
    wire.close()


def forward(v, t, few_row, bias_zero, o, i, d, h, seg_row, seg_col):
    rows, cols, hidden = v.shape[0], o.shape[1], i.shape[1]
    own_rows, width = h.shape
    length = 2 * own_rows
    pairs = cols // (2 * HD)
    S = jax.ShapeDtypeStruct
    dp3 = (4, 2, 2)
    v_all, o_all, i_all = S(dp3 + v.shape, BF16), S((2,) + dp3 + o.shape, BF16), S((2,) + dp3 + i.shape, BF16)
    few = S((16,) + few_row.shape, F32)
    par, time_row = S((128, width), F32), S((1, width), F32)
    embed, qkv = S((2, own_rows, width), BF16), S((length, 3 * cols), BF16)
    mine, far = S((2, own_rows, cols), BF16), S((own_rows, cols), BF16)
    stats = S((pairs, 2, length), F32)
    unit, inv, mid = S((own_rows, width), F32), S((own_rows, 128), F32), S((own_rows, width), BF16)
    act = S((2, own_rows, hidden), BF16)
    outs = [v_all, o_all, i_all, i_all, few, par, time_row, embed, qkv, mine, far, stats, unit, inv, mid, act, act]
    vm, hbm = pl.BlockSpec(memory_space=pltpu.VMEM), pl.BlockSpec(memory_space=pl.ANY)
    out_specs = [hbm] * len(outs)
    out_specs[6] = vm
    part, got = S((16, 1, width), F32), S((15, 1, width), F32)
    h_far, ffn_b = S(h.shape, BF16), S((1, 2 * hidden), F32)
    scratch = [v_all, o_all, i_all, few, part, got, h_far, par, ffn_b, embed, qkv, mine, far, stats, unit, inv, mid, act, act]
    copies = 15 + 15 + 1 + 2 * 9 + 5 * 21 + pairs
    return pl.pallas_call(
        forward_kernel,
        name="forward",
        out_shape=outs,
        in_specs=[vm] * 10,
        out_specs=out_specs,
        scratch_shapes=[pltpu.VMEM(a.shape, a.dtype) for a in scratch]
        + [
            pltpu.SemaphoreType.DMA((copies,)),
            pltpu.SemaphoreType.DMA((copies,)),
            pltpu.SemaphoreType.DMA((FORWARD_LOCAL,)),
            pltpu.SemaphoreType.DMA((2, 2 * hidden // 512)),
        ],
        compiler_params=pltpu.CompilerParams(
            collective_id=0, has_side_effects=True, vmem_limit_bytes=VMEM_LIMIT
        ),
    )(v, t, few_row, bias_zero, o, i, d, h, seg_row, seg_col)


FORWARD_LOCAL = 17


def add_blocks(dst, left, right, lead):
    count = math.prod(lead)

    def one(t, _):
        at = []
        for n in reversed(lead):
            at.append(t % n)
            t = t // n
        at = tuple(reversed(at))
        dst[at] = (left[at].astype(F32) + right[at].astype(F32)).astype(dst.dtype)
        return 0

    lax.fori_loop(0, count, one, 0)


def reduce_dp(wire, at, grad, rc, rx, rz, out):
    z, x, c, y = at.z, at.x, at.c, at.y
    from_c = wire.send(grad.at[:, :, at.nc], rc, at.to_c)
    yield
    wire.both(from_c)
    add_blocks(rc, grad.at[:, :, c], rc, (4, 2))
    from_x = wire.send(rc.at[:, at.nx], rx, at.to_x)
    yield
    from_x.wait_recv()
    add_blocks(rx, rc.at[:, x], rx, (4,))
    from_z = [wire.send(rx.at[p], rz.at[at.count[j]], to) for j, (p, to) in enumerate(zip(at.zs, at.to_z))]
    yield
    for k in from_z:
        k.wait_recv()
    out[...] = ((rx[z].astype(F32) + rz[0].astype(F32)) + rz[1].astype(F32)) + rz[2].astype(F32)


def reduce_all(wire, at, grad, rc, ya, xb, xa, yb, rz, out, lo, mid, hi):
    z, x, c, y = at.z, at.x, at.c, at.y
    a, b, ab = pl.ds(lo, mid - lo), pl.ds(mid, hi - mid), pl.ds(lo, hi - lo)
    half_a, half_b = pl.ds(0, mid - lo), pl.ds(mid - lo, hi - mid)
    from_c = wire.send(grad.at[:, :, :, at.nc, :, ab], rc, at.to_c)
    yield
    wire.both(from_c)
    add_blocks(rc, grad.at[:, :, :, c, :, ab], rc, (2, 4, 2))
    from_y_a = wire.send(rc.at[at.ny, :, :, :, half_a], ya, at.to_y)
    from_x_b = wire.send(rc.at[:, :, at.nx, :, half_b], xb, at.to_x)
    yield
    from_y_a.wait_recv()
    add_blocks(ya, rc.at[y, :, :, :, half_a], ya, (4, 2))
    from_x_a = wire.send(ya.at[:, at.nx], xa, at.to_x)
    from_x_b.wait_recv()
    add_blocks(xb, rc.at[:, :, x, :, half_b], xb, (2, 4))
    from_y_b = wire.send(xb.at[at.ny], yb, at.to_y)
    yield
    from_x_a.wait_recv()
    add_blocks(xa, ya.at[:, x], xa, (4,))
    from_y_b.wait_recv()
    add_blocks(yb, xb.at[y], yb, (4,))
    from_z = []
    for j, (p, to) in enumerate(zip(at.zs, at.to_z)):
        from_z.append(wire.send(xa.at[p], rz.at[at.count[j], :, half_a], to))
        from_z.append(wire.send(yb.at[p], rz.at[at.count[j], :, half_b], to))
    yield
    for k in from_z:
        k.wait_recv()
    for acc, half, cols in ((xa, half_a, a), (yb, half_b, b)):
        out[:, cols] = (
            (acc[z].astype(F32) + rz[0, :, half].astype(F32)) + rz[1, :, half].astype(F32)
        ) + rz[2, :, half].astype(F32)


def reduce_small(wire, at, mine, sums, got, out):
    k = wire.send(mine, got.at[0], at.to_c)
    yield
    k.wait_recv()
    sums[0] = mine[...] + got[0]
    k = wire.send(sums.at[0], got.at[1], at.to_x)
    yield
    k.wait_recv()
    sums[1] = sums[0] + got[1]
    k = wire.send(sums.at[1], got.at[2], at.to_y)
    yield
    k.wait_recv()
    sums[2] = sums[1] + got[2]
    last = [wire.send(sums.at[2], got.at[3 + j], to) for j, to in enumerate(at.to_z)]
    yield
    for k in last:
        k.wait_recv()
    out[...] = ((sums[2] + got[3]) + got[4]) + got[5]


def turn_rows(src, dst):
    def one(t, _):
        r = pl.ds(pl.multiple_of(t * 128, 128), 128)
        dst[r, :] = src[:, r].astype(F32).T.astype(BF16)
        return 0

    lax.fori_loop(0, src.shape[1] // 128, one, 0)


def backward_kernel(
    ffn_ref, mid_ref, attn_ref, act_ref, pre_ref, mix_ref, qkv_ref, embed_ref, v_ref,
    far_ref, mine_ref, stats_ref, sr_ref, sc_ref, small_ref,
    v_out, o_out, i_out, d_out, x_own, x_got, s_out, *rest,
):
    at = Place()
    y = at.y
    at.enter(False)
    rest = iter(rest)
    wire, local = Wire(at, next(rest), next(rest)), Local(next(rest))
    raw, tr, big, d_heads, d_g, i_g, o_g, v_g, acc_k, acc_v, table, sums, got = (next(rest) for _ in range(13))
    own_rows, width = raw.shape
    hidden, cols, length = big.shape[2], d_heads.shape[2], 2 * own_rows

    def stream(grad, out, cut):
        return reduce_all(wire, at, grad, *(next(rest) for _ in range(6)), out, *cut)

    d_s = [stream(d_g, d_out, cut) for cut in parts_of(hidden, 2)]
    i_s = [stream(i_g, i_out, cut) for cut in parts_of(hidden, 2)]
    o_s = stream(o_g, o_out, parts_of(cols, 1)[0])
    v_s = [reduce_dp(wire, at, v_g.at[k], *(next(rest) for _ in range(3)), v_out.at[k]) for k in range(2)]
    tiny = reduce_small(wire, at, table, sums, got, s_out)

    def done(one):
        one.wait()
        local.open = [other for other in local.open if other is not one]

    from_mix = wire.send(mix_ref.at[at.ny], d_heads.at[y], at.to_y)
    halves = [pl.ds(lo, hi - lo) for lo, _, hi in parts_of(hidden, 2)]
    raw_in = local.copy(ffn_ref, raw)
    big_in = [local.copy(act_ref.at[:, :, cut], big.at[:, :, cut]) for cut in halves]
    mix_in = local.copy(mix_ref.at[y], d_heads.at[y])
    table[...] = small_ref[...]
    done(raw_in)
    turn_rows(raw, tr.at[0])
    raw_in = local.copy(mid_ref, raw)

    chunk = 512
    per = hidden // 2 // chunk

    def products(left, grad, part):
        def one(t, _):
            side = t // per
            n = pl.ds(pl.multiple_of(part * (hidden // 2) + (t % per) * chunk, chunk), chunk)
            made = dg(left[...], big[side, :, n], 1, 0).astype(BF16)
            grad[side, :, :, :, :, n] = made.reshape(grad.shape[1:5] + (chunk,))
            return 0

        lax.fori_loop(0, 2 * per, one, 0)

    for part in range(2):
        done(big_in[part])
        products(tr.at[0], d_g, part)
        next(d_s[part])
        big_in[part] = local.copy(pre_ref.at[:, :, halves[part]], big.at[:, :, halves[part]])
    done(raw_in)
    turn_rows(raw, tr.at[1])
    raw_in = local.copy(attn_ref, raw)
    done(big_in[0])
    products(tr.at[1], i_g, 0)
    next(i_s[0])
    next(d_s[0])
    done(big_in[1])
    products(tr.at[1], i_g, 1)
    next(i_s[1])
    qkv_in = local.copy(qkv_ref, big.at[:, :, 0 : 3 * cols])
    done(raw_in)
    turn_rows(raw, tr.at[0])
    for side, right in ((y, mine_ref.at[y]), (at.ny, far_ref)):
        made = dg(tr[0], right[...], 1, 0).astype(BF16)
        o_g[side] = made.reshape(o_g.shape[1:])
    next(o_s)
    next(d_s[1])

    embed_in = local.copy(embed_ref, d_g.at[0, :, :, :, :, 0:width])
    v_in = local.copy(v_ref, d_g.at[1, :, :, :, :, 0 : v_ref.shape[4]])
    done(embed_in)

    def turn_embed(t, _):
        n = pl.ds(pl.multiple_of(t * 128, 128), 128)
        block = d_g[0, :, :, :, :, n].reshape(length, 128)
        d_g[0, t // 2, t % 2, :, :, width : 2 * width] = (
            block.astype(F32).T.astype(BF16).reshape(d_g.shape[3:5] + (length,))
        )
        return 0

    lax.fori_loop(0, width // 128, turn_embed, 0)
    done(v_in)
    done(qkv_in)
    done(mix_in)
    from_mix.wait_recv()

    part_cols = cols // 2

    def project_grad(k):
        def one(j, _):
            n = pl.ds(pl.multiple_of(j * cols + k * part_cols, part_cols), part_cols)
            made = dg(
                d_g[0, :, :, :, :, width : 2 * width].reshape(width, length),
                big[:, :, n].reshape(length, part_cols), 1, 0,
            ).astype(BF16)
            v_g[k, :, :, :, :, pl.ds(pl.multiple_of(j * part_cols, part_cols), part_cols)] = made.reshape(
                v_g.shape[1:5] + (part_cols,)
            )
            return 0

        lax.fori_loop(0, 3, one, 0)

    pair = 2 * HD
    scale = 1.0 / math.sqrt(HD)
    ticks = {
        0: lambda: next(d_s[0]),
        1: lambda: next(i_s[0]),
        2: lambda: next(i_s[1]),
        3: lambda: (project_grad(0), next(v_s[0]), next(d_s[0])),
        4: lambda: (next(d_s[1]), next(o_s)),
        5: lambda: next(v_s[0]),
        6: lambda: next(i_s[0]),
        7: lambda: (next(d_s[0], None), next(d_s[1])),
    }

    def attend_step(t, _):
        p, half = t // 2, t % 2
        n = pl.multiple_of(p * pair, pair)
        r = pl.ds(pl.multiple_of(half * own_rows, own_rows), own_rows)
        cq, ck, cv = pl.ds(n, pair), pl.ds(cols + n, pair), pl.ds(2 * cols + n, pair)
        same = sc_ref[:, 0:1] == sr_ref[:, r]
        queries = big[half, :, cq]
        keys, values = big[:, :, ck].reshape(length, pair), big[:, :, cv].reshape(length, pair)
        d_rows, o_rows = d_heads[half, :, cq], mine_ref[half, :, cq]
        here = pl.ds(pl.multiple_of(y * cols + n, pair), pair)
        d_q, d_k, d_v = [], [], []
        for h in range(2):
            k = slice(h * HD, h * HD + HD)
            delta = jnp.sum((d_rows[:, k].astype(F32) * o_rows[:, k].astype(F32)).T, axis=0, keepdims=True)
            scores = dg(keys[:, k], queries[:, k], 1, 1) * scale
            prob = jnp.where(same, jnp.exp(scores - stats_ref[p, h : h + 1, r]), 0.0)
            d_prob = dg(values[:, k], d_rows[:, k], 1, 1)
            d_score = (prob * (d_prob - delta) * scale).astype(BF16)
            d_v.append(dg(prob.astype(BF16), d_rows[:, k], 1, 0))
            d_k.append(dg(d_score, queries[:, k], 1, 0))
            d_q.append(dg(d_score, keys[:, k], 0, 0))
        d_q, d_k, d_v = (jnp.concatenate(a, axis=1) for a in (d_q, d_k, d_v))
        big[half, :, cq] = d_q.astype(BF16)
        table[16:17, here] += jnp.sum(d_q, axis=0, keepdims=True)
        table[17:18, here] += jnp.sum(d_v, axis=0, keepdims=True)

        @pl.when(half == 0)
        def _():
            acc_k[...] = d_k
            acc_v[...] = d_v

        @pl.when(half == 1)
        def _():
            big[:, :, ck] = (acc_k[...] + d_k).astype(BF16).reshape(2, own_rows, pair)
            big[:, :, cv] = (acc_v[...] + d_v).astype(BF16).reshape(2, own_rows, pair)

        for k, tick in ticks.items():
            pl.when(t == k)(lambda tick=tick: (tick(), None)[1])
        return 0

    lax.fori_loop(0, 2 * (cols // pair), attend_step, 0)
    project_grad(1)
    next(v_s[1])

    step = 256
    total = table[18:19]
    for half in (at.ny, y):

        def embed_grad(t, acc, half=half):
            r = pl.ds(pl.multiple_of(t * step, step), step)
            made = dg(
                big[half, r, 0 : 3 * cols],
                d_g[1, :, :, :, :, 0 : 3 * cols].reshape(width, 3 * cols), 1, 1,
            )
            i_g[0, 2 * half + t, :, :, :, 0:width] = made.astype(BF16).reshape(i_g.shape[2:5] + (width,))
            return acc + jnp.sum(made, axis=0, keepdims=True)

        total = lax.fori_loop(0, own_rows // step, embed_grad, total)
        if half is y:
            local.copy(i_g.at[0, pl.ds(2 * half, 2), :, :, :, 0:width], x_own)
        else:
            from_x = wire.send(i_g.at[0, pl.ds(2 * half, 2), :, :, :, 0:width], x_got, at.to_y)
    down = lax.broadcasted_iota(jnp.int32, (16, width), 0)
    table[0:16] = jnp.where(down == at.i, total, 0.0)
    left = [tiny, i_s[1], v_s[1], o_s, v_s[0], i_s[0], d_s[1]]
    for _ in range(7):
        for one in left:
            next(one, None)
    from_x.wait_recv()
    local.close()
    wire.close()


def backward(d_ffn, mid, d_attn, act, d_pre, d_mix, qkv, embed, v_all, far, mine, stats, seg_row, seg_col, small):
    own_rows, width = mid.shape
    hidden, cols, rows = act.shape[2], far.shape[1], v_all.shape[3]
    dp3 = (4, 2, 2)
    S = jax.ShapeDtypeStruct
    x_part = S((2, 2, 2, rows, width), BF16)
    outs = [
        S((2, rows, 3 * cols // 2), F32), S((rows, cols), F32), S((rows, hidden), F32), S((rows, hidden), F32),
        x_part, x_part, S(small.shape, F32),
    ]
    wide = S((2,) + dp3 + (rows, hidden), BF16)
    acc = S((2 * own_rows, 2 * HD), F32)
    scratch = [
        S((own_rows, width), BF16), S((2, width, own_rows), BF16), S((2, own_rows, hidden), BF16),
        S((2, own_rows, cols), BF16), wide, wide, S((2,) + dp3 + (rows, cols), BF16),
        S((2,) + dp3 + (rows, 3 * cols // 2), BF16), acc, acc,
        S(small.shape, F32), S((3,) + small.shape, F32), S((6,) + small.shape, F32),
    ]
    copies = 1 + 1 + 6
    for n in [hidden // 2] * 4 + [cols]:
        h = n // 2
        copies += 11
        scratch += [
            S(s, BF16)
            for s in ((2, 4, 2, rows, n), (4, 2, rows, h), (2, 4, rows, h), (4, rows, h), (4, rows, h), (3, rows, n))
        ]
    for n in [3 * cols // 2] * 2:
        copies += 5
        scratch += [S(s, BF16) for s in ((4, 2, rows, n), (4, rows, n), (3, rows, n))]
    vm, hbm = pl.BlockSpec(memory_space=pltpu.VMEM), pl.BlockSpec(memory_space=pl.ANY)
    return pl.pallas_call(
        backward_kernel,
        name="backward",
        out_shape=outs,
        in_specs=[hbm] * 9 + [vm] * 6,
        out_specs=[vm] * 4 + [hbm] * 2 + [vm],
        scratch_shapes=[
            pltpu.SemaphoreType.DMA((copies,)), pltpu.SemaphoreType.DMA((copies,)),
            pltpu.SemaphoreType.DMA((BACKWARD_LOCAL,)),
        ]
        + [pltpu.VMEM(a.shape, a.dtype) for a in scratch],
        compiler_params=pltpu.CompilerParams(
            collective_id=1, has_side_effects=True, vmem_limit_bytes=VMEM_ALL
        ),
    )(d_ffn, mid, d_attn, act, d_pre, d_mix, qkv, embed, v_all, far, mine, stats, seg_row, seg_col, small)


BACKWARD_LOCAL = 12


def attend_kernel(tile, q_ref, k_ref, v_ref, sr_ref, sc_ref, o_ref, l_ref):
    length, width = q_ref.shape

    def step(t, _):
        rows = pl.ds(pl.multiple_of(t * tile, tile), tile)
        same = sc_ref[:, 0:1] == sr_ref[:, rows]
        for h in range(width // HD):
            cols = slice(h * HD, h * HD + HD)
            scores = dg(k_ref[:, cols], q_ref[rows, cols], 1, 1) * (1.0 / math.sqrt(HD))
            scores = jnp.where(same, scores, neg_big)
            row_max = jnp.max(scores, axis=0, keepdims=True)
            prob = jnp.exp(scores - row_max)
            total = jnp.sum(prob, axis=0, keepdims=True)
            mixed = dg(v_ref[:, cols], prob.astype(BF16), 0, 0) / total
            o_ref[rows, cols] = mixed.T.astype(BF16)
            l_ref[0, h : h + 1, rows] = row_max + jnp.log(total)
        return 0

    lax.fori_loop(0, length // tile, step, 0)


def attend_specs(length, heads_pairs):
    def col(k):
        return pl.BlockSpec((length, 2 * HD), lambda i, k=k: (0, k * heads_pairs + i))

    stats = pl.BlockSpec((1, 2, length), lambda i: (i, 0, 0))
    seg_row = pl.BlockSpec((1, length), lambda i: (0, 0))
    seg_col = pl.BlockSpec((length, 128), lambda i: (0, 0))
    return col, stats, seg_row, seg_col


def attend(qkv, segments):
    length = qkv.shape[0]
    pairs = qkv.shape[1] // 3 // (2 * HD)
    col, stats, seg_row, seg_col = attend_specs(length, pairs)
    return pl.pallas_call(
        functools.partial(attend_kernel, min(512, length)),
        name="attend",
        grid=(pairs,),
        in_specs=[col(0), col(1), col(2), seg_row, seg_col],
        out_specs=[col(0), stats],
        out_shape=[
            jax.ShapeDtypeStruct((length, pairs * 2 * HD), BF16),
            jax.ShapeDtypeStruct((pairs, 2, length), F32),
        ],
        cost_estimate=pl.CostEstimate(
            flops=8 * length * length * HD * pairs, bytes_accessed=4 * length * pairs * 256, transcendentals=0
        ),
    )(qkv, qkv, qkv, segments, jnp.broadcast_to(segments.reshape(length, 1), (length, 128)))


def attend_back_kernel(
    tile, q_ref, k_ref, v_ref, d_ref, o_ref, l_ref, sr_ref, sc_ref, dq_ref, dk_ref, dv_ref
):
    length, width = q_ref.shape
    scale = 1.0 / math.sqrt(HD)
    dk_ref[...] = jnp.zeros_like(dk_ref)
    dv_ref[...] = jnp.zeros_like(dv_ref)

    def step(t, _):
        rows = pl.ds(pl.multiple_of(t * tile, tile), tile)
        same = sc_ref[:, 0:1] == sr_ref[:, rows]
        for h in range(width // HD):
            cols = slice(h * HD, h * HD + HD)
            keys, q_rows, d_rows = k_ref[:, cols], q_ref[rows, cols], d_ref[rows, cols]
            delta = jnp.sum(
                (d_rows.astype(F32) * o_ref[rows, cols].astype(F32)).T, axis=0, keepdims=True
            )
            scores = dg(keys, q_rows, 1, 1) * scale
            prob = jnp.where(same, jnp.exp(scores - l_ref[0, h : h + 1, rows]), 0.0)
            d_prob = dg(v_ref[:, cols], d_rows, 1, 1)
            d_score = (prob * (d_prob - delta) * scale).astype(BF16)
            dv_ref[:, cols] += dg(prob.astype(BF16), d_rows, 1, 0)
            dk_ref[:, cols] += dg(d_score, q_rows, 1, 0)
            dq_ref[rows, cols] = dg(d_score, keys, 0, 0)
        return 0

    lax.fori_loop(0, length // tile, step, 0)


def attend_back(qkv, d_mixed, mixed, stats_in, segments):
    length = qkv.shape[0]
    pairs = qkv.shape[1] // 3 // (2 * HD)
    col, stats, seg_row, seg_col = attend_specs(length, pairs)
    return pl.pallas_call(
        functools.partial(attend_back_kernel, min(512, length)),
        name="attend_back",
        grid=(pairs,),
        in_specs=[col(0), col(1), col(2), col(0), col(0), stats, seg_row, seg_col],
        out_specs=[col(0)] * 3,
        out_shape=[jax.ShapeDtypeStruct((length, pairs * 2 * HD), F32)] * 3,
        cost_estimate=pl.CostEstimate(
            flops=20 * length * length * HD * pairs, bytes_accessed=8 * length * pairs * 256, transcendentals=0
        ),
    )(qkv, qkv, qkv, d_mixed, mixed, stats_in, segments, jnp.broadcast_to(segments.reshape(length, 1), (length, 128)))


def time_features(step_ids, model_width):
    half_width = model_width // 2
    frequency = jnp.exp(
        jnp.arange(half_width, dtype=F32) * (-math.log(10000.0) / half_width)
    )
    angles = step_ids.astype(F32)[:, None] * frequency[None, :]
    return jnp.concatenate([jnp.sin(angles), jnp.cos(angles)], axis=1)


def normalize(array_in):
    row_mean = jnp.mean(array_in, axis=-1, keepdims=True)
    centered = array_in - row_mean
    variance = jnp.mean(centered * centered, axis=-1, keepdims=True)
    inv_std = lax.rsqrt(variance + eps)
    return (centered * inv_std, inv_std)


def norm_back(grad_rows, unit_rows, inv_std, gain_row):
    d_unit = grad_rows * gain_row
    return inv_std * (
        d_unit
        - jnp.mean(d_unit, axis=-1, keepdims=True)
        - unit_rows * jnp.mean(d_unit * unit_rows, axis=-1, keepdims=True)
    )


def ein(spec, left, right):
    return jnp.einsum(spec, left, right, preferred_element_type=F32)


def on_device(
    hidden_in,
    segments,
    timesteps,
    time_weight,
    qkv_weight,
    out_weight,
    in_weight,
    down_weight,
    biases,
    gains,
    ffn_bias,
    out_grad,
    *,
    dp,
    mp,
):
    own_rows, width = hidden_in.shape
    length = segments.shape[1]
    rows = time_weight.shape[0]
    cols = qkv_weight.shape[2]
    hidden = in_weight.shape[1]
    dp_index, mp_index = lax.axis_index("dp"), lax.axis_index("mp")
    fast = (dp, mp) == (16, 2)

    bias_count = biases.shape[0] + gains.shape[0]
    v_shard = jnp.concatenate(
        [qkv_weight[0], qkv_weight[1], qkv_weight[2], biases.T, gains.T, jnp.zeros((rows, 128 - bias_count), BF16)],
        axis=1,
    )
    feature = time_features(timesteps, width).astype(BF16)
    few_row = jnp.concatenate([feature.astype(F32), ffn_bias.astype(F32)[None]], axis=1)
    seg_col = jnp.broadcast_to(segments.reshape(length, 1), (length, 128))
    if fast:
        (
            v_all, o_all, i_all, d_all, few, par, time_row, embed_low, qkv, mixed_heads, mixed_far,
            stats, unit_one, inv_one, middle_low, hidden_act, slope,
        ) = forward(
            v_shard, time_weight, few_row, biases[:1], out_weight.T, in_weight, down_weight.T,
            hidden_in, segments, seg_col,
        )
        few = few.reshape(dp, -1)
        inv_one = inv_one[:, :1]
    else:
        v_all = lax.all_gather(v_shard, "dp", axis=0)
        o_all, i_all, d_all = (
            lax.all_gather(lax.all_gather(a, "dp", axis=0), "mp", axis=0)
            for a in (out_weight.T, in_weight, down_weight.T)
        )
        few = lax.all_gather(few_row, "dp", axis=0, tiled=True)
        time_w = lax.all_gather(time_weight, "dp", axis=0, tiled=True)
    v_raw, v_all = v_all, v_all.reshape(width, -1)
    o_all, i_all, d_all = (a.reshape(mp, width, -1) for a in (o_all, i_all, d_all))
    qkv_w = v_all[:, : 3 * cols]
    column = mp_index * cols
    if fast:
        bias_all, gain_all = par[:7], par[7:9]
        middle = unit_one * gain_all[0] + bias_all[4]
    else:
        params = v_all[:, 3 * cols :].astype(F32).T
        bias_all, gain_all = params[:7], params[7:9]
        time_row = jnp.dot(feature, time_w, preferred_element_type=F32) + bias_all[0]
        h_all = lax.all_gather(hidden_in, "mp", axis=0, tiled=True)
        embedded = hidden_in.astype(F32) + time_row
        embed_low = (h_all.astype(F32) + time_row).astype(BF16)
        bias_qkv = jnp.concatenate(
            [
                lax.dynamic_slice_in_dim(bias_all[1], column, cols),
                jnp.zeros((cols,), F32),
                lax.dynamic_slice_in_dim(bias_all[2], column, cols),
            ]
        )
        qkv = (jnp.dot(embed_low, qkv_w, preferred_element_type=F32) + bias_qkv).astype(BF16)
        mixed_heads, stats = attend(qkv, segments)
        mixed = lax.all_to_all(mixed_heads.reshape(mp, own_rows, cols), "mp", 0, 0, tiled=True)
        attn_total = ein("yrk,ynk->rn", mixed, o_all)
        unit_one, inv_one = normalize(embedded + attn_total + bias_all[3])
        middle = unit_one * gain_all[0] + bias_all[4]
        middle_low = middle.astype(BF16)
        ffn_b = few[:, width:].reshape(mp, hidden)
        pre_act = ein("rd,ydf->yrf", middle_low, i_all) + ffn_b[:, None, :]
        below = 0.5 + 0.5 * lax.erf(pre_act * math.sqrt(0.5))
        hidden_act = (pre_act * below).astype(BF16)
        slope = below + pre_act * jnp.exp(-0.5 * pre_act * pre_act) * (1.0 / math.sqrt(2.0 * math.pi))

    ffn_total = ein("yrf,ynf->rn", hidden_act, d_all)
    unit_two, inv_two = normalize(middle + ffn_total + bias_all[5])
    layer_out = (unit_two * gain_all[1] + bias_all[6]).astype(BF16)

    grad_out = out_grad.astype(F32)
    gain_two_part = jnp.sum(grad_out * unit_two, axis=0)
    shift_two_part = jnp.sum(grad_out, axis=0)
    d_pre_two = norm_back(grad_out, unit_two, inv_two, gain_all[1])
    bias_five_part = jnp.sum(d_pre_two, axis=0)
    d_ffn = d_pre_two.astype(BF16)
    d_act = ein("rn,ynf->yrf", d_ffn, d_all)
    d_pre_act = d_act * slope.astype(F32)
    ffn_bias_part = jnp.sum(d_pre_act, axis=1).reshape(-1, width)
    d_pre_low = d_pre_act.astype(BF16)
    d_middle = d_pre_two + ein("yrf,ydf->rd", d_pre_low, i_all)
    gain_one_part = jnp.sum(d_middle * unit_one, axis=0)
    shift_one_part = jnp.sum(d_middle, axis=0)
    d_pre_one = norm_back(d_middle, unit_one, inv_one, gain_all[0])
    bias_three_part = jnp.sum(d_pre_one, axis=0)
    d_attn = d_pre_one.astype(BF16)
    d_mix = ein("rn,ynk->yrk", d_attn, o_all).astype(BF16)
    zero_row = jnp.zeros((width,), F32)
    sums = [bias_three_part, shift_one_part, bias_five_part, shift_two_part, gain_one_part, gain_two_part]

    def pad_rows(a):
        return jnp.pad(a, ((0, -a.shape[0] % 8), (0, 0)))

    if fast:
        small = jnp.concatenate([jnp.zeros((dp + 2, width), F32), jnp.stack(sums), ffn_bias_part], axis=0)
        v_sum, o_sum, i_sum, d_sum, d_near, d_far, small = backward(
            d_ffn, middle_low, d_attn, hidden_act, d_pre_low, d_mix, qkv.reshape(mp, own_rows, -1),
            embed_low.reshape(v_raw.shape[:4] + (width,)), v_raw, mixed_far, mixed_heads, stats, segments, seg_col,
            pad_rows(small),
        )
        d_own = (d_near.astype(F32) + d_far.astype(F32)).reshape(own_rows, width)
        qkv_grad = v_sum.reshape(2, rows, 3, -1).transpose(2, 1, 0, 3).reshape(3, rows, cols)
    else:
        embed_low = embed_low.reshape(length, width)
        mixed_heads = mixed_heads.reshape(length, cols)
        down_grad = ein("rn,yrf->ynf", d_ffn, hidden_act).astype(BF16)
        in_grad = ein("rd,yrf->ydf", middle_low, d_pre_low).astype(BF16)
        out_grad_t = ein("rn,yrk->ynk", d_attn, mixed).astype(BF16)
        d_mixed = lax.all_to_all(d_mix, "mp", 0, 0, tiled=True).reshape(length, cols)
        d_q, d_k, d_v = attend_back(qkv, d_mixed, mixed_heads, stats, segments)
        d_qkv = jnp.concatenate([d_q, d_k, d_v], axis=1).astype(BF16)
        v_grad = dg(embed_low, d_qkv, 0, 0).astype(BF16)
        d_embed = dg(d_qkv, qkv_w, 1, 1)
        time_part = bias_three_part + jnp.sum(d_embed, axis=0)
        d_embed = d_embed.astype(BF16).reshape(mp, own_rows, width)
        seq_rows = jnp.where(jnp.arange(dp)[:, None] == dp_index, time_part[None, :], 0.0)
        spread = [lax.dynamic_update_slice_in_dim(zero_row, jnp.sum(a, axis=0), column, 0) for a in (d_q, d_v)]
        small = pad_rows(jnp.concatenate([seq_rows, jnp.stack(spread + sums), ffn_bias_part], axis=0))
        v_sum = lax.psum_scatter(v_grad, "dp", scatter_dimension=0, tiled=True).astype(F32)

        def both(a):
            a = lax.psum_scatter(a, "mp", scatter_dimension=0)
            return lax.psum_scatter(a, "dp", scatter_dimension=0, tiled=True).astype(F32)

        o_sum, i_sum, d_sum = both(out_grad_t), both(in_grad), both(down_grad)
        d_own = lax.psum_scatter(d_embed, "mp", scatter_dimension=0).astype(F32)
        small = lax.psum(small, ("dp", "mp"))
        qkv_grad = v_sum.reshape(rows, 3, cols).transpose(1, 0, 2)

    input_grad = d_pre_one + d_own
    d_time = small[:dp]
    start = dp_index * rows
    features = few[:, :width]
    features = lax.dynamic_slice_in_dim(features, start, rows, axis=1)
    time_grad = lax.dot_general(
        features, d_time, (((0,), (0,)), ((), ())), precision=lax.Precision.HIGHEST
    )
    tail = small[dp:]
    bias_rows = jnp.concatenate([jnp.sum(d_time, axis=0)[None], tail[:6]], axis=0)
    bias_grad = lax.dynamic_slice_in_dim(bias_rows, start, rows, axis=1)
    gain_grad = lax.dynamic_slice_in_dim(tail[6:8], start, rows, axis=1)
    ffn_rows = ffn_bias.shape[0]
    ffn_all = tail[8:].reshape(-1)
    ffn_bias_grad = lax.dynamic_slice_in_dim(ffn_all, dp_index * ffn_rows, ffn_rows)
    return (
        layer_out,
        input_grad,
        time_grad,
        qkv_grad,
        o_sum.T,
        i_sum,
        d_sum.T,
        bias_grad,
        gain_grad,
        ffn_bias_grad,
    )


def solution(mesh):
    dp, mp = mesh.shape["dp"], mesh.shape["mp"]
    placed = (
        P(("dp", "mp"), None),
        P("dp", None),
        P("dp"),
        P("dp", None),
        P(None, "dp", "mp"),
        P("mp", "dp"),
        P("dp", "mp"),
        P("mp", "dp"),
        P(None, "dp"),
        P(None, "dp"),
        P("dp"),
        P(("dp", "mp"), None),
    )
    return jax.shard_map(
        functools.partial(on_device, dp=dp, mp=mp),
        mesh=mesh,
        in_specs=placed,
        out_specs=(
            P(("dp", "mp"), None),
            P(("dp", "mp"), None),
            P("dp", None),
            P(None, "dp", "mp"),
            P("mp", "dp"),
            P("dp", "mp"),
            P("mp", "dp"),
            P(None, "dp"),
            P(None, "dp"),
            P("dp"),
        ),
        check_vma=False,
    )
```

```python
import functools
import math

import jax
import jax.numpy as jnp
from jax import lax
from jax.experimental import pallas as pl
from jax.experimental.pallas import tpu as pltpu
from jax.sharding import PartitionSpec as P

HD = 64
eps = 1e-05
neg_big = -1000000000.0
MESH = pl.DeviceIdType.MESH
F32, BF16 = jnp.float32, jnp.bfloat16
VMEM_LIMIT, VMEM_ALL = 64000000, 67043328


def dg(left, right, left_dim, right_dim):
    return lax.dot_general(
        left, right, (((left_dim,), (right_dim,)), ((), ())), preferred_element_type=F32
    )


class Place:
    def __init__(self):
        i, y = lax.axis_index("dp"), lax.axis_index("mp")
        z, x, c = i // 4, (i // 2) % 2, i % 2
        self.i, self.z, self.x, self.c, self.y = i, z, x, c, y
        self.nx, self.nc, self.ny, self.zero = 1 - x, 1 - c, 1 - y, 0 * i
        low, high = z % 2, z // 2
        flipped = [(1 - 2 * bit) * v + bit for v, bit in ((low, 1), (high, 1))]
        self.zs = [high * 2 + flipped[0], flipped[1] * 2 + low, flipped[1] * 2 + flipped[0]]
        self.to_z = [((p * 2 + x) * 2 + c, y) for p in self.zs]
        self.to_x = ((z * 2 + self.nx) * 2 + c, y)
        self.to_y = (i, self.ny)
        self.to_c = ((z * 2 + x) * 2 + self.nc, y)
        self.count = [self.zero + j for j in range(3)]
        self.dp = [
            (pz * 2 + px) * 2 + pc
            for pz in [z] + self.zs
            for px in (x, self.nx)
            for pc in (c, self.nc)
        ][1:]

    def enter(self, all_dp):
        barrier = pltpu.get_barrier_semaphore()
        near = [self.to_y]
        near += [(p, self.y) for p in self.dp] if all_dp else self.to_z + [self.to_x, self.to_c]
        for one in near:
            pl.semaphore_signal(barrier, inc=1, device_id=one, device_id_type=MESH)
        pl.semaphore_wait(barrier, len(near))


class Wire:
    def __init__(self, at, send_sems, recv_sems):
        self.sems = [(send_sems.at[at.zero + k], recv_sems.at[at.zero + k]) for k in range(send_sems.shape[0])]
        self.used, self.open = 0, []

    def send(self, src, dst, to):
        k = self.used
        self.used += 1
        copy = pltpu.make_async_remote_copy(
            src_ref=src,
            dst_ref=dst,
            send_sem=self.sems[k][0],
            recv_sem=self.sems[k][1],
            device_id=to,
            device_id_type=MESH,
        )
        copy.start()
        self.open.append(copy)
        return copy

    def both(self, copy):
        copy.wait_send()
        self.open = [one for one in self.open if one is not copy]
        copy.wait_recv()

    def close(self):
        assert self.used == len(self.sems), self.used
        for copy in self.open:
            copy.wait_send()


class Local:
    def __init__(self, sems):
        self.sems, self.used, self.open = sems, 0, []

    def copy(self, src, dst):
        one = pltpu.make_async_copy(src, dst, self.sems.at[self.used])
        self.used += 1
        one.start()
        self.open.append(one)
        return one

    def close(self):
        assert self.used == self.sems.shape[0], self.used
        for one in self.open:
            one.wait()


def parts_of(width, parts, first=0.5):
    step = width // parts
    return [(p * step, p * step + int(step * first), (p + 1) * step) for p in range(parts)]


def stagger(streams, ahead=0):
    for depth in range(ahead, len(streams) + 6):
        for k, s in enumerate(streams):
            if k <= depth:
                next(s, None)


def gather_dp(wire, at, shard, whole, lo, hi):
    n = pl.ds(lo, hi - lo)
    own = whole.at[at.z, at.x, at.c, :, n]
    from_z = [wire.send(shard.at[:, n], own, to) for to in at.to_z]
    late = [wire.send(shard.at[:, n], own, at.to_c)]
    yield
    for k in from_z:
        k.wait_recv()
    ref = whole.at[:, at.x, at.c, :, n]
    from_x = wire.send(ref, ref, at.to_x)
    for p in at.zs:
        ref = whole.at[p, at.x, at.c, :, n]
        late.append(wire.send(ref, ref, at.to_c))
    yield
    from_x.wait_recv()
    ref = whole.at[:, at.nx, at.c, :, n]
    late.append(wire.send(ref, ref, at.to_c))
    yield
    for k in late:
        k.wait_recv()


def gather_all(wire, at, shard, whole, lo, mid, hi):
    a, b, ab = pl.ds(lo, mid - lo), pl.ds(mid, hi - mid), pl.ds(lo, hi - lo)
    y, z, x, c = at.y, at.z, at.x, at.c
    from_z_a = [wire.send(shard.at[:, a], whole.at[y, z, x, c, :, a], to) for to in at.to_z]
    from_y_b = wire.send(shard.at[:, b], whole.at[y, z, x, c, :, b], at.to_y)
    late = [wire.send(shard.at[:, ab], whole.at[y, z, x, c, :, ab], at.to_c)]

    def to_core(*refs):
        for ref in refs:
            late.append(wire.send(ref, ref, at.to_c))

    yield
    from_y_b.wait_recv()
    ref = whole.at[:, z, x, c, :, b]
    from_z_b = [wire.send(ref, ref, to) for to in at.to_z]
    to_core(whole.at[at.ny, z, x, c, :, b])
    yield
    for k in from_z_a:
        k.wait_recv()
    ref = whole.at[y, :, x, c, :, a]
    from_x_a = wire.send(ref, ref, at.to_x)
    to_core(*(whole.at[y, p, x, c, :, a] for p in at.zs))
    yield
    from_x_a.wait_recv()
    ref = whole.at[y, :, :, c, :, a]
    from_y_a = wire.send(ref, ref, at.to_y)
    to_core(whole.at[y, :, at.nx, c, :, a])
    yield
    for k in from_z_b:
        k.wait_recv()
    ref = whole.at[:, :, x, c, :, b]
    from_x_b = wire.send(ref, ref, at.to_x)
    to_core(*(whole.at[:, p, x, c, :, b] for p in at.zs))
    yield
    from_y_a.wait_recv()
    from_x_b.wait_recv()
    to_core(whole.at[at.ny, :, :, c, :, a], whole.at[:, :, at.nx, c, :, b])
    yield
    for k in late:
        k.wait_recv()


def one_hot_rows(count, width, start):
    down = lax.broadcasted_iota(jnp.int32, (count, width), 0)
    across = lax.broadcasted_iota(jnp.int32, (count, width), 1)
    return jnp.where(down == across + start, 1.0, 0.0).astype(BF16)


def forward_kernel(
    v_ref, t_ref, f_ref, b_ref, o_ref, i_ref, d_ref, h_ref, sr_ref, sc_ref,
    v_out, o_out, i_out, d_all, few_out, par_out, time_out, embed_out, qkv_out, mine_out, far_out,
    stats_out, unit_out, inv_out, mid_out, act_out, slope_out,
    v_all, o_all, i_all, few, part, got, h_far, par, ffn_b, embed, qkv, mine, far, stats, unit, inv,
    mid, act, slope, send_sems, recv_sems, local_sems, tile_sems,
):
    at = Place()
    y, z, x, c = at.y, at.z, at.x, at.c
    at.enter(True)
    wire, local = Wire(at, send_sems, recv_sems), Local(local_sems)
    width = h_ref.shape[1]
    own_rows = h_ref.shape[0]
    rows = v_ref.shape[0]
    cols = o_ref.shape[1]
    hidden = i_ref.shape[1]
    length = 2 * own_rows

    from_few = [wire.send(f_ref, few.at[at.i], (p, y)) for p in at.dp]
    from_h = wire.send(h_ref, h_far, at.to_y)
    v_mid = 7 * 128
    v0 = gather_dp(wire, at, v_ref, v_all, 0, v_mid)
    v1 = gather_dp(wire, at, v_ref, v_all, v_mid, v_ref.shape[1])
    out_w = gather_all(wire, at, o_ref, o_all, *parts_of(cols, 1)[0])
    in_w = [gather_all(wire, at, i_ref, i_all, *cut) for cut in parts_of(hidden, 2, 0.625)]
    down_w = [gather_all(wire, at, d_ref, d_all, *cut) for cut in parts_of(hidden, 2, 0.625)]
    kept = [
        local.copy(v_ref, v_all.at[z, x, c]),
        local.copy(o_ref, o_all.at[y, z, x, c]),
        local.copy(i_ref, i_all.at[y, z, x, c]),
        local.copy(d_ref, d_all.at[y, z, x, c]),
    ]
    next(v0)
    next(v1)
    next(out_w)
    next(in_w[0])
    few[at.i] = f_ref[...]
    for k in from_few:
        k.wait_recv()
    seqs = few.shape[0]
    table = jnp.concatenate([few[s] for s in range(seqs)], axis=0)
    pick = one_hot_rows(width, rows, at.i * rows)
    feats = dg(table[:, :width].astype(BF16), pick, 1, 0).astype(BF16)
    partial = dg(feats, t_ref[...], 1, 0) + dg(b_ref[...], pick, 1, 1)
    for s in range(seqs):
        part[s] = partial[s : s + 1]
    ffn_b[...] = jnp.concatenate([few[s][:, width:] for s in range(seqs)], axis=1)
    local.copy(few, few_out)
    from_part = [wire.send(part.at[p], got.at[j], (p, y)) for j, p in enumerate(at.dp)]
    for k in kept:
        k.wait()
        local.open.remove(k)
    next(v0)
    next(v1)
    next(out_w)
    next(in_w[1])
    next(down_w[0])
    next(v0)
    next(out_w)
    for k in from_part:
        k.wait_recv()
    total = part[at.i]
    for j in range(seqs - 1):
        total = total + got[j]
    time_out[...] = total
    next(in_w[0])
    next(v1)
    next(in_w[0])
    next(v0, None)

    from_h.wait_recv()
    step = 128

    def embed_rows(t, _):
        r = pl.ds(pl.multiple_of(t * step, step), step)
        embed[y, r] = (h_ref[r].astype(F32) + total).astype(BF16)
        embed[at.ny, r] = (h_far[r].astype(F32) + total).astype(BF16)
        return 0

    lax.fori_loop(0, own_rows // step, embed_rows, 0)
    local.copy(embed, embed_out)
    next(v1, None)
    next(in_w[1])
    next(out_w)
    next(down_w[1])
    local.copy(v_all, v_out)
    par[...] = v_all[:, :, :, :, 3 * cols :].reshape(width, 128).astype(F32).T
    local.copy(par, par_out)
    heads = pl.ds(pl.multiple_of(y * cols, cols), cols)
    bias_q, bias_v = par[1:2, heads], par[2:3, heads]

    step_q = 256

    def project(t, _):
        half, r = t // (own_rows // step_q), pl.ds(pl.multiple_of((t % (own_rows // step_q)) * step_q, step_q), step_q)
        whole_r = pl.ds(pl.multiple_of(t * step_q, step_q), step_q)
        left = embed[half, r]
        for j, bias in enumerate((bias_q, None, bias_v)):
            n = slice(j * cols, (j + 1) * cols)
            made = dg(left, v_all[:, :, :, :, n].reshape(width, cols), 1, 0)
            qkv[whole_r, n] = (made if bias is None else made + bias).astype(BF16)
        return 0

    lax.fori_loop(0, length // step_q, project, 0)
    local.copy(qkv, qkv_out)
    next(in_w[0])
    next(out_w)

    pair, tile = 2 * HD, own_rows
    from_far = []

    def give(p):
        n = pl.ds(p * pair, pair)
        from_far.append(wire.send(mine.at[at.ny, :, n], far.at[:, n], at.to_y))

    ticks = {
        1: lambda: (give(0), next(down_w[0]), next(down_w[1]), next(in_w[1]),),
        3: lambda: (give(1), next(in_w[1]), next(down_w[0]), next(in_w[0]),),
        5: lambda: (give(2),),
        6: lambda: (next(in_w[1]), next(out_w),),
        7: lambda: (give(3), next(in_w[0]), next(down_w[0]), next(out_w, None), next(in_w[1]), next(down_w[1]), next(in_w[0], None), next(down_w[0]),),
    }

    def attend_step(t, _):
        p, half = t // 2, t % 2
        r = pl.ds(pl.multiple_of(half * tile, tile), tile)
        n = pl.multiple_of(p * pair, pair)
        queries = qkv[r, pl.ds(n, pair)]
        keys = qkv[:, pl.ds(cols + n, pair)]
        values = qkv[:, pl.ds(2 * cols + n, pair)]
        same = sc_ref[:, 0:1] == sr_ref[:, r]
        made = []
        for h in range(2):
            k = slice(h * HD, h * HD + HD)
            scores = dg(keys[:, k], queries[:, k], 1, 1) * (1.0 / math.sqrt(HD))
            scores = jnp.where(same, scores, neg_big)
            row_max = jnp.max(scores, axis=0, keepdims=True)
            prob = jnp.exp(scores - row_max)
            row_total = jnp.sum(prob, axis=0, keepdims=True)
            made.append((dg(values[:, k], prob.astype(BF16), 0, 0) / row_total).T)
            stats[p, h : h + 1, r] = row_max + jnp.log(row_total)
        mine[half, :, pl.ds(n, pair)] = jnp.concatenate(made, axis=1).astype(BF16)
        for k, tick in ticks.items():
            pl.when(t == k)(lambda tick=tick: (tick(), None)[1])
        return 0

    lax.fori_loop(0, 2 * (cols // pair), attend_step, 0)
    local.copy(mine, mine_out)
    local.copy(stats, stats_out)
    local.copy(o_all, o_out)

    for k in from_far:
        k.wait_recv()
    local.copy(far, far_out)

    def project_out(t, _):
        r = pl.ds(pl.multiple_of(t * step_q, step_q), step_q)
        total_r = dg(mine[y, r], o_all[y].reshape(width, cols), 1, 1)
        total_r += dg(far[r], o_all[at.ny].reshape(width, cols), 1, 1)
        total_r += h_ref[r].astype(F32) + total + par[3:4]
        made, inv_std = normalize(total_r)
        unit[r] = made
        inv[r] = jnp.broadcast_to(inv_std, (step_q, 128))
        mid[r] = (made * par[7:8] + par[4:5]).astype(BF16)
        return 0

    lax.fori_loop(0, own_rows // step_q, project_out, 0)
    local.copy(unit, unit_out)
    local.copy(inv, inv_out)
    local.copy(mid, mid_out)


    chunk = 512
    per = hidden // 2 // chunk
    later = {
        0: lambda: (next(down_w[1]),),
        2: lambda: (next(in_w[1], None), next(down_w[1]),),
        4: lambda: (next(down_w[0]),),
        6: lambda: (next(down_w[1]),),
    }

    def feed_step(t, _):
        side = (t // per) % 2
        n = pl.multiple_of((t // (2 * per)) * (hidden // 2) + (t % per) * chunk, chunk)
        made = dg(mid[...], i_all[side, :, :, :, :, pl.ds(n, chunk)].reshape(width, chunk), 1, 0)
        made = made + ffn_b[:, pl.ds(pl.multiple_of(side * hidden, hidden) + n, chunk)]
        below = 0.5 + 0.5 * lax.erf(made * math.sqrt(0.5))
        act[side, :, pl.ds(n, chunk)] = (made * below).astype(BF16)
        bell = jnp.exp(-0.5 * made * made) * (1.0 / math.sqrt(2.0 * math.pi))
        slope[side, :, pl.ds(n, chunk)] = (below + made * bell).astype(BF16)
        pltpu.make_async_copy(
            act.at[side, :, pl.ds(n, chunk)], act_out.at[side, :, pl.ds(n, chunk)], tile_sems.at[0, t]
        ).start()
        pltpu.make_async_copy(
            slope.at[side, :, pl.ds(n, chunk)], slope_out.at[side, :, pl.ds(n, chunk)], tile_sems.at[1, t]
        ).start()
        for k, tick in later.items():
            pl.when(t == k)(lambda tick=tick: (tick(), None)[1])
        return 0

    tiles = 4 * per
    lax.fori_loop(0, tiles, feed_step, 0)
    local.copy(i_all, i_out)
    next(down_w[0], None)
    next(down_w[1], None)
    for t in range(tiles):
        n = pl.ds(0, chunk)
        pltpu.make_async_copy(act.at[0, :, n], act_out.at[0, :, n], tile_sems.at[0, t]).wait()
        pltpu.make_async_copy(slope.at[0, :, n], slope_out.at[0, :, n], tile_sems.at[1, t]).wait()
    local.close()
    wire.close()


def forward(v, t, few_row, bias_zero, o, i, d, h, seg_row, seg_col):
    rows, cols, hidden = v.shape[0], o.shape[1], i.shape[1]
    own_rows, width = h.shape
    length = 2 * own_rows
    pairs = cols // (2 * HD)
    S = jax.ShapeDtypeStruct
    dp3 = (4, 2, 2)
    v_all, o_all, i_all = S(dp3 + v.shape, BF16), S((2,) + dp3 + o.shape, BF16), S((2,) + dp3 + i.shape, BF16)
    few = S((16,) + few_row.shape, F32)
    par, time_row = S((128, width), F32), S((1, width), F32)
    embed, qkv = S((2, own_rows, width), BF16), S((length, 3 * cols), BF16)
    mine, far = S((2, own_rows, cols), BF16), S((own_rows, cols), BF16)
    stats = S((pairs, 2, length), F32)
    unit, inv, mid = S((own_rows, width), F32), S((own_rows, 128), F32), S((own_rows, width), BF16)
    act = S((2, own_rows, hidden), BF16)
    outs = [v_all, o_all, i_all, i_all, few, par, time_row, embed, qkv, mine, far, stats, unit, inv, mid, act, act]
    vm, hbm = pl.BlockSpec(memory_space=pltpu.VMEM), pl.BlockSpec(memory_space=pl.ANY)
    out_specs = [hbm] * len(outs)
    out_specs[6] = vm
    part, got = S((16, 1, width), F32), S((15, 1, width), F32)
    h_far, ffn_b = S(h.shape, BF16), S((1, 2 * hidden), F32)
    scratch = [v_all, o_all, i_all, few, part, got, h_far, par, ffn_b, embed, qkv, mine, far, stats, unit, inv, mid, act, act]
    copies = 15 + 15 + 1 + 2 * 9 + 5 * 21 + pairs
    return pl.pallas_call(
        forward_kernel,
        name="forward",
        out_shape=outs,
        in_specs=[vm] * 10,
        out_specs=out_specs,
        scratch_shapes=[pltpu.VMEM(a.shape, a.dtype) for a in scratch]
        + [
            pltpu.SemaphoreType.DMA((copies,)),
            pltpu.SemaphoreType.DMA((copies,)),
            pltpu.SemaphoreType.DMA((FORWARD_LOCAL,)),
            pltpu.SemaphoreType.DMA((2, 2 * hidden // 512)),
        ],
        compiler_params=pltpu.CompilerParams(
            collective_id=0, has_side_effects=True, vmem_limit_bytes=VMEM_LIMIT
        ),
    )(v, t, few_row, bias_zero, o, i, d, h, seg_row, seg_col)


FORWARD_LOCAL = 17


def add_blocks(dst, left, right, lead):
    count = math.prod(lead)

    def one(t, _):
        at = []
        for n in reversed(lead):
            at.append(t % n)
            t = t // n
        at = tuple(reversed(at))
        dst[at] = (left[at].astype(F32) + right[at].astype(F32)).astype(dst.dtype)
        return 0

    lax.fori_loop(0, count, one, 0)


def reduce_dp(wire, at, grad, rc, rx, rz, out):
    z, x, c, y = at.z, at.x, at.c, at.y
    from_c = wire.send(grad.at[:, :, at.nc], rc, at.to_c)
    yield
    wire.both(from_c)
    add_blocks(rc, grad.at[:, :, c], rc, (4, 2))
    from_x = wire.send(rc.at[:, at.nx], rx, at.to_x)
    yield
    from_x.wait_recv()
    add_blocks(rx, rc.at[:, x], rx, (4,))
    from_z = [wire.send(rx.at[p], rz.at[at.count[j]], to) for j, (p, to) in enumerate(zip(at.zs, at.to_z))]
    yield
    for k in from_z:
        k.wait_recv()
    out[...] = ((rx[z].astype(F32) + rz[0].astype(F32)) + rz[1].astype(F32)) + rz[2].astype(F32)


def reduce_all(wire, at, grad, bufs, out, lo, mid, hi, early):
    rc, ya, xb, xa, za, zb, yb, zs = bufs
    z, x, c, y = at.z, at.x, at.c, at.y
    a, b, ab = pl.ds(lo, mid - lo), pl.ds(mid, hi - mid), pl.ds(lo, hi - lo)
    half_a, half_b = pl.ds(0, mid - lo), pl.ds(mid - lo, hi - mid)

    def over_z(pick, got):
        return [wire.send(pick(p), got.at[at.count[j]], to) for j, (p, to) in enumerate(zip(at.zs, at.to_z))]

    def add_z(own, got):
        return ((own.astype(F32) + got[0].astype(F32)) + got[1].astype(F32)) + got[2].astype(F32)

    from_c = wire.send(grad.at[:, :, :, at.nc, :, ab], rc, at.to_c)
    yield
    wire.both(from_c)
    add_blocks(rc, grad.at[:, :, :, c, :, ab], rc, (2, 4, 2))
    from_y_a = wire.send(rc.at[at.ny, :, :, :, half_a], ya, at.to_y)
    from_x_b = wire.send(rc.at[:, :, at.nx, :, half_b], xb, at.to_x)
    yield
    from_y_a.wait_recv()
    add_blocks(ya, rc.at[y, :, :, :, half_a], ya, (4, 2))
    from_x_a = wire.send(ya.at[:, at.nx], xa, at.to_x)
    yield
    from_x_b.wait_recv()
    add_blocks(xb, rc.at[:, :, x, :, half_b], xb, (2, 4))
    if early:
        from_z_b = over_z(lambda p: xb.at[:, p], zb)
    else:
        from_y_b = wire.send(xb.at[at.ny], yb, at.to_y)
    yield
    from_x_a.wait_recv()
    add_blocks(xa, ya.at[:, x], xa, (4,))
    from_z_a = over_z(lambda p: xa.at[p], za)
    yield
    if early:
        for k in from_z_b:
            k.wait_recv()
        zs[...] = add_z(xb[:, z], zb).astype(BF16)
        from_y_b = wire.send(zs.at[at.ny], yb, at.to_y)
    else:
        from_y_b.wait_recv()
        add_blocks(yb, xb.at[y], yb, (4,))
        from_z_b = over_z(lambda p: yb.at[p], zb)
    yield
    for k in from_z_a:
        k.wait_recv()
    out[:, a] = add_z(xa[z], za)
    if early:
        from_y_b.wait_recv()
        out[:, b] = zs[y].astype(F32) + yb[...].astype(F32)
    else:
        for k in from_z_b:
            k.wait_recv()
        out[:, b] = add_z(yb[z], zb)


def reduce_bufs(rows, lo, mid, hi, early):
    ha, hb = mid - lo, hi - mid
    last = [(3, 2, rows, hb), (rows, hb), (2, rows, hb)] if early else [(3, rows, hb), (4, rows, hb), (8, 128)]
    return [(2, 4, 2, rows, hi - lo), (4, 2, rows, ha), (2, 4, rows, hb), (4, rows, ha), (3, rows, ha)] + last


def reduce_small(wire, at, mine, sums, got, out):
    k = wire.send(mine, got.at[0], at.to_c)
    yield
    k.wait_recv()
    sums[0] = mine[...] + got[0]
    k = wire.send(sums.at[0], got.at[1], at.to_x)
    yield
    k.wait_recv()
    sums[1] = sums[0] + got[1]
    k = wire.send(sums.at[1], got.at[2], at.to_y)
    yield
    k.wait_recv()
    sums[2] = sums[1] + got[2]
    last = [wire.send(sums.at[2], got.at[3 + j], to) for j, to in enumerate(at.to_z)]
    yield
    for k in last:
        k.wait_recv()
    out[...] = ((sums[2] + got[3]) + got[4]) + got[5]


D_PARTS = ((0.75, True), (0.5, True), (0.75, True), (0.5, True))
I_PARTS = ((0.75, True), (0.5, True), (0.5, False), (0.75, False))
O_PARTS = ((0.5, False),)

AFTER = {
    "pd0": ("d0",),
    "pd2": ("d1",),
    "pd3": ("d3", "d0",),
    "pi0": ("d1",),
    "pi1": ("i0",),
    "pi2": ("d2", "d3", "i1",),
    "pi3": ("d0",),
    "po": ("d1", "d2", "d1", "i3",),
    "emb": ("d0", "i2", "d0", "i1",),
    "a0": ("d3", "i0", "d3",),
    "a1": ("d2", "d1", "i2", "o", "d2",),
    "a2": ("i1",),
    "a3": ("d3", "i1",),
    "vp0": ("i0", "i0", "o", "d2",),
    "a4": ("i2", "i1", "i3",),
    "a5": ("o", "i2",),
    "a6": ("i0",),
    "a7": ("i2",),
    "vp1": ("v0", "v1", "i3", "o", "i3", "i2",),
    "e0": ("o", "v0", "o", "i3",),
    "e1": ("t", "i0", "v1", "i3", "v0", "t", "v1", "i3", "t", "i2", "t", "v1", "i1", "o", "d3", "d1", "d2", "d2", "d1", "d3", "v0", "i1", "d0", "d0", "i0", "t",),
}


def cuts_of(width, parts):
    step = width // len(parts)
    return [(k * step, k * step + int(step * first), (k + 1) * step, early) for k, (first, early) in enumerate(parts)]


def turn_rows(src, dst):
    def one(t, _):
        r = pl.ds(pl.multiple_of(t * 128, 128), 128)
        dst[r, :] = src[:, r].astype(F32).T.astype(BF16)
        return 0

    lax.fori_loop(0, src.shape[1] // 128, one, 0)


def backward_kernel(
    ffn_ref, mid_ref, attn_ref, act_ref, pre_ref, mix_ref, qkv_ref, embed_ref, v_ref,
    far_ref, mine_ref, stats_ref, sr_ref, sc_ref, small_ref,
    v_out, o_out, i_out, d_out, x_own, x_got, s_out, *rest,
):
    at = Place()
    y = at.y
    at.enter(False)
    rest = iter(rest)
    wire, local = Wire(at, next(rest), next(rest)), Local(next(rest))
    raw, tr, big, d_heads, d_g, i_g, o_g, v_g, acc_k, acc_v, table, sums, got = (next(rest) for _ in range(13))
    own_rows, width = raw.shape
    hidden, cols, length = big.shape[2], d_heads.shape[2], 2 * own_rows

    streams = {}
    for name, grad, out, parts in (("d", d_g, d_out, D_PARTS), ("i", i_g, i_out, I_PARTS), ("o", o_g, o_out, O_PARTS)):
        for k, cut in enumerate(cuts_of(out.shape[1], parts)):
            bufs = [next(rest) for _ in range(8)]
            streams[name + str(k)] = reduce_all(wire, at, grad, bufs, out, *cut)
    streams["o"] = streams["o0"]
    for k in range(2):
        bufs = [next(rest) for _ in range(3)]
        streams["v" + str(k)] = reduce_dp(wire, at, v_g.at[k], *bufs, v_out.at[k])
    streams["t"] = reduce_small(wire, at, table, sums, got, s_out)

    def run(step):
        for name in AFTER.get(step, ()):
            next(streams[name], None)

    def done(one):
        one.wait()
        local.open = [other for other in local.open if other is not one]

    from_mix = wire.send(mix_ref.at[at.ny], d_heads.at[y], at.to_y)
    chunk = 512
    pieces = [pl.ds(lo, chunk) for lo in range(0, hidden, chunk)]
    raw_in = local.copy(ffn_ref, raw)
    act_in = [local.copy(act_ref.at[:, :, n], big.at[:, :, n]) for n in pieces]
    pre_in = []
    mix_in = local.copy(mix_ref.at[y], d_heads.at[y])
    table[...] = small_ref[...]
    done(raw_in)
    turn_rows(raw, tr.at[0])
    raw_in = local.copy(mid_ref, raw)

    def products(left, grad, lo, hi):
        per = (hi - lo) // chunk

        def one(t, _):
            side = t // per
            n = pl.ds(pl.multiple_of(lo + (t % per) * chunk, chunk), chunk)
            made = dg(left[...], big[side, :, n], 1, 0).astype(BF16)
            grad[side, :, :, :, :, n] = made.reshape(grad.shape[1:5] + (chunk,))
            return 0

        lax.fori_loop(0, 2 * per, one, 0)

    for k, (lo, _, hi, _) in enumerate(cuts_of(hidden, D_PARTS)):
        mine = range(lo // chunk, hi // chunk)
        for n in mine:
            done(act_in[n])
        products(tr.at[0], d_g, lo, hi)
        pre_in += [local.copy(pre_ref.at[:, :, pieces[n]], big.at[:, :, pieces[n]]) for n in mine]
        run("pd" + str(k))
    done(raw_in)
    turn_rows(raw, tr.at[1])
    raw_in = local.copy(attn_ref, raw)
    for k, (lo, _, hi, _) in enumerate(cuts_of(hidden, I_PARTS)):
        for n in range(lo // chunk, hi // chunk):
            done(pre_in[n])
        products(tr.at[1], i_g, lo, hi)
        run("pi" + str(k))
    qkv_in = local.copy(qkv_ref, big.at[:, :, 0 : 3 * cols])
    done(raw_in)
    turn_rows(raw, tr.at[0])
    for side, right in ((y, mine_ref.at[y]), (at.ny, far_ref)):
        made = dg(tr[0], right[...], 1, 0).astype(BF16)
        o_g[side] = made.reshape(o_g.shape[1:])
    run("po")

    embed_in = local.copy(embed_ref, d_g.at[0, :, :, :, :, 0:width])
    v_in = local.copy(v_ref, d_g.at[1, :, :, :, :, 0 : v_ref.shape[4]])
    done(embed_in)

    def turn_embed(t, _):
        n = pl.ds(pl.multiple_of(t * 128, 128), 128)
        block = d_g[0, :, :, :, :, n].reshape(length, 128)
        d_g[0, t // 2, t % 2, :, :, width : 2 * width] = (
            block.astype(F32).T.astype(BF16).reshape(d_g.shape[3:5] + (length,))
        )
        return 0

    lax.fori_loop(0, width // 128, turn_embed, 0)
    done(v_in)
    done(qkv_in)
    done(mix_in)
    from_mix.wait_recv()
    run("emb")

    part_cols = cols // 2

    def project_grad(k):
        def one(j, _):
            n = pl.ds(pl.multiple_of(j * cols + k * part_cols, part_cols), part_cols)
            made = dg(
                d_g[0, :, :, :, :, width : 2 * width].reshape(width, length),
                big[:, :, n].reshape(length, part_cols), 1, 0,
            ).astype(BF16)
            v_g[k, :, :, :, :, pl.ds(pl.multiple_of(j * part_cols, part_cols), part_cols)] = made.reshape(
                v_g.shape[1:5] + (part_cols,)
            )
            return 0

        lax.fori_loop(0, 3, one, 0)

    pair = 2 * HD
    scale = 1.0 / math.sqrt(HD)
    ticks = {t: lambda t=t: run("a" + str(t)) for t in range(8) if "a" + str(t) in AFTER}
    ticks[3] = lambda: (run("a3"), project_grad(0), run("vp0"))

    def attend_step(t, _):
        p, half = t // 2, t % 2
        n = pl.multiple_of(p * pair, pair)
        r = pl.ds(pl.multiple_of(half * own_rows, own_rows), own_rows)
        cq, ck, cv = pl.ds(n, pair), pl.ds(cols + n, pair), pl.ds(2 * cols + n, pair)
        same = sc_ref[:, 0:1] == sr_ref[:, r]
        queries = big[half, :, cq]
        keys, values = big[:, :, ck].reshape(length, pair), big[:, :, cv].reshape(length, pair)
        d_rows, o_rows = d_heads[half, :, cq], mine_ref[half, :, cq]
        here = pl.ds(pl.multiple_of(y * cols + n, pair), pair)
        d_q, d_k, d_v = [], [], []
        for h in range(2):
            k = slice(h * HD, h * HD + HD)
            delta = jnp.sum((d_rows[:, k].astype(F32) * o_rows[:, k].astype(F32)).T, axis=0, keepdims=True)
            scores = dg(keys[:, k], queries[:, k], 1, 1) * scale
            prob = jnp.where(same, jnp.exp(scores - stats_ref[p, h : h + 1, r]), 0.0)
            d_prob = dg(values[:, k], d_rows[:, k], 1, 1)
            d_score = (prob * (d_prob - delta) * scale).astype(BF16)
            d_v.append(dg(prob.astype(BF16), d_rows[:, k], 1, 0))
            d_k.append(dg(d_score, queries[:, k], 1, 0))
            d_q.append(dg(d_score, keys[:, k], 0, 0))
        d_q, d_k, d_v = (jnp.concatenate(a, axis=1) for a in (d_q, d_k, d_v))
        big[half, :, cq] = d_q.astype(BF16)
        table[16:17, here] += jnp.sum(d_q, axis=0, keepdims=True)
        table[17:18, here] += jnp.sum(d_v, axis=0, keepdims=True)

        @pl.when(half == 0)
        def _():
            acc_k[...] = d_k
            acc_v[...] = d_v

        @pl.when(half == 1)
        def _():
            big[:, :, ck] = (acc_k[...] + d_k).astype(BF16).reshape(2, own_rows, pair)
            big[:, :, cv] = (acc_v[...] + d_v).astype(BF16).reshape(2, own_rows, pair)

        for k, tick in ticks.items():
            pl.when(t == k)(lambda tick=tick: (tick(), None)[1])
        return 0

    lax.fori_loop(0, 2 * (cols // pair), attend_step, 0)
    project_grad(1)
    run("vp1")

    step = 256
    total = table[18:19]
    for half in (at.ny, y):

        def embed_grad(t, acc, half=half):
            r = pl.ds(pl.multiple_of(t * step, step), step)
            made = dg(
                big[half, r, 0 : 3 * cols],
                d_g[1, :, :, :, :, 0 : 3 * cols].reshape(width, 3 * cols), 1, 1,
            )
            i_g[0, 2 * half + t, :, :, :, 0:width] = made.astype(BF16).reshape(i_g.shape[2:5] + (width,))
            return acc + jnp.sum(made, axis=0, keepdims=True)

        total = lax.fori_loop(0, own_rows // step, embed_grad, total)
        if half is y:
            local.copy(i_g.at[0, pl.ds(2 * half, 2), :, :, :, 0:width], x_own)
        else:
            from_x = wire.send(i_g.at[0, pl.ds(2 * half, 2), :, :, :, 0:width], x_got, at.to_y)
            run("e0")
    down = lax.broadcasted_iota(jnp.int32, (16, width), 0)
    table[0:16] = jnp.where(down == at.i, total, 0.0)
    run("e1")
    from_x.wait_recv()
    local.close()
    wire.close()


def backward(d_ffn, mid, d_attn, act, d_pre, d_mix, qkv, embed, v_all, far, mine, stats, seg_row, seg_col, small):
    own_rows, width = mid.shape
    hidden, cols, rows = act.shape[2], far.shape[1], v_all.shape[3]
    dp3 = (4, 2, 2)
    S = jax.ShapeDtypeStruct
    x_part = S((2, 2, 2, rows, width), BF16)
    outs = [
        S((2, rows, 3 * cols // 2), F32), S((rows, cols), F32), S((rows, hidden), F32), S((rows, hidden), F32),
        x_part, x_part, S(small.shape, F32),
    ]
    wide = S((2,) + dp3 + (rows, hidden), BF16)
    acc = S((2 * own_rows, 2 * HD), F32)
    scratch = [
        S((own_rows, width), BF16), S((2, width, own_rows), BF16), S((2, own_rows, hidden), BF16),
        S((2, own_rows, cols), BF16), wide, wide, S((2,) + dp3 + (rows, cols), BF16),
        S((2,) + dp3 + (rows, 3 * cols // 2), BF16), acc, acc,
        S(small.shape, F32), S((3,) + small.shape, F32), S((6,) + small.shape, F32),
    ]
    copies = 1 + 1 + 6
    for n, parts in ((hidden, D_PARTS), (hidden, I_PARTS), (cols, O_PARTS)):
        for cut in cuts_of(n, parts):
            copies += 11
            scratch += [S(a, BF16) for a in reduce_bufs(rows, *cut)]
    for n in [3 * cols // 2] * 2:
        copies += 5
        scratch += [S(s, BF16) for s in ((4, 2, rows, n), (4, rows, n), (3, rows, n))]
    vm, hbm = pl.BlockSpec(memory_space=pltpu.VMEM), pl.BlockSpec(memory_space=pl.ANY)
    return pl.pallas_call(
        backward_kernel,
        name="backward",
        out_shape=outs,
        in_specs=[hbm] * 9 + [vm] * 6,
        out_specs=[vm] * 4 + [hbm] * 2 + [vm],
        scratch_shapes=[
            pltpu.SemaphoreType.DMA((copies,)), pltpu.SemaphoreType.DMA((copies,)),
            pltpu.SemaphoreType.DMA((BACKWARD_LOCAL,)),
        ]
        + [pltpu.VMEM(a.shape, a.dtype) for a in scratch],
        compiler_params=pltpu.CompilerParams(
            collective_id=1, has_side_effects=True, vmem_limit_bytes=VMEM_ALL
        ),
    )(d_ffn, mid, d_attn, act, d_pre, d_mix, qkv, embed, v_all, far, mine, stats, seg_row, seg_col, small)


BACKWARD_LOCAL = 16


def attend_kernel(tile, q_ref, k_ref, v_ref, sr_ref, sc_ref, o_ref, l_ref):
    length, width = q_ref.shape

    def step(t, _):
        rows = pl.ds(pl.multiple_of(t * tile, tile), tile)
        same = sc_ref[:, 0:1] == sr_ref[:, rows]
        for h in range(width // HD):
            cols = slice(h * HD, h * HD + HD)
            scores = dg(k_ref[:, cols], q_ref[rows, cols], 1, 1) * (1.0 / math.sqrt(HD))
            scores = jnp.where(same, scores, neg_big)
            row_max = jnp.max(scores, axis=0, keepdims=True)
            prob = jnp.exp(scores - row_max)
            total = jnp.sum(prob, axis=0, keepdims=True)
            mixed = dg(v_ref[:, cols], prob.astype(BF16), 0, 0) / total
            o_ref[rows, cols] = mixed.T.astype(BF16)
            l_ref[0, h : h + 1, rows] = row_max + jnp.log(total)
        return 0

    lax.fori_loop(0, length // tile, step, 0)


def attend_specs(length, heads_pairs):
    def col(k):
        return pl.BlockSpec((length, 2 * HD), lambda i, k=k: (0, k * heads_pairs + i))

    stats = pl.BlockSpec((1, 2, length), lambda i: (i, 0, 0))
    seg_row = pl.BlockSpec((1, length), lambda i: (0, 0))
    seg_col = pl.BlockSpec((length, 128), lambda i: (0, 0))
    return col, stats, seg_row, seg_col


def attend(qkv, segments):
    length = qkv.shape[0]
    pairs = qkv.shape[1] // 3 // (2 * HD)
    col, stats, seg_row, seg_col = attend_specs(length, pairs)
    return pl.pallas_call(
        functools.partial(attend_kernel, min(512, length)),
        name="attend",
        grid=(pairs,),
        in_specs=[col(0), col(1), col(2), seg_row, seg_col],
        out_specs=[col(0), stats],
        out_shape=[
            jax.ShapeDtypeStruct((length, pairs * 2 * HD), BF16),
            jax.ShapeDtypeStruct((pairs, 2, length), F32),
        ],
        cost_estimate=pl.CostEstimate(
            flops=8 * length * length * HD * pairs, bytes_accessed=4 * length * pairs * 256, transcendentals=0
        ),
    )(qkv, qkv, qkv, segments, jnp.broadcast_to(segments.reshape(length, 1), (length, 128)))


def attend_back_kernel(
    tile, q_ref, k_ref, v_ref, d_ref, o_ref, l_ref, sr_ref, sc_ref, dq_ref, dk_ref, dv_ref
):
    length, width = q_ref.shape
    scale = 1.0 / math.sqrt(HD)
    dk_ref[...] = jnp.zeros_like(dk_ref)
    dv_ref[...] = jnp.zeros_like(dv_ref)

    def step(t, _):
        rows = pl.ds(pl.multiple_of(t * tile, tile), tile)
        same = sc_ref[:, 0:1] == sr_ref[:, rows]
        for h in range(width // HD):
            cols = slice(h * HD, h * HD + HD)
            keys, q_rows, d_rows = k_ref[:, cols], q_ref[rows, cols], d_ref[rows, cols]
            delta = jnp.sum(
                (d_rows.astype(F32) * o_ref[rows, cols].astype(F32)).T, axis=0, keepdims=True
            )
            scores = dg(keys, q_rows, 1, 1) * scale
            prob = jnp.where(same, jnp.exp(scores - l_ref[0, h : h + 1, rows]), 0.0)
            d_prob = dg(v_ref[:, cols], d_rows, 1, 1)
            d_score = (prob * (d_prob - delta) * scale).astype(BF16)
            dv_ref[:, cols] += dg(prob.astype(BF16), d_rows, 1, 0)
            dk_ref[:, cols] += dg(d_score, q_rows, 1, 0)
            dq_ref[rows, cols] = dg(d_score, keys, 0, 0)
        return 0

    lax.fori_loop(0, length // tile, step, 0)


def attend_back(qkv, d_mixed, mixed, stats_in, segments):
    length = qkv.shape[0]
    pairs = qkv.shape[1] // 3 // (2 * HD)
    col, stats, seg_row, seg_col = attend_specs(length, pairs)
    return pl.pallas_call(
        functools.partial(attend_back_kernel, min(512, length)),
        name="attend_back",
        grid=(pairs,),
        in_specs=[col(0), col(1), col(2), col(0), col(0), stats, seg_row, seg_col],
        out_specs=[col(0)] * 3,
        out_shape=[jax.ShapeDtypeStruct((length, pairs * 2 * HD), F32)] * 3,
        cost_estimate=pl.CostEstimate(
            flops=20 * length * length * HD * pairs, bytes_accessed=8 * length * pairs * 256, transcendentals=0
        ),
    )(qkv, qkv, qkv, d_mixed, mixed, stats_in, segments, jnp.broadcast_to(segments.reshape(length, 1), (length, 128)))


def time_features(step_ids, model_width):
    half_width = model_width // 2
    frequency = jnp.exp(
        jnp.arange(half_width, dtype=F32) * (-math.log(10000.0) / half_width)
    )
    angles = step_ids.astype(F32)[:, None] * frequency[None, :]
    return jnp.concatenate([jnp.sin(angles), jnp.cos(angles)], axis=1)


def normalize(array_in):
    row_mean = jnp.mean(array_in, axis=-1, keepdims=True)
    centered = array_in - row_mean
    variance = jnp.mean(centered * centered, axis=-1, keepdims=True)
    inv_std = lax.rsqrt(variance + eps)
    return (centered * inv_std, inv_std)


def norm_back(grad_rows, unit_rows, inv_std, gain_row):
    d_unit = grad_rows * gain_row
    return inv_std * (
        d_unit
        - jnp.mean(d_unit, axis=-1, keepdims=True)
        - unit_rows * jnp.mean(d_unit * unit_rows, axis=-1, keepdims=True)
    )


def ein(spec, left, right):
    return jnp.einsum(spec, left, right, preferred_element_type=F32)


def on_device(
    hidden_in,
    segments,
    timesteps,
    time_weight,
    qkv_weight,
    out_weight,
    in_weight,
    down_weight,
    biases,
    gains,
    ffn_bias,
    out_grad,
    *,
    dp,
    mp,
):
    own_rows, width = hidden_in.shape
    length = segments.shape[1]
    rows = time_weight.shape[0]
    cols = qkv_weight.shape[2]
    hidden = in_weight.shape[1]
    dp_index, mp_index = lax.axis_index("dp"), lax.axis_index("mp")
    fast = (dp, mp) == (16, 2)

    bias_count = biases.shape[0] + gains.shape[0]
    v_shard = jnp.concatenate(
        [qkv_weight[0], qkv_weight[1], qkv_weight[2], biases.T, gains.T, jnp.zeros((rows, 128 - bias_count), BF16)],
        axis=1,
    )
    feature = time_features(timesteps, width).astype(BF16)
    few_row = jnp.concatenate([feature.astype(F32), ffn_bias.astype(F32)[None]], axis=1)
    seg_col = jnp.broadcast_to(segments.reshape(length, 1), (length, 128))
    if fast:
        (
            v_all, o_all, i_all, d_all, few, par, time_row, embed_low, qkv, mixed_heads, mixed_far,
            stats, unit_one, inv_one, middle_low, hidden_act, slope,
        ) = forward(
            v_shard, time_weight, few_row, biases[:1], out_weight.T, in_weight, down_weight.T,
            hidden_in, segments, seg_col,
        )
        few = few.reshape(dp, -1)
        inv_one = inv_one[:, :1]
    else:
        v_all = lax.all_gather(v_shard, "dp", axis=0)
        o_all, i_all, d_all = (
            lax.all_gather(lax.all_gather(a, "dp", axis=0), "mp", axis=0)
            for a in (out_weight.T, in_weight, down_weight.T)
        )
        few = lax.all_gather(few_row, "dp", axis=0, tiled=True)
        time_w = lax.all_gather(time_weight, "dp", axis=0, tiled=True)
    v_raw, v_all = v_all, v_all.reshape(width, -1)
    o_all, i_all, d_all = (a.reshape(mp, width, -1) for a in (o_all, i_all, d_all))
    qkv_w = v_all[:, : 3 * cols]
    column = mp_index * cols
    if fast:
        bias_all, gain_all = par[:7], par[7:9]
        middle = unit_one * gain_all[0] + bias_all[4]
    else:
        params = v_all[:, 3 * cols :].astype(F32).T
        bias_all, gain_all = params[:7], params[7:9]
        time_row = jnp.dot(feature, time_w, preferred_element_type=F32) + bias_all[0]
        h_all = lax.all_gather(hidden_in, "mp", axis=0, tiled=True)
        embedded = hidden_in.astype(F32) + time_row
        embed_low = (h_all.astype(F32) + time_row).astype(BF16)
        bias_qkv = jnp.concatenate(
            [
                lax.dynamic_slice_in_dim(bias_all[1], column, cols),
                jnp.zeros((cols,), F32),
                lax.dynamic_slice_in_dim(bias_all[2], column, cols),
            ]
        )
        qkv = (jnp.dot(embed_low, qkv_w, preferred_element_type=F32) + bias_qkv).astype(BF16)
        mixed_heads, stats = attend(qkv, segments)
        mixed = lax.all_to_all(mixed_heads.reshape(mp, own_rows, cols), "mp", 0, 0, tiled=True)
        attn_total = ein("yrk,ynk->rn", mixed, o_all)
        unit_one, inv_one = normalize(embedded + attn_total + bias_all[3])
        middle = unit_one * gain_all[0] + bias_all[4]
        middle_low = middle.astype(BF16)
        ffn_b = few[:, width:].reshape(mp, hidden)
        pre_act = ein("rd,ydf->yrf", middle_low, i_all) + ffn_b[:, None, :]
        below = 0.5 + 0.5 * lax.erf(pre_act * math.sqrt(0.5))
        hidden_act = (pre_act * below).astype(BF16)
        slope = below + pre_act * jnp.exp(-0.5 * pre_act * pre_act) * (1.0 / math.sqrt(2.0 * math.pi))

    ffn_total = ein("yrf,ynf->rn", hidden_act, d_all)
    unit_two, inv_two = normalize(middle + ffn_total + bias_all[5])
    layer_out = (unit_two * gain_all[1] + bias_all[6]).astype(BF16)

    grad_out = out_grad.astype(F32)
    gain_two_part = jnp.sum(grad_out * unit_two, axis=0)
    shift_two_part = jnp.sum(grad_out, axis=0)
    d_pre_two = norm_back(grad_out, unit_two, inv_two, gain_all[1])
    bias_five_part = jnp.sum(d_pre_two, axis=0)
    d_ffn = d_pre_two.astype(BF16)
    d_act = ein("rn,ynf->yrf", d_ffn, d_all)
    d_pre_act = d_act * slope.astype(F32)
    ffn_bias_part = jnp.sum(d_pre_act, axis=1).reshape(-1, width)
    d_pre_low = d_pre_act.astype(BF16)
    d_middle = d_pre_two + ein("yrf,ydf->rd", d_pre_low, i_all)
    gain_one_part = jnp.sum(d_middle * unit_one, axis=0)
    shift_one_part = jnp.sum(d_middle, axis=0)
    d_pre_one = norm_back(d_middle, unit_one, inv_one, gain_all[0])
    bias_three_part = jnp.sum(d_pre_one, axis=0)
    d_attn = d_pre_one.astype(BF16)
    d_mix = ein("rn,ynk->yrk", d_attn, o_all).astype(BF16)
    zero_row = jnp.zeros((width,), F32)
    sums = [bias_three_part, shift_one_part, bias_five_part, shift_two_part, gain_one_part, gain_two_part]

    def pad_rows(a):
        return jnp.pad(a, ((0, -a.shape[0] % 8), (0, 0)))

    if fast:
        small = jnp.concatenate([jnp.zeros((dp + 2, width), F32), jnp.stack(sums), ffn_bias_part], axis=0)
        v_sum, o_sum, i_sum, d_sum, d_near, d_far, small = backward(
            d_ffn, middle_low, d_attn, hidden_act, d_pre_low, d_mix, qkv.reshape(mp, own_rows, -1),
            embed_low.reshape(v_raw.shape[:4] + (width,)), v_raw, mixed_far, mixed_heads, stats, segments, seg_col,
            pad_rows(small),
        )
        d_own = (d_near.astype(F32) + d_far.astype(F32)).reshape(own_rows, width)
        qkv_grad = v_sum.reshape(2, rows, 3, -1).transpose(2, 1, 0, 3).reshape(3, rows, cols)
    else:
        embed_low = embed_low.reshape(length, width)
        mixed_heads = mixed_heads.reshape(length, cols)
        down_grad = ein("rn,yrf->ynf", d_ffn, hidden_act).astype(BF16)
        in_grad = ein("rd,yrf->ydf", middle_low, d_pre_low).astype(BF16)
        out_grad_t = ein("rn,yrk->ynk", d_attn, mixed).astype(BF16)
        d_mixed = lax.all_to_all(d_mix, "mp", 0, 0, tiled=True).reshape(length, cols)
        d_q, d_k, d_v = attend_back(qkv, d_mixed, mixed_heads, stats, segments)
        d_qkv = jnp.concatenate([d_q, d_k, d_v], axis=1).astype(BF16)
        v_grad = dg(embed_low, d_qkv, 0, 0).astype(BF16)
        d_embed = dg(d_qkv, qkv_w, 1, 1)
        time_part = bias_three_part + jnp.sum(d_embed, axis=0)
        d_embed = d_embed.astype(BF16).reshape(mp, own_rows, width)
        seq_rows = jnp.where(jnp.arange(dp)[:, None] == dp_index, time_part[None, :], 0.0)
        spread = [lax.dynamic_update_slice_in_dim(zero_row, jnp.sum(a, axis=0), column, 0) for a in (d_q, d_v)]
        small = pad_rows(jnp.concatenate([seq_rows, jnp.stack(spread + sums), ffn_bias_part], axis=0))
        v_sum = lax.psum_scatter(v_grad, "dp", scatter_dimension=0, tiled=True).astype(F32)

        def both(a):
            a = lax.psum_scatter(a, "mp", scatter_dimension=0)
            return lax.psum_scatter(a, "dp", scatter_dimension=0, tiled=True).astype(F32)

        o_sum, i_sum, d_sum = both(out_grad_t), both(in_grad), both(down_grad)
        d_own = lax.psum_scatter(d_embed, "mp", scatter_dimension=0).astype(F32)
        small = lax.psum(small, ("dp", "mp"))
        qkv_grad = v_sum.reshape(rows, 3, cols).transpose(1, 0, 2)

    input_grad = d_pre_one + d_own
    d_time = small[:dp]
    start = dp_index * rows
    features = few[:, :width]
    features = lax.dynamic_slice_in_dim(features, start, rows, axis=1)
    time_grad = lax.dot_general(
        features, d_time, (((0,), (0,)), ((), ())), precision=lax.Precision.HIGHEST
    )
    tail = small[dp:]
    bias_rows = jnp.concatenate([jnp.sum(d_time, axis=0)[None], tail[:6]], axis=0)
    bias_grad = lax.dynamic_slice_in_dim(bias_rows, start, rows, axis=1)
    gain_grad = lax.dynamic_slice_in_dim(tail[6:8], start, rows, axis=1)
    ffn_rows = ffn_bias.shape[0]
    ffn_all = tail[8:].reshape(-1)
    ffn_bias_grad = lax.dynamic_slice_in_dim(ffn_all, dp_index * ffn_rows, ffn_rows)
    return (
        layer_out,
        input_grad,
        time_grad,
        qkv_grad,
        o_sum.T,
        i_sum,
        d_sum.T,
        bias_grad,
        gain_grad,
        ffn_bias_grad,
    )


def solution(mesh):
    dp, mp = mesh.shape["dp"], mesh.shape["mp"]
    placed = (
        P(("dp", "mp"), None),
        P("dp", None),
        P("dp"),
        P("dp", None),
        P(None, "dp", "mp"),
        P("mp", "dp"),
        P("dp", "mp"),
        P("mp", "dp"),
        P(None, "dp"),
        P(None, "dp"),
        P("dp"),
        P(("dp", "mp"), None),
    )
    return jax.shard_map(
        functools.partial(on_device, dp=dp, mp=mp),
        mesh=mesh,
        in_specs=placed,
        out_specs=(
            P(("dp", "mp"), None),
            P(("dp", "mp"), None),
            P("dp", None),
            P(None, "dp", "mp"),
            P("mp", "dp"),
            P("dp", "mp"),
            P("mp", "dp"),
            P(None, "dp"),
            P(None, "dp"),
            P("dp"),
        ),
        check_vma=False,
    )
```

```python
import functools
import math

import jax
import jax.numpy as jnp
from jax import lax
from jax.experimental import pallas as pl
from jax.experimental.pallas import tpu as pltpu
from jax.sharding import PartitionSpec as P

HD = 64
eps = 1e-05
neg_big = -1000000000.0
MESH = pl.DeviceIdType.MESH
F32, BF16 = jnp.float32, jnp.bfloat16
VMEM_LIMIT, VMEM_ALL = 64000000, 67043328


def dg(left, right, left_dim, right_dim):
    return lax.dot_general(
        left, right, (((left_dim,), (right_dim,)), ((), ())), preferred_element_type=F32
    )


class Place:
    def __init__(self):
        i, y = lax.axis_index("dp"), lax.axis_index("mp")
        z, x, c = i // 4, (i // 2) % 2, i % 2
        self.i, self.z, self.x, self.c, self.y = i, z, x, c, y
        self.nx, self.nc, self.ny, self.zero = 1 - x, 1 - c, 1 - y, 0 * i
        low, high = z % 2, z // 2
        flipped = [(1 - 2 * bit) * v + bit for v, bit in ((low, 1), (high, 1))]
        self.zs = [high * 2 + flipped[0], flipped[1] * 2 + low, flipped[1] * 2 + flipped[0]]
        self.to_z = [((p * 2 + x) * 2 + c, y) for p in self.zs]
        self.to_x = ((z * 2 + self.nx) * 2 + c, y)
        self.to_y = (i, self.ny)
        self.to_c = ((z * 2 + x) * 2 + self.nc, y)
        self.count = [self.zero + j for j in range(3)]
        self.dp = [
            (pz * 2 + px) * 2 + pc
            for pz in [z] + self.zs
            for px in (x, self.nx)
            for pc in (c, self.nc)
        ][1:]

    def enter(self, all_dp):
        barrier = pltpu.get_barrier_semaphore()
        near = [self.to_y]
        near += [(p, self.y) for p in self.dp] if all_dp else self.to_z + [self.to_x, self.to_c]
        for one in near:
            pl.semaphore_signal(barrier, inc=1, device_id=one, device_id_type=MESH)
        pl.semaphore_wait(barrier, len(near))


class Wire:
    def __init__(self, at, send_sems, recv_sems):
        self.sems = [(send_sems.at[at.zero + k], recv_sems.at[at.zero + k]) for k in range(send_sems.shape[0])]
        self.used, self.open = 0, []

    def send(self, src, dst, to):
        k = self.used
        self.used += 1
        copy = pltpu.make_async_remote_copy(
            src_ref=src,
            dst_ref=dst,
            send_sem=self.sems[k][0],
            recv_sem=self.sems[k][1],
            device_id=to,
            device_id_type=MESH,
        )
        copy.start()
        self.open.append(copy)
        return copy

    def both(self, copy):
        copy.wait_send()
        self.open = [one for one in self.open if one is not copy]
        copy.wait_recv()

    def close(self):
        assert self.used == len(self.sems), self.used
        for copy in self.open:
            copy.wait_send()


class Local:
    def __init__(self, at, sems):
        self.sems, self.used, self.open = [sems.at[at.zero + k] for k in range(sems.shape[0])], 0, []

    def copy(self, src, dst):
        one = pltpu.make_async_copy(src, dst, self.sems[self.used])
        self.used += 1
        one.start()
        self.open.append(one)
        return one

    def wait(self, one):
        one.wait()
        self.open = [other for other in self.open if other is not one]

    def close(self):
        assert self.used == len(self.sems), self.used
        for one in self.open:
            one.wait()


D_CUTS = ((0.625, True), (0.625, True))
I_CUTS = ((0.625, True), (0.625, True))
O_CUTS = ((0.5, True),)

FORWARD_AFTER = {
    "start": ("v0", "v1", "o", "i0",),
    "few": ("v0", "v1", "o", "i1", "d0", "v0", "o",),
    "part": ("i0", "v1", "i0", "v0",),
    "emb": ("v1", "i1", "o", "d1",),
    "proj": ("i0", "o",),
    "a1": ("d0", "d1", "i1",),
    "a3": ("i1", "d0", "i0",),
    "a6": ("i1", "o",),
    "a7": ("i0", "d0", "o", "i1", "d1", "i0", "d0",),
    "f0": ("d1",),
    "f2": ("i1", "d1",),
    "f4": ("d0",),
    "f6": ("d1",),
    "end": ("d0", "d1",),
}


def cuts_of(width, parts):
    step = width // len(parts)
    return [(k * step, k * step + int(step * first), (k + 1) * step, early) for k, (first, early) in enumerate(parts)]


def gather_dp(wire, at, shard, whole, lo, hi):
    n = pl.ds(lo, hi - lo)
    own = whole.at[at.z, at.x, at.c, :, n]
    from_z = [wire.send(shard.at[:, n], own, to) for to in at.to_z]
    late = [wire.send(shard.at[:, n], own, at.to_c)]
    yield
    for k in from_z:
        k.wait_recv()
    ref = whole.at[:, at.x, at.c, :, n]
    from_x = wire.send(ref, ref, at.to_x)
    for p in at.zs:
        ref = whole.at[p, at.x, at.c, :, n]
        late.append(wire.send(ref, ref, at.to_c))
    yield
    from_x.wait_recv()
    ref = whole.at[:, at.nx, at.c, :, n]
    late.append(wire.send(ref, ref, at.to_c))
    yield
    for k in late:
        k.wait_recv()


def gather_all(wire, at, shard, whole, lo, mid, hi, early):
    a, b, ab = pl.ds(lo, mid - lo), pl.ds(mid, hi - mid), pl.ds(lo, hi - lo)
    y, z, x, c = at.y, at.z, at.x, at.c
    first = a if early else ab
    from_z_a = [wire.send(shard.at[:, first], whole.at[y, z, x, c, :, first], to) for to in at.to_z]
    if early:
        from_y_b = wire.send(shard.at[:, b], whole.at[y, z, x, c, :, b], at.to_y)
    late = [wire.send(shard.at[:, ab], whole.at[y, z, x, c, :, ab], at.to_c)]

    def to_core(*refs):
        for ref in refs:
            late.append(wire.send(ref, ref, at.to_c))

    yield
    if early:
        from_y_b.wait_recv()
        ref = whole.at[:, z, x, c, :, b]
        from_z_b = [wire.send(ref, ref, to) for to in at.to_z]
        to_core(whole.at[at.ny, z, x, c, :, b])
    else:
        for k in from_z_a:
            k.wait_recv()
        ref = whole.at[y, :, x, c, :, b]
        from_y_b = wire.send(ref, ref, at.to_y)
        to_core(*(whole.at[y, p, x, c, :, b] for p in at.zs))
    yield
    if early:
        for k in from_z_a:
            k.wait_recv()
    ref = whole.at[y, :, x, c, :, a]
    from_x_a = wire.send(ref, ref, at.to_x)
    to_core(*(whole.at[y, p, x, c, :, a] for p in at.zs))
    yield
    from_x_a.wait_recv()
    ref = whole.at[y, :, :, c, :, a]
    from_y_a = wire.send(ref, ref, at.to_y)
    to_core(whole.at[y, :, at.nx, c, :, a])
    yield
    if early:
        for k in from_z_b:
            k.wait_recv()
        to_core(*(whole.at[:, p, x, c, :, b] for p in at.zs))
    else:
        from_y_b.wait_recv()
        to_core(whole.at[at.ny, :, x, c, :, b])
    ref = whole.at[:, :, x, c, :, b]
    from_x_b = wire.send(ref, ref, at.to_x)
    yield
    from_y_a.wait_recv()
    from_x_b.wait_recv()
    to_core(whole.at[at.ny, :, :, c, :, a], whole.at[:, :, at.nx, c, :, b])
    yield
    for k in late:
        k.wait_recv()


def one_hot_rows(count, width, start):
    down = lax.broadcasted_iota(jnp.int32, (count, width), 0)
    across = lax.broadcasted_iota(jnp.int32, (count, width), 1)
    return jnp.where(down == across + start, 1.0, 0.0).astype(BF16)


def forward_kernel(
    v_ref, t_ref, f_ref, b_ref, o_ref, i_ref, d_ref, h_ref, sr_ref, sc_ref,
    v_out, o_out, i_out, d_all, few_out, par_out, time_out, embed_out, qkv_out, mine_out, far_out,
    stats_out, unit_out, inv_out, mid_out, act_out, slope_out,
    v_all, o_all, i_all, few, part, got, h_far, par, ffn_b, embed, qkv, mine, far, stats, unit, inv,
    mid, act, slope, send_sems, recv_sems, local_sems, tile_sems,
):
    at = Place()
    y, z, x, c = at.y, at.z, at.x, at.c
    at.enter(True)
    wire, local = Wire(at, send_sems, recv_sems), Local(at, local_sems)
    width = h_ref.shape[1]
    own_rows = h_ref.shape[0]
    rows = v_ref.shape[0]
    cols = o_ref.shape[1]
    hidden = i_ref.shape[1]
    length = 2 * own_rows

    from_few = [wire.send(f_ref, few.at[at.i], (p, y)) for p in at.dp]
    from_h = wire.send(h_ref, h_far, at.to_y)
    v_mid = 7 * 128
    streams = {
        "v0": gather_dp(wire, at, v_ref, v_all, 0, v_mid),
        "v1": gather_dp(wire, at, v_ref, v_all, v_mid, v_ref.shape[1]),
    }
    for name, shard, whole, parts in (("d", d_ref, d_all, D_CUTS), ("i", i_ref, i_all, I_CUTS), ("o", o_ref, o_all, O_CUTS)):
        for k, cut in enumerate(cuts_of(shard.shape[1], parts)):
            streams[name + str(k)] = gather_all(wire, at, shard, whole, *cut)
    streams["o"] = streams["o0"]
    begun = set()

    kept = [
        local.copy(v_ref, v_all.at[z, x, c]),
        local.copy(o_ref, o_all.at[y, z, x, c]),
        local.copy(i_ref, i_all.at[y, z, x, c]),
        local.copy(d_ref, d_all.at[y, z, x, c]),
    ]

    def run(step):
        for name in FORWARD_AFTER.get(step, ()):
            if name in begun:
                while kept:
                    local.wait(kept.pop())
            begun.add(name)
            next(streams[name], None)

    run("start")
    few[at.i] = f_ref[...]
    for k in from_few:
        k.wait_recv()
    seqs = few.shape[0]
    table = jnp.concatenate([few[s] for s in range(seqs)], axis=0)
    pick = one_hot_rows(width, rows, at.i * rows)
    feats = dg(table[:, :width].astype(BF16), pick, 1, 0).astype(BF16)
    partial = dg(feats, t_ref[...], 1, 0) + dg(b_ref[...], pick, 1, 1)
    for s in range(seqs):
        part[s] = partial[s : s + 1]
    ffn_b[...] = jnp.concatenate([few[s][:, width:] for s in range(seqs)], axis=1)
    local.copy(few, few_out)
    from_part = [wire.send(part.at[p], got.at[j], (p, y)) for j, p in enumerate(at.dp)]
    run("few")
    for k in from_part:
        k.wait_recv()
    total = part[at.i]
    for j in range(seqs - 1):
        total = total + got[j]
    time_out[...] = total
    run("part")

    from_h.wait_recv()
    step = 128

    def embed_rows(t, _):
        r = pl.ds(pl.multiple_of(t * step, step), step)
        embed[y, r] = (h_ref[r].astype(F32) + total).astype(BF16)
        embed[at.ny, r] = (h_far[r].astype(F32) + total).astype(BF16)
        return 0

    lax.fori_loop(0, own_rows // step, embed_rows, 0)
    local.copy(embed, embed_out)
    run("emb")
    local.copy(v_all, v_out)
    run("vdone")
    par[...] = v_all[:, :, :, :, 3 * cols :].reshape(width, 128).astype(F32).T
    local.copy(par, par_out)
    heads = pl.ds(pl.multiple_of(y * cols, cols), cols)
    bias_q, bias_v = par[1:2, heads], par[2:3, heads]

    step_q = 256

    def project(t, _):
        half, r = t // (own_rows // step_q), pl.ds(pl.multiple_of((t % (own_rows // step_q)) * step_q, step_q), step_q)
        whole_r = pl.ds(pl.multiple_of(t * step_q, step_q), step_q)
        left = embed[half, r]
        for j, bias in enumerate((bias_q, None, bias_v)):
            n = slice(j * cols, (j + 1) * cols)
            made = dg(left, v_all[:, :, :, :, n].reshape(width, cols), 1, 0)
            qkv[whole_r, n] = (made if bias is None else made + bias).astype(BF16)
        return 0

    lax.fori_loop(0, length // step_q, project, 0)
    local.copy(qkv, qkv_out)
    run("proj")

    pair, tile = 2 * HD, own_rows
    from_far = []

    def give(p):
        n = pl.ds(p * pair, pair)
        from_far.append(wire.send(mine.at[at.ny, :, n], far.at[:, n], at.to_y))

    def tick_of(t):
        if t % 2:
            give(t // 2)
        run("a" + str(t))

    ticks = {t: lambda t=t: tick_of(t) for t in range(8) if t % 2 or "a" + str(t) in FORWARD_AFTER}

    def attend_step(t, _):
        p, half = t // 2, t % 2
        r = pl.ds(pl.multiple_of(half * tile, tile), tile)
        n = pl.multiple_of(p * pair, pair)
        queries = qkv[r, pl.ds(n, pair)]
        keys = qkv[:, pl.ds(cols + n, pair)]
        values = qkv[:, pl.ds(2 * cols + n, pair)]
        same = sc_ref[:, 0:1] == sr_ref[:, r]
        made = []
        for h in range(2):
            k = slice(h * HD, h * HD + HD)
            scores = dg(keys[:, k], queries[:, k], 1, 1) * (1.0 / math.sqrt(HD))
            scores = jnp.where(same, scores, neg_big)
            row_max = jnp.max(scores, axis=0, keepdims=True)
            prob = jnp.exp(scores - row_max)
            row_total = jnp.sum(prob, axis=0, keepdims=True)
            made.append((dg(values[:, k], prob.astype(BF16), 0, 0) / row_total).T)
            stats[p, h : h + 1, r] = row_max + jnp.log(row_total)
        mine[half, :, pl.ds(n, pair)] = jnp.concatenate(made, axis=1).astype(BF16)
        for k, tick in ticks.items():
            pl.when(t == k)(lambda tick=tick: (tick(), None)[1])
        return 0

    lax.fori_loop(0, 2 * (cols // pair), attend_step, 0)
    local.copy(mine, mine_out)
    local.copy(stats, stats_out)
    local.copy(o_all, o_out)

    for k in from_far:
        k.wait_recv()
    local.copy(far, far_out)

    def project_out(t, _):
        r = pl.ds(pl.multiple_of(t * step_q, step_q), step_q)
        total_r = dg(mine[y, r], o_all[y].reshape(width, cols), 1, 1)
        total_r += dg(far[r], o_all[at.ny].reshape(width, cols), 1, 1)
        total_r += h_ref[r].astype(F32) + total + par[3:4]
        made, inv_std = normalize(total_r)
        unit[r] = made
        inv[r] = jnp.broadcast_to(inv_std, (step_q, 128))
        mid[r] = (made * par[7:8] + par[4:5]).astype(BF16)
        return 0

    lax.fori_loop(0, own_rows // step_q, project_out, 0)
    local.copy(unit, unit_out)
    local.copy(inv, inv_out)
    local.copy(mid, mid_out)
    run("out")

    chunk = 512
    later = {t: lambda t=t: run("f" + str(t)) for t in range(8) if "f" + str(t) in FORWARD_AFTER}

    def feed_step(t, _):
        side = t % 2
        n = pl.multiple_of((t // 2) * chunk, chunk)
        made = dg(mid[...], i_all[side, :, :, :, :, pl.ds(n, chunk)].reshape(width, chunk), 1, 0)
        made = made + ffn_b[:, pl.ds(pl.multiple_of(side * hidden, hidden) + n, chunk)]
        below = 0.5 + 0.5 * lax.erf(made * math.sqrt(0.5))
        act[side, :, pl.ds(n, chunk)] = (made * below).astype(BF16)
        bell = jnp.exp(-0.5 * made * made) * (1.0 / math.sqrt(2.0 * math.pi))
        slope[side, :, pl.ds(n, chunk)] = (below + made * bell).astype(BF16)
        pltpu.make_async_copy(
            act.at[side, :, pl.ds(n, chunk)], act_out.at[side, :, pl.ds(n, chunk)], tile_sems.at[0, t]
        ).start()
        pltpu.make_async_copy(
            slope.at[side, :, pl.ds(n, chunk)], slope_out.at[side, :, pl.ds(n, chunk)], tile_sems.at[1, t]
        ).start()
        for k, tick in later.items():
            pl.when(t == k)(lambda tick=tick: (tick(), None)[1])
        return 0

    tiles = 2 * hidden // chunk
    lax.fori_loop(0, tiles, feed_step, 0)
    local.copy(i_all, i_out)
    run("end")
    for t in range(tiles):
        n = pl.ds(0, chunk)
        pltpu.make_async_copy(act.at[0, :, n], act_out.at[0, :, n], tile_sems.at[0, t]).wait()
        pltpu.make_async_copy(slope.at[0, :, n], slope_out.at[0, :, n], tile_sems.at[1, t]).wait()
    local.close()
    wire.close()


def forward(v, t, few_row, bias_zero, o, i, d, h, seg_row, seg_col):
    rows, cols, hidden = v.shape[0], o.shape[1], i.shape[1]
    own_rows, width = h.shape
    length = 2 * own_rows
    pairs = cols // (2 * HD)
    S = jax.ShapeDtypeStruct
    dp3 = (4, 2, 2)
    v_all, o_all, i_all = S(dp3 + v.shape, BF16), S((2,) + dp3 + o.shape, BF16), S((2,) + dp3 + i.shape, BF16)
    few = S((16,) + few_row.shape, F32)
    par, time_row = S((128, width), F32), S((1, width), F32)
    embed, qkv = S((2, own_rows, width), BF16), S((length, 3 * cols), BF16)
    mine, far = S((2, own_rows, cols), BF16), S((own_rows, cols), BF16)
    stats = S((pairs, 2, length), F32)
    unit, inv, mid = S((own_rows, width), F32), S((own_rows, 128), F32), S((own_rows, width), BF16)
    act = S((2, own_rows, hidden), BF16)
    outs = [v_all, o_all, i_all, i_all, few, par, time_row, embed, qkv, mine, far, stats, unit, inv, mid, act, act]
    vm, hbm = pl.BlockSpec(memory_space=pltpu.VMEM), pl.BlockSpec(memory_space=pl.ANY)
    out_specs = [hbm] * len(outs)
    out_specs[6] = vm
    part, got = S((16, 1, width), F32), S((15, 1, width), F32)
    h_far, ffn_b = S(h.shape, BF16), S((1, 2 * hidden), F32)
    scratch = [v_all, o_all, i_all, few, part, got, h_far, par, ffn_b, embed, qkv, mine, far, stats, unit, inv, mid, act, act]
    copies = 15 + 15 + 1 + 2 * 9 + sum(21 if early else 18 for _, early in D_CUTS + I_CUTS + O_CUTS) + pairs
    return pl.pallas_call(
        forward_kernel,
        name="forward",
        out_shape=outs,
        in_specs=[vm] * 10,
        out_specs=out_specs,
        scratch_shapes=[pltpu.VMEM(a.shape, a.dtype) for a in scratch]
        + [
            pltpu.SemaphoreType.DMA((copies,)),
            pltpu.SemaphoreType.DMA((copies,)),
            pltpu.SemaphoreType.DMA((FORWARD_LOCAL,)),
            pltpu.SemaphoreType.DMA((2, 2 * hidden // 512)),
        ],
        compiler_params=pltpu.CompilerParams(
            collective_id=0, has_side_effects=True, vmem_limit_bytes=VMEM_LIMIT
        ),
    )(v, t, few_row, bias_zero, o, i, d, h, seg_row, seg_col)


FORWARD_LOCAL = 17


def add_blocks(dst, left, right, lead):
    count = math.prod(lead)

    def one(t, _):
        at = []
        for n in reversed(lead):
            at.append(t % n)
            t = t // n
        at = tuple(reversed(at))
        dst[at] = (left[at].astype(F32) + right[at].astype(F32)).astype(dst.dtype)
        return 0

    lax.fori_loop(0, count, one, 0)


def reduce_dp(wire, at, grad, rc, rx, rz, out):
    z, x, c, y = at.z, at.x, at.c, at.y
    from_c = wire.send(grad.at[:, :, at.nc], rc, at.to_c)
    yield
    wire.both(from_c)
    add_blocks(rc, grad.at[:, :, c], rc, (4, 2))
    from_x = wire.send(rc.at[:, at.nx], rx, at.to_x)
    yield
    from_x.wait_recv()
    add_blocks(rx, rc.at[:, x], rx, (4,))
    from_z = [wire.send(rx.at[p], rz.at[at.count[j]], to) for j, (p, to) in enumerate(zip(at.zs, at.to_z))]
    yield
    for k in from_z:
        k.wait_recv()
    out[...] = ((rx[z].astype(F32) + rz[0].astype(F32)) + rz[1].astype(F32)) + rz[2].astype(F32)


def reduce_all(wire, at, grad, bufs, out, lo, mid, hi, early):
    rc, ya, xb, xa, za, zb, yb, zs = bufs
    z, x, c, y = at.z, at.x, at.c, at.y
    a, b, ab = pl.ds(lo, mid - lo), pl.ds(mid, hi - mid), pl.ds(lo, hi - lo)
    half_a, half_b = pl.ds(0, mid - lo), pl.ds(mid - lo, hi - mid)

    def over_z(pick, got):
        return [wire.send(pick(p), got.at[at.count[j]], to) for j, (p, to) in enumerate(zip(at.zs, at.to_z))]

    def add_z(own, got):
        return ((own.astype(F32) + got[0].astype(F32)) + got[1].astype(F32)) + got[2].astype(F32)

    from_c = wire.send(grad.at[:, :, :, at.nc, :, ab], rc, at.to_c)
    yield
    wire.both(from_c)
    add_blocks(rc, grad.at[:, :, :, c, :, ab], rc, (2, 4, 2))
    from_y_a = wire.send(rc.at[at.ny, :, :, :, half_a], ya, at.to_y)
    from_x_b = wire.send(rc.at[:, :, at.nx, :, half_b], xb, at.to_x)
    yield
    from_y_a.wait_recv()
    add_blocks(ya, rc.at[y, :, :, :, half_a], ya, (4, 2))
    from_x_a = wire.send(ya.at[:, at.nx], xa, at.to_x)
    yield
    from_x_b.wait_recv()
    add_blocks(xb, rc.at[:, :, x, :, half_b], xb, (2, 4))
    if early:
        from_z_b = over_z(lambda p: xb.at[:, p], zb)
    else:
        from_y_b = wire.send(xb.at[at.ny], yb, at.to_y)
    yield
    from_x_a.wait_recv()
    add_blocks(xa, ya.at[:, x], xa, (4,))
    from_z_a = over_z(lambda p: xa.at[p], za)
    yield
    if early:
        for k in from_z_b:
            k.wait_recv()
        zs[...] = add_z(xb[:, z], zb).astype(BF16)
        from_y_b = wire.send(zs.at[at.ny], yb, at.to_y)
    else:
        from_y_b.wait_recv()
        add_blocks(yb, xb.at[y], yb, (4,))
        from_z_b = over_z(lambda p: yb.at[p], zb)
    yield
    for k in from_z_a:
        k.wait_recv()
    out[:, a] = add_z(xa[z], za)
    if early:
        from_y_b.wait_recv()
        out[:, b] = zs[y].astype(F32) + yb[...].astype(F32)
    else:
        for k in from_z_b:
            k.wait_recv()
        out[:, b] = add_z(yb[z], zb)


def reduce_bufs(rows, lo, mid, hi, early):
    ha, hb = mid - lo, hi - mid
    last = [(3, 2, rows, hb), (rows, hb), (2, rows, hb)] if early else [(3, rows, hb), (4, rows, hb), (8, 128)]
    return [(2, 4, 2, rows, hi - lo), (4, 2, rows, ha), (2, 4, rows, hb), (4, rows, ha), (3, rows, ha)] + last


def reduce_small(wire, at, mine, sums, got, out):
    k = wire.send(mine, got.at[0], at.to_c)
    yield
    k.wait_recv()
    sums[0] = mine[...] + got[0]
    k = wire.send(sums.at[0], got.at[1], at.to_x)
    yield
    k.wait_recv()
    sums[1] = sums[0] + got[1]
    k = wire.send(sums.at[1], got.at[2], at.to_y)
    yield
    k.wait_recv()
    sums[2] = sums[1] + got[2]
    last = [wire.send(sums.at[2], got.at[3 + j], to) for j, to in enumerate(at.to_z)]
    yield
    for k in last:
        k.wait_recv()
    out[...] = ((sums[2] + got[3]) + got[4]) + got[5]


D_PARTS = ((0.75, True), (0.5, True), (0.75, True), (0.5, True))
I_PARTS = ((0.75, True), (0.5, True), (0.5, False), (0.75, False))
O_PARTS = ((0.5, False),)

AFTER = {
    "pd0": ("d0",),
    "pd2": ("d1",),
    "pd3": ("d3", "d0",),
    "pi0": ("d1",),
    "pi1": ("i0",),
    "pi2": ("d2", "d3", "i1",),
    "pi3": ("d0",),
    "po": ("d1", "d2", "d1", "i3",),
    "emb": ("d0", "i2", "d0", "i1",),
    "a0": ("d3", "i0", "d3",),
    "a1": ("d2", "d1", "i2", "o", "d2",),
    "a2": ("i1",),
    "a3": ("d3", "i1",),
    "vp0": ("i0", "i0", "o", "d2",),
    "a4": ("i2", "i1", "i3",),
    "a5": ("o", "i2",),
    "a6": ("i0",),
    "a7": ("i2",),
    "vp1": ("v0", "v1", "i3", "o", "i3", "i2",),
    "e0": ("o", "v0", "o", "i3",),
    "e1": ("t", "i0", "v1", "i3", "v0", "t", "v1", "i3", "t", "i2", "t", "v1", "i1", "o", "d3", "d1", "d2", "d2", "d1", "d3", "v0", "i1", "d0", "d0", "i0", "t",),
}


def turn_rows(src, dst):
    def one(t, _):
        r = pl.ds(pl.multiple_of(t * 128, 128), 128)
        dst[r, :] = src[:, r].astype(F32).T.astype(BF16)
        return 0

    lax.fori_loop(0, src.shape[1] // 128, one, 0)


def backward_kernel(
    ffn_ref, mid_ref, attn_ref, act_ref, pre_ref, mix_ref, qkv_ref, embed_ref, v_ref,
    far_ref, mine_ref, stats_ref, sr_ref, sc_ref, small_ref,
    v_out, o_out, i_out, d_out, x_own, x_got, s_out, *rest,
):
    at = Place()
    y = at.y
    at.enter(False)
    rest = iter(rest)
    wire, local = Wire(at, next(rest), next(rest)), Local(at, next(rest))
    raw, tr, big, d_heads, d_g, i_g, o_g, v_g, acc_k, acc_v, table, sums, got = (next(rest) for _ in range(13))
    own_rows, width = raw.shape
    hidden, cols, length = big.shape[2], d_heads.shape[2], 2 * own_rows

    streams = {}
    for name, grad, out, parts in (("d", d_g, d_out, D_PARTS), ("i", i_g, i_out, I_PARTS), ("o", o_g, o_out, O_PARTS)):
        for k, cut in enumerate(cuts_of(out.shape[1], parts)):
            bufs = [next(rest) for _ in range(8)]
            streams[name + str(k)] = reduce_all(wire, at, grad, bufs, out, *cut)
    streams["o"] = streams["o0"]
    for k in range(2):
        bufs = [next(rest) for _ in range(3)]
        streams["v" + str(k)] = reduce_dp(wire, at, v_g.at[at.count[k]], *bufs, v_out.at[at.count[k]])
    streams["t"] = reduce_small(wire, at, table, sums, got, s_out)

    def run(step):
        for name in AFTER.get(step, ()):
            next(streams[name], None)

    done = local.wait

    from_mix = wire.send(mix_ref.at[at.ny], d_heads.at[y], at.to_y)
    chunk = 512
    pieces = [pl.ds(lo, chunk) for lo in range(0, hidden, chunk)]
    raw_in = local.copy(ffn_ref, raw)
    act_in = [local.copy(act_ref.at[:, :, n], big.at[:, :, n]) for n in pieces]
    pre_in = []
    mix_in = local.copy(mix_ref.at[y], d_heads.at[y])
    table[...] = small_ref[...]
    done(raw_in)
    turn_rows(raw, tr.at[0])
    raw_in = local.copy(mid_ref, raw)

    def products(left, grad, arrived, after):
        steps = {2 * k + 1: (lambda k=k: after(k)) for k in range(len(pieces))}

        def one(t, _):
            n = pl.ds(pl.multiple_of((t // 2) * chunk, chunk), chunk)
            made = dg(left[...], big[t % 2, :, n], 1, 0).astype(BF16)
            grad[t % 2, :, :, :, :, n] = made.reshape(grad.shape[1:5] + (chunk,))
            for k, step in steps.items():
                pl.when(t == k)(lambda step=step: (step(), None)[1])
            return 0

        done(arrived[0])
        lax.fori_loop(0, 2 * len(pieces), one, 0)

    def after_down(k):
        pre_in.append(local.copy(pre_ref.at[:, :, pieces[k]], big.at[:, :, pieces[k]]))
        run("pd" + str(k))
        if k + 1 < len(pieces):
            done(act_in[k + 1])

    def after_in(k):
        run("pi" + str(k))
        if k + 1 < len(pieces):
            done(pre_in[k + 1])

    products(tr.at[0], d_g, act_in, after_down)
    done(raw_in)
    turn_rows(raw, tr.at[1])
    raw_in = local.copy(attn_ref, raw)
    products(tr.at[1], i_g, pre_in, after_in)
    qkv_in = local.copy(qkv_ref, big.at[:, :, 0 : 3 * cols])
    done(raw_in)
    turn_rows(raw, tr.at[0])
    for side, right in ((y, mine_ref.at[y]), (at.ny, far_ref)):
        made = dg(tr[0], right[...], 1, 0).astype(BF16)
        o_g[side] = made.reshape(o_g.shape[1:])
    run("po")

    embed_in = local.copy(embed_ref, d_g.at[0, :, :, :, :, 0:width])
    v_in = local.copy(v_ref, d_g.at[1, :, :, :, :, 0 : v_ref.shape[4]])
    done(embed_in)

    def turn_embed(t, _):
        n = pl.ds(pl.multiple_of(t * 128, 128), 128)
        block = d_g[0, :, :, :, :, n].reshape(length, 128)
        d_g[0, t // 2, t % 2, :, :, width : 2 * width] = (
            block.astype(F32).T.astype(BF16).reshape(d_g.shape[3:5] + (length,))
        )
        return 0

    lax.fori_loop(0, width // 128, turn_embed, 0)
    done(v_in)
    done(qkv_in)
    done(mix_in)
    from_mix.wait_recv()
    run("emb")

    part_cols = cols // 2

    def project_grad(k):
        def one(j, _):
            n = pl.ds(pl.multiple_of(j * cols + k * part_cols, part_cols), part_cols)
            made = dg(
                d_g[0, :, :, :, :, width : 2 * width].reshape(width, length),
                big[:, :, n].reshape(length, part_cols), 1, 0,
            ).astype(BF16)
            v_g[k, :, :, :, :, pl.ds(pl.multiple_of(j * part_cols, part_cols), part_cols)] = made.reshape(
                v_g.shape[1:5] + (part_cols,)
            )
            return 0

        lax.fori_loop(0, 3, one, 0)

    pair = 2 * HD
    scale = 1.0 / math.sqrt(HD)
    def tick_of(t):
        run("a" + str(t))
        if t % 4 == 3:
            run("vp" + str(t // 4))

    ticks = {t: lambda t=t: tick_of(t) for t in range(8)}

    def attend_step(t, _):
        p, half = t // 2, t % 2
        n = pl.multiple_of(p * pair, pair)
        r = pl.ds(pl.multiple_of(half * own_rows, own_rows), own_rows)
        cq, ck, cv = pl.ds(n, pair), pl.ds(cols + n, pair), pl.ds(2 * cols + n, pair)
        same = sc_ref[:, 0:1] == sr_ref[:, r]
        queries = big[half, :, cq]
        keys, values = big[:, :, ck].reshape(length, pair), big[:, :, cv].reshape(length, pair)
        d_rows, o_rows = d_heads[half, :, cq], mine_ref[half, :, cq]
        here = pl.ds(pl.multiple_of(y * cols + n, pair), pair)
        d_q, d_k, d_v = [], [], []
        for h in range(2):
            k = slice(h * HD, h * HD + HD)
            delta = jnp.sum((d_rows[:, k].astype(F32) * o_rows[:, k].astype(F32)).T, axis=0, keepdims=True)
            scores = dg(keys[:, k], queries[:, k], 1, 1) * scale
            prob = jnp.where(same, jnp.exp(scores - stats_ref[p, h : h + 1, r]), 0.0)
            d_prob = dg(values[:, k], d_rows[:, k], 1, 1)
            d_score = (prob * (d_prob - delta) * scale).astype(BF16)
            d_v.append(dg(prob.astype(BF16), d_rows[:, k], 1, 0))
            d_k.append(dg(d_score, queries[:, k], 1, 0))
            d_q.append(dg(d_score, keys[:, k], 0, 0))
        d_q, d_k, d_v = (jnp.concatenate(a, axis=1) for a in (d_q, d_k, d_v))
        big[half, :, cq] = d_q.astype(BF16)
        table[16:17, here] += jnp.sum(d_q, axis=0, keepdims=True)
        table[17:18, here] += jnp.sum(d_v, axis=0, keepdims=True)

        @pl.when(half == 0)
        def _():
            acc_k[...] = d_k
            acc_v[...] = d_v

        @pl.when(half == 1)
        def _():
            big[:, :, ck] = (acc_k[...] + d_k).astype(BF16).reshape(2, own_rows, pair)
            big[:, :, cv] = (acc_v[...] + d_v).astype(BF16).reshape(2, own_rows, pair)

        pl.when(t % 4 == 3)(lambda: project_grad(t // 4))
        for k, tick in ticks.items():
            pl.when(t == k)(lambda tick=tick: (tick(), None)[1])
        return 0

    lax.fori_loop(0, 2 * (cols // pair), attend_step, 0)

    step = 256
    per_half = own_rows // step

    def rows_of(half):
        return i_g.at[at.zero, pl.ds(2 * half, 2), :, :, :, 0:width]

    def embed_grad(t, acc):
        half = (at.ny + t // per_half) % 2
        r = pl.ds(pl.multiple_of((t % per_half) * step, step), step)
        made = dg(
            big[half, r, 0 : 3 * cols],
            d_g[1, :, :, :, :, 0 : 3 * cols].reshape(width, 3 * cols), 1, 1,
        )
        i_g[0, 2 * half + t % per_half, :, :, :, 0:width] = made.astype(BF16).reshape(i_g.shape[2:5] + (width,))

        @pl.when(t == per_half - 1)
        def _():
            from_x.append(wire.send(far_rows, x_got, at.to_y))
            run("e0")

        return acc + jnp.sum(made, axis=0, keepdims=True)

    from_x, far_rows = [], rows_of(at.ny)
    total = lax.fori_loop(0, 2 * per_half, embed_grad, table[18:19])
    local.copy(rows_of(y), x_own)
    down = lax.broadcasted_iota(jnp.int32, (16, width), 0)
    table[0:16] = jnp.where(down == at.i, total, 0.0)
    run("e1")
    from_x[0].wait_recv()
    local.close()
    wire.close()


def backward(d_ffn, mid, d_attn, act, d_pre, d_mix, qkv, embed, v_all, far, mine, stats, seg_row, seg_col, small):
    own_rows, width = mid.shape
    hidden, cols, rows = act.shape[2], far.shape[1], v_all.shape[3]
    dp3 = (4, 2, 2)
    S = jax.ShapeDtypeStruct
    x_part = S((2, 2, 2, rows, width), BF16)
    outs = [
        S((2, rows, 3 * cols // 2), F32), S((rows, cols), F32), S((rows, hidden), F32), S((rows, hidden), F32),
        x_part, x_part, S(small.shape, F32),
    ]
    wide = S((2,) + dp3 + (rows, hidden), BF16)
    acc = S((2 * own_rows, 2 * HD), F32)
    scratch = [
        S((own_rows, width), BF16), S((2, width, own_rows), BF16), S((2, own_rows, hidden), BF16),
        S((2, own_rows, cols), BF16), wide, wide, S((2,) + dp3 + (rows, cols), BF16),
        S((2,) + dp3 + (rows, 3 * cols // 2), BF16), acc, acc,
        S(small.shape, F32), S((3,) + small.shape, F32), S((6,) + small.shape, F32),
    ]
    copies = 1 + 1 + 6
    for n, parts in ((hidden, D_PARTS), (hidden, I_PARTS), (cols, O_PARTS)):
        for cut in cuts_of(n, parts):
            copies += 11
            scratch += [S(a, BF16) for a in reduce_bufs(rows, *cut)]
    for n in [3 * cols // 2] * 2:
        copies += 5
        scratch += [S(s, BF16) for s in ((4, 2, rows, n), (4, rows, n), (3, rows, n))]
    vm, hbm = pl.BlockSpec(memory_space=pltpu.VMEM), pl.BlockSpec(memory_space=pl.ANY)
    return pl.pallas_call(
        backward_kernel,
        name="backward",
        out_shape=outs,
        in_specs=[hbm] * 9 + [vm] * 6,
        out_specs=[vm] * 4 + [hbm] * 2 + [vm],
        scratch_shapes=[
            pltpu.SemaphoreType.DMA((copies,)), pltpu.SemaphoreType.DMA((copies,)),
            pltpu.SemaphoreType.DMA((BACKWARD_LOCAL,)),
        ]
        + [pltpu.VMEM(a.shape, a.dtype) for a in scratch],
        compiler_params=pltpu.CompilerParams(
            collective_id=1, has_side_effects=True, vmem_limit_bytes=VMEM_ALL
        ),
    )(d_ffn, mid, d_attn, act, d_pre, d_mix, qkv, embed, v_all, far, mine, stats, seg_row, seg_col, small)


BACKWARD_LOCAL = 16


def attend_kernel(tile, q_ref, k_ref, v_ref, sr_ref, sc_ref, o_ref, l_ref):
    length, width = q_ref.shape

    def step(t, _):
        rows = pl.ds(pl.multiple_of(t * tile, tile), tile)
        same = sc_ref[:, 0:1] == sr_ref[:, rows]
        for h in range(width // HD):
            cols = slice(h * HD, h * HD + HD)
            scores = dg(k_ref[:, cols], q_ref[rows, cols], 1, 1) * (1.0 / math.sqrt(HD))
            scores = jnp.where(same, scores, neg_big)
            row_max = jnp.max(scores, axis=0, keepdims=True)
            prob = jnp.exp(scores - row_max)
            total = jnp.sum(prob, axis=0, keepdims=True)
            mixed = dg(v_ref[:, cols], prob.astype(BF16), 0, 0) / total
            o_ref[rows, cols] = mixed.T.astype(BF16)
            l_ref[0, h : h + 1, rows] = row_max + jnp.log(total)
        return 0

    lax.fori_loop(0, length // tile, step, 0)


def attend_specs(length, heads_pairs):
    def col(k):
        return pl.BlockSpec((length, 2 * HD), lambda i, k=k: (0, k * heads_pairs + i))

    stats = pl.BlockSpec((1, 2, length), lambda i: (i, 0, 0))
    seg_row = pl.BlockSpec((1, length), lambda i: (0, 0))
    seg_col = pl.BlockSpec((length, 128), lambda i: (0, 0))
    return col, stats, seg_row, seg_col


def attend(qkv, segments):
    length = qkv.shape[0]
    pairs = qkv.shape[1] // 3 // (2 * HD)
    col, stats, seg_row, seg_col = attend_specs(length, pairs)
    return pl.pallas_call(
        functools.partial(attend_kernel, min(512, length)),
        name="attend",
        grid=(pairs,),
        in_specs=[col(0), col(1), col(2), seg_row, seg_col],
        out_specs=[col(0), stats],
        out_shape=[
            jax.ShapeDtypeStruct((length, pairs * 2 * HD), BF16),
            jax.ShapeDtypeStruct((pairs, 2, length), F32),
        ],
        cost_estimate=pl.CostEstimate(
            flops=8 * length * length * HD * pairs, bytes_accessed=4 * length * pairs * 256, transcendentals=0
        ),
    )(qkv, qkv, qkv, segments, jnp.broadcast_to(segments.reshape(length, 1), (length, 128)))


def attend_back_kernel(
    tile, q_ref, k_ref, v_ref, d_ref, o_ref, l_ref, sr_ref, sc_ref, dq_ref, dk_ref, dv_ref
):
    length, width = q_ref.shape
    scale = 1.0 / math.sqrt(HD)
    dk_ref[...] = jnp.zeros_like(dk_ref)
    dv_ref[...] = jnp.zeros_like(dv_ref)

    def step(t, _):
        rows = pl.ds(pl.multiple_of(t * tile, tile), tile)
        same = sc_ref[:, 0:1] == sr_ref[:, rows]
        for h in range(width // HD):
            cols = slice(h * HD, h * HD + HD)
            keys, q_rows, d_rows = k_ref[:, cols], q_ref[rows, cols], d_ref[rows, cols]
            delta = jnp.sum(
                (d_rows.astype(F32) * o_ref[rows, cols].astype(F32)).T, axis=0, keepdims=True
            )
            scores = dg(keys, q_rows, 1, 1) * scale
            prob = jnp.where(same, jnp.exp(scores - l_ref[0, h : h + 1, rows]), 0.0)
            d_prob = dg(v_ref[:, cols], d_rows, 1, 1)
            d_score = (prob * (d_prob - delta) * scale).astype(BF16)
            dv_ref[:, cols] += dg(prob.astype(BF16), d_rows, 1, 0)
            dk_ref[:, cols] += dg(d_score, q_rows, 1, 0)
            dq_ref[rows, cols] = dg(d_score, keys, 0, 0)
        return 0

    lax.fori_loop(0, length // tile, step, 0)


def attend_back(qkv, d_mixed, mixed, stats_in, segments):
    length = qkv.shape[0]
    pairs = qkv.shape[1] // 3 // (2 * HD)
    col, stats, seg_row, seg_col = attend_specs(length, pairs)
    return pl.pallas_call(
        functools.partial(attend_back_kernel, min(512, length)),
        name="attend_back",
        grid=(pairs,),
        in_specs=[col(0), col(1), col(2), col(0), col(0), stats, seg_row, seg_col],
        out_specs=[col(0)] * 3,
        out_shape=[jax.ShapeDtypeStruct((length, pairs * 2 * HD), F32)] * 3,
        cost_estimate=pl.CostEstimate(
            flops=20 * length * length * HD * pairs, bytes_accessed=8 * length * pairs * 256, transcendentals=0
        ),
    )(qkv, qkv, qkv, d_mixed, mixed, stats_in, segments, jnp.broadcast_to(segments.reshape(length, 1), (length, 128)))


def time_features(step_ids, model_width):
    half_width = model_width // 2
    frequency = jnp.exp(
        jnp.arange(half_width, dtype=F32) * (-math.log(10000.0) / half_width)
    )
    angles = step_ids.astype(F32)[:, None] * frequency[None, :]
    return jnp.concatenate([jnp.sin(angles), jnp.cos(angles)], axis=1)


def normalize(array_in):
    row_mean = jnp.mean(array_in, axis=-1, keepdims=True)
    centered = array_in - row_mean
    variance = jnp.mean(centered * centered, axis=-1, keepdims=True)
    inv_std = lax.rsqrt(variance + eps)
    return (centered * inv_std, inv_std)


def norm_back(grad_rows, unit_rows, inv_std, gain_row):
    d_unit = grad_rows * gain_row
    return inv_std * (
        d_unit
        - jnp.mean(d_unit, axis=-1, keepdims=True)
        - unit_rows * jnp.mean(d_unit * unit_rows, axis=-1, keepdims=True)
    )


def ein(spec, left, right):
    return jnp.einsum(spec, left, right, preferred_element_type=F32)


def on_device(
    hidden_in,
    segments,
    timesteps,
    time_weight,
    qkv_weight,
    out_weight,
    in_weight,
    down_weight,
    biases,
    gains,
    ffn_bias,
    out_grad,
    *,
    dp,
    mp,
):
    own_rows, width = hidden_in.shape
    length = segments.shape[1]
    rows = time_weight.shape[0]
    cols = qkv_weight.shape[2]
    hidden = in_weight.shape[1]
    dp_index, mp_index = lax.axis_index("dp"), lax.axis_index("mp")
    fast = (dp, mp) == (16, 2)

    bias_count = biases.shape[0] + gains.shape[0]
    v_shard = jnp.concatenate(
        [qkv_weight[0], qkv_weight[1], qkv_weight[2], biases.T, gains.T, jnp.zeros((rows, 128 - bias_count), BF16)],
        axis=1,
    )
    feature = time_features(timesteps, width).astype(BF16)
    few_row = jnp.concatenate([feature.astype(F32), ffn_bias.astype(F32)[None]], axis=1)
    seg_col = jnp.broadcast_to(segments.reshape(length, 1), (length, 128))
    if fast:
        (
            v_all, o_all, i_all, d_all, few, par, time_row, embed_low, qkv, mixed_heads, mixed_far,
            stats, unit_one, inv_one, middle_low, hidden_act, slope,
        ) = forward(
            v_shard, time_weight, few_row, biases[:1], out_weight.T, in_weight, down_weight.T,
            hidden_in, segments, seg_col,
        )
        few = few.reshape(dp, -1)
        inv_one = inv_one[:, :1]
    else:
        v_all = lax.all_gather(v_shard, "dp", axis=0)
        o_all, i_all, d_all = (
            lax.all_gather(lax.all_gather(a, "dp", axis=0), "mp", axis=0)
            for a in (out_weight.T, in_weight, down_weight.T)
        )
        few = lax.all_gather(few_row, "dp", axis=0, tiled=True)
        time_w = lax.all_gather(time_weight, "dp", axis=0, tiled=True)
    v_raw, v_all = v_all, v_all.reshape(width, -1)
    o_all, i_all, d_all = (a.reshape(mp, width, -1) for a in (o_all, i_all, d_all))
    qkv_w = v_all[:, : 3 * cols]
    column = mp_index * cols
    if fast:
        bias_all, gain_all = par[:7], par[7:9]
        middle = unit_one * gain_all[0] + bias_all[4]
    else:
        params = v_all[:, 3 * cols :].astype(F32).T
        bias_all, gain_all = params[:7], params[7:9]
        time_row = jnp.dot(feature, time_w, preferred_element_type=F32) + bias_all[0]
        h_all = lax.all_gather(hidden_in, "mp", axis=0, tiled=True)
        embedded = hidden_in.astype(F32) + time_row
        embed_low = (h_all.astype(F32) + time_row).astype(BF16)
        bias_qkv = jnp.concatenate(
            [
                lax.dynamic_slice_in_dim(bias_all[1], column, cols),
                jnp.zeros((cols,), F32),
                lax.dynamic_slice_in_dim(bias_all[2], column, cols),
            ]
        )
        qkv = (jnp.dot(embed_low, qkv_w, preferred_element_type=F32) + bias_qkv).astype(BF16)
        mixed_heads, stats = attend(qkv, segments)
        mixed = lax.all_to_all(mixed_heads.reshape(mp, own_rows, cols), "mp", 0, 0, tiled=True)
        attn_total = ein("yrk,ynk->rn", mixed, o_all)
        unit_one, inv_one = normalize(embedded + attn_total + bias_all[3])
        middle = unit_one * gain_all[0] + bias_all[4]
        middle_low = middle.astype(BF16)
        ffn_b = few[:, width:].reshape(mp, hidden)
        pre_act = ein("rd,ydf->yrf", middle_low, i_all) + ffn_b[:, None, :]
        below = 0.5 + 0.5 * lax.erf(pre_act * math.sqrt(0.5))
        hidden_act = (pre_act * below).astype(BF16)
        slope = below + pre_act * jnp.exp(-0.5 * pre_act * pre_act) * (1.0 / math.sqrt(2.0 * math.pi))

    ffn_total = ein("yrf,ynf->rn", hidden_act, d_all)
    unit_two, inv_two = normalize(middle + ffn_total + bias_all[5])
    layer_out = (unit_two * gain_all[1] + bias_all[6]).astype(BF16)

    grad_out = out_grad.astype(F32)
    gain_two_part = jnp.sum(grad_out * unit_two, axis=0)
    shift_two_part = jnp.sum(grad_out, axis=0)
    d_pre_two = norm_back(grad_out, unit_two, inv_two, gain_all[1])
    bias_five_part = jnp.sum(d_pre_two, axis=0)
    d_ffn = d_pre_two.astype(BF16)
    d_act = ein("rn,ynf->yrf", d_ffn, d_all)
    d_pre_act = d_act * slope.astype(F32)
    ffn_bias_part = jnp.sum(d_pre_act, axis=1).reshape(-1, width)
    d_pre_low = d_pre_act.astype(BF16)
    d_middle = d_pre_two + ein("yrf,ydf->rd", d_pre_low, i_all)
    gain_one_part = jnp.sum(d_middle * unit_one, axis=0)
    shift_one_part = jnp.sum(d_middle, axis=0)
    d_pre_one = norm_back(d_middle, unit_one, inv_one, gain_all[0])
    bias_three_part = jnp.sum(d_pre_one, axis=0)
    d_attn = d_pre_one.astype(BF16)
    d_mix = ein("rn,ynk->yrk", d_attn, o_all).astype(BF16)
    zero_row = jnp.zeros((width,), F32)
    sums = [bias_three_part, shift_one_part, bias_five_part, shift_two_part, gain_one_part, gain_two_part]

    def pad_rows(a):
        return jnp.pad(a, ((0, -a.shape[0] % 8), (0, 0)))

    if fast:
        small = jnp.concatenate([jnp.zeros((dp + 2, width), F32), jnp.stack(sums), ffn_bias_part], axis=0)
        v_sum, o_sum, i_sum, d_sum, d_near, d_far, small = backward(
            d_ffn, middle_low, d_attn, hidden_act, d_pre_low, d_mix, qkv.reshape(mp, own_rows, -1),
            embed_low.reshape(v_raw.shape[:4] + (width,)), v_raw, mixed_far, mixed_heads, stats, segments, seg_col,
            pad_rows(small),
        )
        d_own = (d_near.astype(F32) + d_far.astype(F32)).reshape(own_rows, width)
        qkv_grad = v_sum.reshape(2, rows, 3, -1).transpose(2, 1, 0, 3).reshape(3, rows, cols)
    else:
        embed_low = embed_low.reshape(length, width)
        mixed_heads = mixed_heads.reshape(length, cols)
        down_grad = ein("rn,yrf->ynf", d_ffn, hidden_act).astype(BF16)
        in_grad = ein("rd,yrf->ydf", middle_low, d_pre_low).astype(BF16)
        out_grad_t = ein("rn,yrk->ynk", d_attn, mixed).astype(BF16)
        d_mixed = lax.all_to_all(d_mix, "mp", 0, 0, tiled=True).reshape(length, cols)
        d_q, d_k, d_v = attend_back(qkv, d_mixed, mixed_heads, stats, segments)
        d_qkv = jnp.concatenate([d_q, d_k, d_v], axis=1).astype(BF16)
        v_grad = dg(embed_low, d_qkv, 0, 0).astype(BF16)
        d_embed = dg(d_qkv, qkv_w, 1, 1)
        time_part = bias_three_part + jnp.sum(d_embed, axis=0)
        d_embed = d_embed.astype(BF16).reshape(mp, own_rows, width)
        seq_rows = jnp.where(jnp.arange(dp)[:, None] == dp_index, time_part[None, :], 0.0)
        spread = [lax.dynamic_update_slice_in_dim(zero_row, jnp.sum(a, axis=0), column, 0) for a in (d_q, d_v)]
        small = pad_rows(jnp.concatenate([seq_rows, jnp.stack(spread + sums), ffn_bias_part], axis=0))
        v_sum = lax.psum_scatter(v_grad, "dp", scatter_dimension=0, tiled=True).astype(F32)

        def both(a):
            a = lax.psum_scatter(a, "mp", scatter_dimension=0)
            return lax.psum_scatter(a, "dp", scatter_dimension=0, tiled=True).astype(F32)

        o_sum, i_sum, d_sum = both(out_grad_t), both(in_grad), both(down_grad)
        d_own = lax.psum_scatter(d_embed, "mp", scatter_dimension=0).astype(F32)
        small = lax.psum(small, ("dp", "mp"))
        qkv_grad = v_sum.reshape(rows, 3, cols).transpose(1, 0, 2)

    input_grad = d_pre_one + d_own
    d_time = small[:dp]
    start = dp_index * rows
    features = few[:, :width]
    features = lax.dynamic_slice_in_dim(features, start, rows, axis=1)
    time_grad = lax.dot_general(
        features, d_time, (((0,), (0,)), ((), ())), precision=lax.Precision.HIGHEST
    )
    tail = small[dp:]
    bias_rows = jnp.concatenate([jnp.sum(d_time, axis=0)[None], tail[:6]], axis=0)
    bias_grad = lax.dynamic_slice_in_dim(bias_rows, start, rows, axis=1)
    gain_grad = lax.dynamic_slice_in_dim(tail[6:8], start, rows, axis=1)
    ffn_rows = ffn_bias.shape[0]
    ffn_all = tail[8:].reshape(-1)
    ffn_bias_grad = lax.dynamic_slice_in_dim(ffn_all, dp_index * ffn_rows, ffn_rows)
    return (
        layer_out,
        input_grad,
        time_grad,
        qkv_grad,
        o_sum.T,
        i_sum,
        d_sum.T,
        bias_grad,
        gain_grad,
        ffn_bias_grad,
    )


def solution(mesh):
    dp, mp = mesh.shape["dp"], mesh.shape["mp"]
    placed = (
        P(("dp", "mp"), None),
        P("dp", None),
        P("dp"),
        P("dp", None),
        P(None, "dp", "mp"),
        P("mp", "dp"),
        P("dp", "mp"),
        P("mp", "dp"),
        P(None, "dp"),
        P(None, "dp"),
        P("dp"),
        P(("dp", "mp"), None),
    )
    return jax.shard_map(
        functools.partial(on_device, dp=dp, mp=mp),
        mesh=mesh,
        in_specs=placed,
        out_specs=(
            P(("dp", "mp"), None),
            P(("dp", "mp"), None),
            P("dp", None),
            P(None, "dp", "mp"),
            P("mp", "dp"),
            P("dp", "mp"),
            P("mp", "dp"),
            P(None, "dp"),
            P(None, "dp"),
            P("dp"),
        ),
        check_vma=False,
    )
```

```python
import functools
import math

import jax
import jax.numpy as jnp
from jax import lax
from jax.experimental import pallas as pl
from jax.experimental.pallas import tpu as pltpu
from jax.sharding import PartitionSpec as P

HD = 64
eps = 1e-05
neg_big = -1000000000.0
MESH = pl.DeviceIdType.MESH
F32, BF16 = jnp.float32, jnp.bfloat16
VMEM_LIMIT, VMEM_ALL = 64000000, 67043328


def dg(left, right, left_dim, right_dim):
    return lax.dot_general(
        left, right, (((left_dim,), (right_dim,)), ((), ())), preferred_element_type=F32
    )


class Place:
    def __init__(self):
        i, y = lax.axis_index("dp"), lax.axis_index("mp")
        z, x, c = i // 4, (i // 2) % 2, i % 2
        self.i, self.z, self.x, self.c, self.y = i, z, x, c, y
        self.nx, self.nc, self.ny, self.zero = 1 - x, 1 - c, 1 - y, 0 * i
        low, high = z % 2, z // 2
        flipped = [(1 - 2 * bit) * v + bit for v, bit in ((low, 1), (high, 1))]
        self.zs = [high * 2 + flipped[0], flipped[1] * 2 + low, flipped[1] * 2 + flipped[0]]
        self.to_z = [((p * 2 + x) * 2 + c, y) for p in self.zs]
        self.to_x = ((z * 2 + self.nx) * 2 + c, y)
        self.to_y = (i, self.ny)
        self.to_c = ((z * 2 + x) * 2 + self.nc, y)
        self.count = [self.zero + j for j in range(3)]
        self.dp = [
            (pz * 2 + px) * 2 + pc
            for pz in [z] + self.zs
            for px in (x, self.nx)
            for pc in (c, self.nc)
        ][1:]

    def enter(self, all_dp):
        barrier = pltpu.get_barrier_semaphore()
        near = [self.to_y]
        near += [(p, self.y) for p in self.dp] if all_dp else self.to_z + [self.to_x, self.to_c]
        for one in near:
            pl.semaphore_signal(barrier, inc=1, device_id=one, device_id_type=MESH)
        pl.semaphore_wait(barrier, len(near))


class Wire:
    def __init__(self, at, send_sems, recv_sems):
        self.sems = [(send_sems.at[at.zero + k], recv_sems.at[at.zero + k]) for k in range(send_sems.shape[0])]
        self.used, self.open = 0, []

    def send(self, src, dst, to):
        k = self.used
        self.used += 1
        copy = pltpu.make_async_remote_copy(
            src_ref=src,
            dst_ref=dst,
            send_sem=self.sems[k][0],
            recv_sem=self.sems[k][1],
            device_id=to,
            device_id_type=MESH,
        )
        copy.start()
        self.open.append(copy)
        return copy

    def both(self, copy):
        copy.wait_send()
        self.open = [one for one in self.open if one is not copy]
        copy.wait_recv()

    def close(self):
        assert self.used == len(self.sems), self.used
        for copy in self.open:
            copy.wait_send()


class Local:
    def __init__(self, at, sems):
        self.sems, self.used, self.open = [sems.at[at.zero + k] for k in range(sems.shape[0])], 0, []

    def copy(self, src, dst):
        one = pltpu.make_async_copy(src, dst, self.sems[self.used])
        self.used += 1
        one.start()
        self.open.append(one)
        return one

    def wait(self, one):
        one.wait()
        self.open = [other for other in self.open if other is not one]

    def close(self):
        assert self.used == len(self.sems), self.used
        for one in self.open:
            one.wait()


D_CUTS = ((0.625, True), (0.625, True))
I_CUTS = ((0.625, True), (0.625, True))
O_CUTS = ((0.5, True),)

FORWARD_AFTER = {
    "start": ("v0", "v1", "o", "i0",),
    "few": ("v0", "v1", "o", "i1", "d0", "v0", "o",),
    "part": ("i0", "v1", "i0", "v0",),
    "emb": ("v1", "i1", "o", "d1",),
    "proj": ("i0", "o",),
    "a1": ("d0", "d1", "i1",),
    "a3": ("i1", "d0", "i0",),
    "a6": ("i1", "o",),
    "a7": ("i0", "d0", "o", "i1", "d1", "i0", "d0",),
    "f0": ("d1",),
    "f2": ("i1", "d1",),
    "f4": ("d0",),
    "f6": ("d1",),
    "end": ("d0", "d1",),
}


def cuts_of(width, parts):
    step = width // len(parts)
    return [(k * step, k * step + int(step * first), (k + 1) * step, early) for k, (first, early) in enumerate(parts)]


def gather_dp(wire, at, shard, whole, lo, hi):
    n = pl.ds(lo, hi - lo)
    own = whole.at[at.z, at.x, at.c, :, n]
    from_z = [wire.send(shard.at[:, n], own, to) for to in at.to_z]
    late = [wire.send(shard.at[:, n], own, at.to_c)]
    yield
    for k in from_z:
        k.wait_recv()
    ref = whole.at[:, at.x, at.c, :, n]
    from_x = wire.send(ref, ref, at.to_x)
    for p in at.zs:
        ref = whole.at[p, at.x, at.c, :, n]
        late.append(wire.send(ref, ref, at.to_c))
    yield
    from_x.wait_recv()
    ref = whole.at[:, at.nx, at.c, :, n]
    late.append(wire.send(ref, ref, at.to_c))
    yield
    for k in late:
        k.wait_recv()


def gather_all(wire, at, shard, whole, lo, mid, hi, early):
    a, b, ab = pl.ds(lo, mid - lo), pl.ds(mid, hi - mid), pl.ds(lo, hi - lo)
    y, z, x, c = at.y, at.z, at.x, at.c
    first = a if early else ab
    from_z_a = [wire.send(shard.at[:, first], whole.at[y, z, x, c, :, first], to) for to in at.to_z]
    if early:
        from_y_b = wire.send(shard.at[:, b], whole.at[y, z, x, c, :, b], at.to_y)
    late = [wire.send(shard.at[:, ab], whole.at[y, z, x, c, :, ab], at.to_c)]

    def to_core(*refs):
        for ref in refs:
            late.append(wire.send(ref, ref, at.to_c))

    yield
    if early:
        from_y_b.wait_recv()
        ref = whole.at[:, z, x, c, :, b]
        from_z_b = [wire.send(ref, ref, to) for to in at.to_z]
        to_core(whole.at[at.ny, z, x, c, :, b])
    else:
        for k in from_z_a:
            k.wait_recv()
        ref = whole.at[y, :, x, c, :, b]
        from_y_b = wire.send(ref, ref, at.to_y)
        to_core(*(whole.at[y, p, x, c, :, b] for p in at.zs))
    yield
    if early:
        for k in from_z_a:
            k.wait_recv()
    ref = whole.at[y, :, x, c, :, a]
    from_x_a = wire.send(ref, ref, at.to_x)
    to_core(*(whole.at[y, p, x, c, :, a] for p in at.zs))
    yield
    from_x_a.wait_recv()
    ref = whole.at[y, :, :, c, :, a]
    from_y_a = wire.send(ref, ref, at.to_y)
    to_core(whole.at[y, :, at.nx, c, :, a])
    yield
    if early:
        for k in from_z_b:
            k.wait_recv()
        to_core(*(whole.at[:, p, x, c, :, b] for p in at.zs))
    else:
        from_y_b.wait_recv()
        to_core(whole.at[at.ny, :, x, c, :, b])
    ref = whole.at[:, :, x, c, :, b]
    from_x_b = wire.send(ref, ref, at.to_x)
    yield
    from_y_a.wait_recv()
    from_x_b.wait_recv()
    to_core(whole.at[at.ny, :, :, c, :, a], whole.at[:, :, at.nx, c, :, b])
    yield
    for k in late:
        k.wait_recv()


def one_hot_rows(count, width, start):
    down = lax.broadcasted_iota(jnp.int32, (count, width), 0)
    across = lax.broadcasted_iota(jnp.int32, (count, width), 1)
    return jnp.where(down == across + start, 1.0, 0.0).astype(BF16)


def forward_kernel(
    v_ref, t_ref, f_ref, b_ref, o_ref, i_ref, d_ref, h_ref, sr_ref, sc_ref,
    v_out, o_out, i_out, d_all, few_out, par_out, time_out, embed_out, qkv_out, mine_out, far_out,
    stats_out, unit_out, inv_out, mid_out, act_out, slope_out,
    v_all, o_all, i_all, few, part, got, h_far, par, ffn_b, embed, qkv, mine, far, stats, unit, inv,
    mid, act, slope, send_sems, recv_sems, local_sems, tile_sems,
):
    at = Place()
    y, z, x, c = at.y, at.z, at.x, at.c
    at.enter(True)
    wire, local = Wire(at, send_sems, recv_sems), Local(at, local_sems)
    width = h_ref.shape[1]
    own_rows = h_ref.shape[0]
    rows = v_ref.shape[0]
    cols = o_ref.shape[1]
    hidden = i_ref.shape[1]
    length = 2 * own_rows

    from_few = [wire.send(f_ref, few.at[at.i], (p, y)) for p in at.dp]
    from_h = wire.send(h_ref, h_far, at.to_y)
    v_mid = 7 * 128
    streams = {
        "v0": gather_dp(wire, at, v_ref, v_all, 0, v_mid),
        "v1": gather_dp(wire, at, v_ref, v_all, v_mid, v_ref.shape[1]),
    }
    for name, shard, whole, parts in (("d", d_ref, d_all, D_CUTS), ("i", i_ref, i_all, I_CUTS), ("o", o_ref, o_all, O_CUTS)):
        for k, cut in enumerate(cuts_of(shard.shape[1], parts)):
            streams[name + str(k)] = gather_all(wire, at, shard, whole, *cut)
    streams["o"] = streams["o0"]
    begun = set()

    kept = [
        local.copy(v_ref, v_all.at[z, x, c]),
        local.copy(o_ref, o_all.at[y, z, x, c]),
        local.copy(i_ref, i_all.at[y, z, x, c]),
        local.copy(d_ref, d_all.at[y, z, x, c]),
    ]

    def run(step):
        for name in FORWARD_AFTER.get(step, ()):
            if name in begun:
                while kept:
                    local.wait(kept.pop())
            begun.add(name)
            next(streams[name], None)

    run("start")
    few[at.i] = f_ref[...]
    for k in from_few:
        k.wait_recv()
    seqs = few.shape[0]
    table = jnp.concatenate([few[s] for s in range(seqs)], axis=0)
    pick = one_hot_rows(width, rows, at.i * rows)
    feats = dg(table[:, :width].astype(BF16), pick, 1, 0).astype(BF16)
    partial = dg(feats, t_ref[...], 1, 0) + dg(b_ref[...], pick, 1, 1)
    for s in range(seqs):
        part[s] = partial[s : s + 1]
    ffn_b[...] = jnp.concatenate([few[s][:, width:] for s in range(seqs)], axis=1)
    local.copy(few, few_out)
    from_part = [wire.send(part.at[p], got.at[j], (p, y)) for j, p in enumerate(at.dp)]
    run("few")
    for k in from_part:
        k.wait_recv()
    total = part[at.i]
    for j in range(seqs - 1):
        total = total + got[j]
    time_out[...] = total
    run("part")

    from_h.wait_recv()
    step = 128

    def embed_rows(t, _):
        r = pl.ds(pl.multiple_of(t * step, step), step)
        embed[y, r] = (h_ref[r].astype(F32) + total).astype(BF16)
        embed[at.ny, r] = (h_far[r].astype(F32) + total).astype(BF16)
        return 0

    lax.fori_loop(0, own_rows // step, embed_rows, 0)
    local.copy(embed, embed_out)
    run("emb")
    local.copy(v_all, v_out)
    run("vdone")
    par[...] = v_all[:, :, :, :, 3 * cols :].reshape(width, 128).astype(F32).T
    local.copy(par, par_out)
    heads = pl.ds(pl.multiple_of(y * cols, cols), cols)
    bias_q, bias_v = par[1:2, heads], par[2:3, heads]

    step_q = 256

    def project(t, _):
        half, r = t // (own_rows // step_q), pl.ds(pl.multiple_of((t % (own_rows // step_q)) * step_q, step_q), step_q)
        whole_r = pl.ds(pl.multiple_of(t * step_q, step_q), step_q)
        left = embed[half, r]
        for j, bias in enumerate((bias_q, None, bias_v)):
            n = slice(j * cols, (j + 1) * cols)
            made = dg(left, v_all[:, :, :, :, n].reshape(width, cols), 1, 0)
            qkv[whole_r, n] = (made if bias is None else made + bias).astype(BF16)
        return 0

    lax.fori_loop(0, length // step_q, project, 0)
    local.copy(qkv, qkv_out)
    run("proj")

    pair, tile = 2 * HD, own_rows
    from_far = []

    def give(p):
        n = pl.ds(p * pair, pair)
        from_far.append(wire.send(mine.at[at.ny, :, n], far.at[:, n], at.to_y))

    def tick_of(t):
        if t % 2:
            give(t // 2)
        run("a" + str(t))

    ticks = {t: lambda t=t: tick_of(t) for t in range(8) if t % 2 or "a" + str(t) in FORWARD_AFTER}

    def attend_step(t, _):
        p, half = t // 2, t % 2
        r = pl.ds(pl.multiple_of(half * tile, tile), tile)
        n = pl.multiple_of(p * pair, pair)
        queries = qkv[r, pl.ds(n, pair)]
        keys = qkv[:, pl.ds(cols + n, pair)]
        values = qkv[:, pl.ds(2 * cols + n, pair)]
        same = sc_ref[:, 0:1] == sr_ref[:, r]
        made = []
        for h in range(2):
            k = slice(h * HD, h * HD + HD)
            scores = dg(keys[:, k], queries[:, k], 1, 1) * (1.0 / math.sqrt(HD))
            scores = jnp.where(same, scores, neg_big)
            row_max = jnp.max(scores, axis=0, keepdims=True)
            prob = jnp.exp(scores - row_max)
            row_total = jnp.sum(prob, axis=0, keepdims=True)
            made.append((dg(values[:, k], prob.astype(BF16), 0, 0) / row_total).T)
            stats[p, h : h + 1, r] = row_max + jnp.log(row_total)
        mine[half, :, pl.ds(n, pair)] = jnp.concatenate(made, axis=1).astype(BF16)
        for k, tick in ticks.items():
            pl.when(t == k)(lambda tick=tick: (tick(), None)[1])
        return 0

    lax.fori_loop(0, 2 * (cols // pair), attend_step, 0)
    local.copy(mine, mine_out)
    local.copy(stats, stats_out)
    local.copy(o_all, o_out)

    for k in from_far:
        k.wait_recv()
    local.copy(far, far_out)

    def project_out(t, _):
        r = pl.ds(pl.multiple_of(t * step_q, step_q), step_q)
        total_r = dg(mine[y, r], o_all[y].reshape(width, cols), 1, 1)
        total_r += dg(far[r], o_all[at.ny].reshape(width, cols), 1, 1)
        total_r += h_ref[r].astype(F32) + total + par[3:4]
        made, inv_std = normalize(total_r)
        unit[r] = made
        inv[r] = jnp.broadcast_to(inv_std, (step_q, 128))
        mid[r] = (made * par[7:8] + par[4:5]).astype(BF16)
        return 0

    lax.fori_loop(0, own_rows // step_q, project_out, 0)
    local.copy(unit, unit_out)
    local.copy(inv, inv_out)
    local.copy(mid, mid_out)
    run("out")

    chunk = 512
    later = {t: lambda t=t: run("f" + str(t)) for t in range(8) if "f" + str(t) in FORWARD_AFTER}

    def feed_step(t, _):
        side = t % 2
        n = pl.multiple_of((t // 2) * chunk, chunk)
        made = dg(mid[...], i_all[side, :, :, :, :, pl.ds(n, chunk)].reshape(width, chunk), 1, 0)
        made = made + ffn_b[:, pl.ds(pl.multiple_of(side * hidden, hidden) + n, chunk)]
        below = 0.5 + 0.5 * lax.erf(made * math.sqrt(0.5))
        act[side, :, pl.ds(n, chunk)] = (made * below).astype(BF16)
        bell = jnp.exp(-0.5 * made * made) * (1.0 / math.sqrt(2.0 * math.pi))
        slope[side, :, pl.ds(n, chunk)] = (below + made * bell).astype(BF16)
        pltpu.make_async_copy(
            act.at[side, :, pl.ds(n, chunk)], act_out.at[side, :, pl.ds(n, chunk)], tile_sems.at[0, t]
        ).start()
        pltpu.make_async_copy(
            slope.at[side, :, pl.ds(n, chunk)], slope_out.at[side, :, pl.ds(n, chunk)], tile_sems.at[1, t]
        ).start()
        for k, tick in later.items():
            pl.when(t == k)(lambda tick=tick: (tick(), None)[1])
        return 0

    tiles = 2 * hidden // chunk
    lax.fori_loop(0, tiles, feed_step, 0)
    local.copy(i_all, i_out)
    run("end")
    for t in range(tiles):
        n = pl.ds(0, chunk)
        pltpu.make_async_copy(act.at[0, :, n], act_out.at[0, :, n], tile_sems.at[0, t]).wait()
        pltpu.make_async_copy(slope.at[0, :, n], slope_out.at[0, :, n], tile_sems.at[1, t]).wait()
    local.close()
    wire.close()


def forward(v, t, few_row, bias_zero, o, i, d, h, seg_row, seg_col):
    rows, cols, hidden = v.shape[0], o.shape[1], i.shape[1]
    own_rows, width = h.shape
    length = 2 * own_rows
    pairs = cols // (2 * HD)
    S = jax.ShapeDtypeStruct
    dp3 = (4, 2, 2)
    v_all, o_all, i_all = S(dp3 + v.shape, BF16), S((2,) + dp3 + o.shape, BF16), S((2,) + dp3 + i.shape, BF16)
    few = S((16,) + few_row.shape, F32)
    par, time_row = S((128, width), F32), S((1, width), F32)
    embed, qkv = S((2, own_rows, width), BF16), S((length, 3 * cols), BF16)
    mine, far = S((2, own_rows, cols), BF16), S((own_rows, cols), BF16)
    stats = S((pairs, 2, length), F32)
    unit, inv, mid = S((own_rows, width), F32), S((own_rows, 128), F32), S((own_rows, width), BF16)
    act = S((2, own_rows, hidden), BF16)
    outs = [v_all, o_all, i_all, i_all, few, par, time_row, embed, qkv, mine, far, stats, unit, inv, mid, act, act]
    vm, hbm = pl.BlockSpec(memory_space=pltpu.VMEM), pl.BlockSpec(memory_space=pl.ANY)
    out_specs = [hbm] * len(outs)
    out_specs[6] = vm
    part, got = S((16, 1, width), F32), S((15, 1, width), F32)
    h_far, ffn_b = S(h.shape, BF16), S((1, 2 * hidden), F32)
    scratch = [v_all, o_all, i_all, few, part, got, h_far, par, ffn_b, embed, qkv, mine, far, stats, unit, inv, mid, act, act]
    copies = 15 + 15 + 1 + 2 * 9 + sum(21 if early else 18 for _, early in D_CUTS + I_CUTS + O_CUTS) + pairs
    return pl.pallas_call(
        forward_kernel,
        name="forward",
        out_shape=outs,
        in_specs=[vm] * 10,
        out_specs=out_specs,
        scratch_shapes=[pltpu.VMEM(a.shape, a.dtype) for a in scratch]
        + [
            pltpu.SemaphoreType.DMA((copies,)),
            pltpu.SemaphoreType.DMA((copies,)),
            pltpu.SemaphoreType.DMA((FORWARD_LOCAL,)),
            pltpu.SemaphoreType.DMA((2, 2 * hidden // 512)),
        ],
        compiler_params=pltpu.CompilerParams(
            collective_id=0, has_side_effects=True, vmem_limit_bytes=VMEM_LIMIT
        ),
    )(v, t, few_row, bias_zero, o, i, d, h, seg_row, seg_col)


FORWARD_LOCAL = 17


def add_blocks(dst, left, right, lead):
    count = math.prod(lead)

    def one(t, _):
        at = []
        for n in reversed(lead):
            at.append(t % n)
            t = t // n
        at = tuple(reversed(at))
        dst[at] = (left[at].astype(F32) + right[at].astype(F32)).astype(dst.dtype)
        return 0

    lax.fori_loop(0, count, one, 0)


def reduce_dp(wire, at, grad, rc, rx, rz, out):
    z, x, c, y = at.z, at.x, at.c, at.y
    from_c = wire.send(grad.at[:, :, at.nc], rc, at.to_c)
    yield
    wire.both(from_c)
    add_blocks(rc, grad.at[:, :, c], rc, (4, 2))
    from_x = wire.send(rc.at[:, at.nx], rx, at.to_x)
    yield
    from_x.wait_recv()
    add_blocks(rx, rc.at[:, x], rx, (4,))
    from_z = [wire.send(rx.at[p], rz.at[at.count[j]], to) for j, (p, to) in enumerate(zip(at.zs, at.to_z))]
    yield
    for k in from_z:
        k.wait_recv()
    out[...] = ((rx[z].astype(F32) + rz[0].astype(F32)) + rz[1].astype(F32)) + rz[2].astype(F32)


def reduce_all(wire, at, grad, bufs, out, lo, mid, hi, early):
    rc, ya, xb, xa, za, zb, yb, zs = bufs
    z, x, c, y = at.z, at.x, at.c, at.y
    a, b, ab = pl.ds(lo, mid - lo), pl.ds(mid, hi - mid), pl.ds(lo, hi - lo)
    half_a, half_b = pl.ds(0, mid - lo), pl.ds(mid - lo, hi - mid)

    def over_z(pick, got):
        return [wire.send(pick(p), got.at[at.count[j]], to) for j, (p, to) in enumerate(zip(at.zs, at.to_z))]

    def add_z(own, got):
        return ((own.astype(F32) + got[0].astype(F32)) + got[1].astype(F32)) + got[2].astype(F32)

    from_c = wire.send(grad.at[:, :, :, at.nc, :, ab], rc, at.to_c)
    yield
    wire.both(from_c)
    add_blocks(rc, grad.at[:, :, :, c, :, ab], rc, (2, 4, 2))
    from_y_a = wire.send(rc.at[at.ny, :, :, :, half_a], ya, at.to_y)
    from_x_b = wire.send(rc.at[:, :, at.nx, :, half_b], xb, at.to_x)
    yield
    from_y_a.wait_recv()
    add_blocks(ya, rc.at[y, :, :, :, half_a], ya, (4, 2))
    from_x_a = wire.send(ya.at[:, at.nx], xa, at.to_x)
    yield
    from_x_b.wait_recv()
    add_blocks(xb, rc.at[:, :, x, :, half_b], xb, (2, 4))
    if early:
        from_z_b = over_z(lambda p: xb.at[:, p], zb)
    else:
        from_y_b = wire.send(xb.at[at.ny], yb, at.to_y)
    yield
    from_x_a.wait_recv()
    add_blocks(xa, ya.at[:, x], xa, (4,))
    from_z_a = over_z(lambda p: xa.at[p], za)
    yield
    if early:
        for k in from_z_b:
            k.wait_recv()
        zs[...] = add_z(xb[:, z], zb).astype(BF16)
        from_y_b = wire.send(zs.at[at.ny], yb, at.to_y)
    else:
        from_y_b.wait_recv()
        add_blocks(yb, xb.at[y], yb, (4,))
        from_z_b = over_z(lambda p: yb.at[p], zb)
    yield
    for k in from_z_a:
        k.wait_recv()
    out[:, a] = add_z(xa[z], za)
    if early:
        from_y_b.wait_recv()
        out[:, b] = zs[y].astype(F32) + yb[...].astype(F32)
    else:
        for k in from_z_b:
            k.wait_recv()
        out[:, b] = add_z(yb[z], zb)


def reduce_bufs(rows, lo, mid, hi, early):
    ha, hb = mid - lo, hi - mid
    last = [(3, 2, rows, hb), (rows, hb), (2, rows, hb)] if early else [(3, rows, hb), (4, rows, hb), (8, 128)]
    return [(2, 4, 2, rows, hi - lo), (4, 2, rows, ha), (2, 4, rows, hb), (4, rows, ha), (3, rows, ha)] + last


def reduce_small(wire, at, mine, sums, got, out):
    k = wire.send(mine, got.at[0], at.to_c)
    yield
    k.wait_recv()
    sums[0] = mine[...] + got[0]
    k = wire.send(sums.at[0], got.at[1], at.to_x)
    yield
    k.wait_recv()
    sums[1] = sums[0] + got[1]
    k = wire.send(sums.at[1], got.at[2], at.to_y)
    yield
    k.wait_recv()
    sums[2] = sums[1] + got[2]
    last = [wire.send(sums.at[2], got.at[3 + j], to) for j, to in enumerate(at.to_z)]
    yield
    for k in last:
        k.wait_recv()
    out[...] = ((sums[2] + got[3]) + got[4]) + got[5]


D_PARTS = ((0.75, True), (0.5, True), (0.75, True), (0.5, True))
I_PARTS = ((0.75, True), (0.5, True), (0.5, False), (0.75, False))
O_PARTS = ((0.5, False),)

AFTER = {
    "pd0": ("d0",),
    "pd2": ("d1",),
    "pd3": ("d3", "d0",),
    "pi0": ("d1",),
    "pi1": ("i0",),
    "pi2": ("d2", "d3", "i1",),
    "pi3": ("d0",),
    "po": ("d1", "d2", "d1", "i3",),
    "emb": ("d0", "i2", "d0", "i1",),
    "a0": ("d3", "i0", "d3",),
    "a1": ("d2", "d1", "i2", "o", "d2",),
    "a2": ("i1",),
    "a3": ("d3", "i1",),
    "vp0": ("i0", "i0", "o", "d2",),
    "a4": ("i2", "i1", "i3",),
    "a5": ("o", "i2",),
    "a6": ("i0",),
    "a7": ("i2",),
    "vp1": ("v0", "v1", "i3", "o", "i3", "i2",),
    "e0": ("o", "v0", "o", "i3",),
    "e1": ("t", "i0", "v1", "i3", "v0", "t", "v1", "i3", "t", "i2", "t", "v1", "i1", "o", "d3", "d1", "d2", "d2", "d1", "d3", "v0", "i1", "d0", "d0", "i0", "t",),
}


def turn_rows(src, dst):
    def one(t, _):
        r = pl.ds(pl.multiple_of(t * 128, 128), 128)
        dst[r, :] = src[:, r].astype(F32).T.astype(BF16)
        return 0

    lax.fori_loop(0, src.shape[1] // 128, one, 0)


def backward_kernel(
    ffn_ref, mid_ref, attn_ref, act_ref, pre_ref, mix_ref, qkv_ref, embed_ref, v_ref,
    far_ref, mine_ref, stats_ref, sr_ref, sc_ref, small_ref,
    v_out, o_out, i_out, d_out, x_own, x_got, s_out, *rest,
):
    at = Place()
    y = at.y
    at.enter(False)
    rest = iter(rest)
    wire, local = Wire(at, next(rest), next(rest)), Local(at, next(rest))
    raw, tr, big, d_heads, d_g, i_g, o_g, v_g, acc_k, acc_v, table, sums, got = (next(rest) for _ in range(13))
    own_rows, width = raw.shape
    hidden, cols, length = big.shape[2], d_heads.shape[2], 2 * own_rows

    streams = {}
    for name, grad, out, parts in (("d", d_g, d_out, D_PARTS), ("i", i_g, i_out, I_PARTS), ("o", o_g, o_out, O_PARTS)):
        for k, cut in enumerate(cuts_of(out.shape[1], parts)):
            bufs = [next(rest) for _ in range(8)]
            streams[name + str(k)] = reduce_all(wire, at, grad, bufs, out, *cut)
    streams["o"] = streams["o0"]
    for k in range(2):
        bufs = [next(rest) for _ in range(3)]
        streams["v" + str(k)] = reduce_dp(wire, at, v_g.at[at.count[k]], *bufs, v_out.at[at.count[k]])
    streams["t"] = reduce_small(wire, at, table, sums, got, s_out)

    def run(step):
        for name in AFTER.get(step, ()):
            next(streams[name], None)

    done = local.wait

    from_mix = wire.send(mix_ref.at[at.ny], d_heads.at[y], at.to_y)
    chunk = 512
    pieces = [pl.ds(lo, chunk) for lo in range(0, hidden, chunk)]
    raw_in = local.copy(ffn_ref, raw)
    act_in = [local.copy(act_ref.at[:, :, n], big.at[:, :, n]) for n in pieces]
    pre_in = []
    mix_in = local.copy(mix_ref.at[y], d_heads.at[y])
    table[...] = small_ref[...]
    done(raw_in)
    turn_rows(raw, tr.at[0])
    raw_in = local.copy(mid_ref, raw)

    def products(left, grad, arrived, after):
        steps = {2 * k + 1: (lambda k=k: after(k)) for k in range(len(pieces))}

        def one(t, _):
            n = pl.ds(pl.multiple_of((t // 2) * chunk, chunk), chunk)
            made = dg(left[...], big[t % 2, :, n], 1, 0).astype(BF16)
            grad[t % 2, :, :, :, :, n] = made.reshape(grad.shape[1:5] + (chunk,))
            for k, step in steps.items():
                pl.when(t == k)(lambda step=step: (step(), None)[1])
            return 0

        done(arrived[0])
        lax.fori_loop(0, 2 * len(pieces), one, 0)

    def after_down(k):
        pre_in.append(local.copy(pre_ref.at[:, :, pieces[k]], big.at[:, :, pieces[k]]))
        run("pd" + str(k))
        if k + 1 < len(pieces):
            done(act_in[k + 1])

    def after_in(k):
        run("pi" + str(k))
        if k + 1 < len(pieces):
            done(pre_in[k + 1])

    products(tr.at[0], d_g, act_in, after_down)
    done(raw_in)
    turn_rows(raw, tr.at[1])
    raw_in = local.copy(attn_ref, raw)
    products(tr.at[1], i_g, pre_in, after_in)
    qkv_in = local.copy(qkv_ref, big.at[:, :, 0 : 3 * cols])
    done(raw_in)
    turn_rows(raw, tr.at[0])
    for side, right in ((y, mine_ref.at[y]), (at.ny, far_ref)):
        made = dg(tr[0], right[...], 1, 0).astype(BF16)
        o_g[side] = made.reshape(o_g.shape[1:])
    run("po")

    embed_in = local.copy(embed_ref, d_g.at[0, :, :, :, :, 0:width])
    v_in = local.copy(v_ref, d_g.at[1, :, :, :, :, 0 : v_ref.shape[4]])
    done(embed_in)

    def turn_embed(t, _):
        n = pl.ds(pl.multiple_of(t * 128, 128), 128)
        block = d_g[0, :, :, :, :, n].reshape(length, 128)
        d_g[0, t // 2, t % 2, :, :, width : 2 * width] = (
            block.astype(F32).T.astype(BF16).reshape(d_g.shape[3:5] + (length,))
        )
        return 0

    lax.fori_loop(0, width // 128, turn_embed, 0)
    done(v_in)
    done(qkv_in)
    done(mix_in)
    from_mix.wait_recv()
    run("emb")

    part_cols = cols // 2

    def project_grad(k):
        def one(j, _):
            n = pl.ds(pl.multiple_of(j * cols + k * part_cols, part_cols), part_cols)
            made = dg(
                d_g[0, :, :, :, :, width : 2 * width].reshape(width, length),
                big[:, :, n].reshape(length, part_cols), 1, 0,
            ).astype(BF16)
            v_g[k, :, :, :, :, pl.ds(pl.multiple_of(j * part_cols, part_cols), part_cols)] = made.reshape(
                v_g.shape[1:5] + (part_cols,)
            )
            return 0

        lax.fori_loop(0, 3, one, 0)

    pair = 2 * HD
    scale = 1.0 / math.sqrt(HD)
    def tick_of(t):
        run("a" + str(t))
        if t % 4 == 3:
            run("vp" + str(t // 4))

    ticks = {t: lambda t=t: tick_of(t) for t in range(8)}

    def attend_step(t, _):
        p, half = t // 2, t % 2
        n = pl.multiple_of(p * pair, pair)
        r = pl.ds(pl.multiple_of(half * own_rows, own_rows), own_rows)
        cq, ck, cv = pl.ds(n, pair), pl.ds(cols + n, pair), pl.ds(2 * cols + n, pair)
        same = sc_ref[:, 0:1] == sr_ref[:, r]
        queries = big[half, :, cq]
        keys, values = big[:, :, ck].reshape(length, pair), big[:, :, cv].reshape(length, pair)
        d_rows, o_rows = d_heads[half, :, cq], mine_ref[half, :, cq]
        here = pl.ds(pl.multiple_of(y * cols + n, pair), pair)
        d_q, d_k, d_v = [], [], []
        for h in range(2):
            k = slice(h * HD, h * HD + HD)
            delta = jnp.sum((d_rows[:, k].astype(F32) * o_rows[:, k].astype(F32)).T, axis=0, keepdims=True)
            scores = dg(keys[:, k], queries[:, k], 1, 1) * scale
            prob = jnp.where(same, jnp.exp(scores - stats_ref[p, h : h + 1, r]), 0.0)
            d_prob = dg(values[:, k], d_rows[:, k], 1, 1)
            d_score = (prob * (d_prob - delta) * scale).astype(BF16)
            d_v.append(dg(prob.astype(BF16), d_rows[:, k], 1, 0))
            d_k.append(dg(d_score, queries[:, k], 1, 0))
            d_q.append(dg(d_score, keys[:, k], 0, 0))
        d_q, d_k, d_v = (jnp.concatenate(a, axis=1) for a in (d_q, d_k, d_v))
        big[half, :, cq] = d_q.astype(BF16)
        table[16:17, here] += jnp.sum(d_q, axis=0, keepdims=True)
        table[17:18, here] += jnp.sum(d_v, axis=0, keepdims=True)

        @pl.when(half == 0)
        def _():
            acc_k[...] = d_k
            acc_v[...] = d_v

        @pl.when(half == 1)
        def _():
            big[:, :, ck] = (acc_k[...] + d_k).astype(BF16).reshape(2, own_rows, pair)
            big[:, :, cv] = (acc_v[...] + d_v).astype(BF16).reshape(2, own_rows, pair)

        pl.when(t % 4 == 3)(lambda: project_grad(t // 4))
        for k, tick in ticks.items():
            pl.when(t == k)(lambda tick=tick: (tick(), None)[1])
        return 0

    lax.fori_loop(0, 2 * (cols // pair), attend_step, 0)

    step = 256
    per_half = own_rows // step

    def rows_of(half):
        return i_g.at[at.zero, pl.ds(2 * half, 2), :, :, :, 0:width]

    def embed_grad(t, acc):
        half = (at.ny + t // per_half) % 2
        r = pl.ds(pl.multiple_of((t % per_half) * step, step), step)
        made = dg(
            big[half, r, 0 : 3 * cols],
            d_g[1, :, :, :, :, 0 : 3 * cols].reshape(width, 3 * cols), 1, 1,
        )
        i_g[0, 2 * half + t % per_half, :, :, :, 0:width] = made.astype(BF16).reshape(i_g.shape[2:5] + (width,))

        @pl.when(t == per_half - 1)
        def _():
            from_x.append(wire.send(far_rows, x_got, at.to_y))
            run("e0")

        return acc + jnp.sum(made, axis=0, keepdims=True)

    from_x, far_rows = [], rows_of(at.ny)
    total = lax.fori_loop(0, 2 * per_half, embed_grad, table[18:19])
    local.copy(rows_of(y), x_own)
    down = lax.broadcasted_iota(jnp.int32, (16, width), 0)
    table[0:16] = jnp.where(down == at.i, total, 0.0)
    run("e1")
    from_x[0].wait_recv()
    local.close()
    wire.close()


def backward(d_ffn, mid, d_attn, act, d_pre, d_mix, qkv, embed, v_all, far, mine, stats, seg_row, seg_col, small):
    own_rows, width = mid.shape
    hidden, cols, rows = act.shape[2], far.shape[1], v_all.shape[3]
    dp3 = (4, 2, 2)
    S = jax.ShapeDtypeStruct
    x_part = S((2, 2, 2, rows, width), BF16)
    outs = [
        S((2, rows, 3 * cols // 2), F32), S((rows, cols), F32), S((rows, hidden), F32), S((rows, hidden), F32),
        x_part, x_part, S(small.shape, F32),
    ]
    wide = S((2,) + dp3 + (rows, hidden), BF16)
    acc = S((2 * own_rows, 2 * HD), F32)
    scratch = [
        S((own_rows, width), BF16), S((2, width, own_rows), BF16), S((2, own_rows, hidden), BF16),
        S((2, own_rows, cols), BF16), wide, wide, S((2,) + dp3 + (rows, cols), BF16),
        S((2,) + dp3 + (rows, 3 * cols // 2), BF16), acc, acc,
        S(small.shape, F32), S((3,) + small.shape, F32), S((6,) + small.shape, F32),
    ]
    copies = 1 + 1 + 6
    for n, parts in ((hidden, D_PARTS), (hidden, I_PARTS), (cols, O_PARTS)):
        for cut in cuts_of(n, parts):
            copies += 11
            scratch += [S(a, BF16) for a in reduce_bufs(rows, *cut)]
    for n in [3 * cols // 2] * 2:
        copies += 5
        scratch += [S(s, BF16) for s in ((4, 2, rows, n), (4, rows, n), (3, rows, n))]
    vm, hbm = pl.BlockSpec(memory_space=pltpu.VMEM), pl.BlockSpec(memory_space=pl.ANY)
    return pl.pallas_call(
        backward_kernel,
        name="backward",
        out_shape=outs,
        in_specs=[hbm] * 9 + [vm] * 6,
        out_specs=[vm] * 4 + [hbm] * 2 + [vm],
        scratch_shapes=[
            pltpu.SemaphoreType.DMA((copies,)), pltpu.SemaphoreType.DMA((copies,)),
            pltpu.SemaphoreType.DMA((BACKWARD_LOCAL,)),
        ]
        + [pltpu.VMEM(a.shape, a.dtype) for a in scratch],
        compiler_params=pltpu.CompilerParams(
            collective_id=1, has_side_effects=True, vmem_limit_bytes=VMEM_ALL
        ),
    )(d_ffn, mid, d_attn, act, d_pre, d_mix, qkv, embed, v_all, far, mine, stats, seg_row, seg_col, small)


BACKWARD_LOCAL = 16


def attend_kernel(tile, q_ref, k_ref, v_ref, sr_ref, sc_ref, o_ref, l_ref):
    length, width = q_ref.shape

    def step(t, _):
        rows = pl.ds(pl.multiple_of(t * tile, tile), tile)
        same = sc_ref[:, 0:1] == sr_ref[:, rows]
        for h in range(width // HD):
            cols = slice(h * HD, h * HD + HD)
            scores = dg(k_ref[:, cols], q_ref[rows, cols], 1, 1) * (1.0 / math.sqrt(HD))
            scores = jnp.where(same, scores, neg_big)
            row_max = jnp.max(scores, axis=0, keepdims=True)
            prob = jnp.exp(scores - row_max)
            total = jnp.sum(prob, axis=0, keepdims=True)
            mixed = dg(v_ref[:, cols], prob.astype(BF16), 0, 0) / total
            o_ref[rows, cols] = mixed.T.astype(BF16)
            l_ref[0, h : h + 1, rows] = row_max + jnp.log(total)
        return 0

    lax.fori_loop(0, length // tile, step, 0)


def attend_specs(length, heads_pairs):
    def col(k):
        return pl.BlockSpec((length, 2 * HD), lambda i, k=k: (0, k * heads_pairs + i))

    stats = pl.BlockSpec((1, 2, length), lambda i: (i, 0, 0))
    seg_row = pl.BlockSpec((1, length), lambda i: (0, 0))
    seg_col = pl.BlockSpec((length, 128), lambda i: (0, 0))
    return col, stats, seg_row, seg_col


def attend(qkv, segments):
    length = qkv.shape[0]
    pairs = qkv.shape[1] // 3 // (2 * HD)
    col, stats, seg_row, seg_col = attend_specs(length, pairs)
    return pl.pallas_call(
        functools.partial(attend_kernel, min(512, length)),
        name="attend",
        grid=(pairs,),
        in_specs=[col(0), col(1), col(2), seg_row, seg_col],
        out_specs=[col(0), stats],
        out_shape=[
            jax.ShapeDtypeStruct((length, pairs * 2 * HD), BF16),
            jax.ShapeDtypeStruct((pairs, 2, length), F32),
        ],
        cost_estimate=pl.CostEstimate(
            flops=8 * length * length * HD * pairs, bytes_accessed=4 * length * pairs * 256, transcendentals=0
        ),
    )(qkv, qkv, qkv, segments, jnp.broadcast_to(segments.reshape(length, 1), (length, 128)))


def attend_back_kernel(
    tile, q_ref, k_ref, v_ref, d_ref, o_ref, l_ref, sr_ref, sc_ref, dq_ref, dk_ref, dv_ref
):
    length, width = q_ref.shape
    scale = 1.0 / math.sqrt(HD)
    dk_ref[...] = jnp.zeros_like(dk_ref)
    dv_ref[...] = jnp.zeros_like(dv_ref)

    def step(t, _):
        rows = pl.ds(pl.multiple_of(t * tile, tile), tile)
        same = sc_ref[:, 0:1] == sr_ref[:, rows]
        for h in range(width // HD):
            cols = slice(h * HD, h * HD + HD)
            keys, q_rows, d_rows = k_ref[:, cols], q_ref[rows, cols], d_ref[rows, cols]
            delta = jnp.sum(
                (d_rows.astype(F32) * o_ref[rows, cols].astype(F32)).T, axis=0, keepdims=True
            )
            scores = dg(keys, q_rows, 1, 1) * scale
            prob = jnp.where(same, jnp.exp(scores - l_ref[0, h : h + 1, rows]), 0.0)
            d_prob = dg(v_ref[:, cols], d_rows, 1, 1)
            d_score = (prob * (d_prob - delta) * scale).astype(BF16)
            dv_ref[:, cols] += dg(prob.astype(BF16), d_rows, 1, 0)
            dk_ref[:, cols] += dg(d_score, q_rows, 1, 0)
            dq_ref[rows, cols] = dg(d_score, keys, 0, 0)
        return 0

    lax.fori_loop(0, length // tile, step, 0)


def attend_back(qkv, d_mixed, mixed, stats_in, segments):
    length = qkv.shape[0]
    pairs = qkv.shape[1] // 3 // (2 * HD)
    col, stats, seg_row, seg_col = attend_specs(length, pairs)
    return pl.pallas_call(
        functools.partial(attend_back_kernel, min(512, length)),
        name="attend_back",
        grid=(pairs,),
        in_specs=[col(0), col(1), col(2), col(0), col(0), stats, seg_row, seg_col],
        out_specs=[col(0)] * 3,
        out_shape=[jax.ShapeDtypeStruct((length, pairs * 2 * HD), F32)] * 3,
        cost_estimate=pl.CostEstimate(
            flops=20 * length * length * HD * pairs, bytes_accessed=8 * length * pairs * 256, transcendentals=0
        ),
    )(qkv, qkv, qkv, d_mixed, mixed, stats_in, segments, jnp.broadcast_to(segments.reshape(length, 1), (length, 128)))


def time_features(step_ids, model_width):
    half_width = model_width // 2
    frequency = jnp.exp(
        jnp.arange(half_width, dtype=F32) * (-math.log(10000.0) / half_width)
    )
    angles = step_ids.astype(F32)[:, None] * frequency[None, :]
    return jnp.concatenate([jnp.sin(angles), jnp.cos(angles)], axis=1)


def normalize(array_in):
    row_mean = jnp.mean(array_in, axis=-1, keepdims=True)
    centered = array_in - row_mean
    variance = jnp.mean(centered * centered, axis=-1, keepdims=True)
    inv_std = lax.rsqrt(variance + eps)
    return (centered * inv_std, inv_std)


def norm_back(grad_rows, unit_rows, inv_std, gain_row):
    d_unit = grad_rows * gain_row
    return inv_std * (
        d_unit
        - jnp.mean(d_unit, axis=-1, keepdims=True)
        - unit_rows * jnp.mean(d_unit * unit_rows, axis=-1, keepdims=True)
    )


def ein(spec, left, right):
    return jnp.einsum(spec, left, right, preferred_element_type=F32)


def on_device(
    hidden_in,
    segments,
    timesteps,
    time_weight,
    qkv_weight,
    out_weight,
    in_weight,
    down_weight,
    biases,
    gains,
    ffn_bias,
    out_grad,
    *,
    dp,
    mp,
):
    own_rows, width = hidden_in.shape
    length = segments.shape[1]
    rows = time_weight.shape[0]
    cols = qkv_weight.shape[2]
    hidden = in_weight.shape[1]
    dp_index, mp_index = lax.axis_index("dp"), lax.axis_index("mp")
    fast = (dp, mp) == (16, 2)

    bias_count = biases.shape[0] + gains.shape[0]
    v_shard = jnp.concatenate(
        [qkv_weight[0], qkv_weight[1], qkv_weight[2], biases.T, gains.T, jnp.zeros((rows, 128 - bias_count), BF16)],
        axis=1,
    )
    feature = time_features(timesteps, width).astype(BF16)
    few_row = jnp.concatenate([feature.astype(F32), ffn_bias.astype(F32)[None]], axis=1)
    seg_col = jnp.broadcast_to(segments.reshape(length, 1), (length, 128))
    if fast:
        (
            v_all, o_all, i_all, d_all, few, par, time_row, embed_low, qkv, mixed_heads, mixed_far,
            stats, unit_one, inv_one, middle_low, hidden_act, slope,
        ) = forward(
            v_shard, time_weight, few_row, biases[:1], out_weight.T, in_weight, down_weight.T,
            hidden_in, segments, seg_col,
        )
        few = few.reshape(dp, -1)
        inv_one = inv_one[:, :1]
    else:
        v_all = lax.all_gather(v_shard, "dp", axis=0)
        o_all, i_all, d_all = (
            lax.all_gather(lax.all_gather(a, "dp", axis=0), "mp", axis=0)
            for a in (out_weight.T, in_weight, down_weight.T)
        )
        few = lax.all_gather(few_row, "dp", axis=0, tiled=True)
        time_w = lax.all_gather(time_weight, "dp", axis=0, tiled=True)
    v_raw, v_all = v_all, v_all.reshape(width, -1)
    o_all, i_all, d_all = (a.reshape(mp, width, -1) for a in (o_all, i_all, d_all))
    qkv_w = v_all[:, : 3 * cols]
    column = mp_index * cols
    if fast:
        bias_all, gain_all = par[:7], par[7:9]
        middle = unit_one * gain_all[0] + bias_all[4]
    else:
        params = v_all[:, 3 * cols :].astype(F32).T
        bias_all, gain_all = params[:7], params[7:9]
        time_row = jnp.dot(feature, time_w, preferred_element_type=F32) + bias_all[0]
        h_all = lax.all_gather(hidden_in, "mp", axis=0, tiled=True)
        embedded = hidden_in.astype(F32) + time_row
        embed_low = (h_all.astype(F32) + time_row).astype(BF16)
        bias_qkv = jnp.concatenate(
            [
                lax.dynamic_slice_in_dim(bias_all[1], column, cols),
                jnp.zeros((cols,), F32),
                lax.dynamic_slice_in_dim(bias_all[2], column, cols),
            ]
        )
        qkv = (jnp.dot(embed_low, qkv_w, preferred_element_type=F32) + bias_qkv).astype(BF16)
        mixed_heads, stats = attend(qkv, segments)
        mixed = lax.all_to_all(mixed_heads.reshape(mp, own_rows, cols), "mp", 0, 0, tiled=True)
        attn_total = ein("yrk,ynk->rn", mixed, o_all)
        unit_one, inv_one = normalize(embedded + attn_total + bias_all[3])
        middle = unit_one * gain_all[0] + bias_all[4]
        middle_low = middle.astype(BF16)
        ffn_b = few[:, width:].reshape(mp, hidden)
        pre_act = ein("rd,ydf->yrf", middle_low, i_all) + ffn_b[:, None, :]
        below = 0.5 + 0.5 * lax.erf(pre_act * math.sqrt(0.5))
        hidden_act = (pre_act * below).astype(BF16)
        slope = below + pre_act * jnp.exp(-0.5 * pre_act * pre_act) * (1.0 / math.sqrt(2.0 * math.pi))

    ffn_total = ein("yrf,ynf->rn", hidden_act, d_all)
    unit_two, inv_two = normalize(middle + ffn_total + bias_all[5])
    layer_out = (unit_two * gain_all[1] + bias_all[6]).astype(BF16)

    grad_out = out_grad.astype(F32)
    gain_two_part = jnp.sum(grad_out * unit_two, axis=0)
    shift_two_part = jnp.sum(grad_out, axis=0)
    d_pre_two = norm_back(grad_out, unit_two, inv_two, gain_all[1])
    bias_five_part = jnp.sum(d_pre_two, axis=0)
    d_ffn = d_pre_two.astype(BF16)
    d_act = ein("rn,ynf->yrf", d_ffn, d_all)
    d_pre_act = d_act * slope.astype(F32)
    ffn_bias_part = jnp.sum(d_pre_act, axis=1).reshape(-1, width)
    d_pre_low = d_pre_act.astype(BF16)
    d_middle = d_pre_two + ein("yrf,ydf->rd", d_pre_low, i_all)
    gain_one_part = jnp.sum(d_middle * unit_one, axis=0)
    shift_one_part = jnp.sum(d_middle, axis=0)
    d_pre_one = norm_back(d_middle, unit_one, inv_one, gain_all[0])
    bias_three_part = jnp.sum(d_pre_one, axis=0)
    d_attn = d_pre_one.astype(BF16)
    d_mix = ein("rn,ynk->yrk", d_attn, o_all).astype(BF16)
    zero_row = jnp.zeros((width,), F32)
    sums = [bias_three_part, shift_one_part, bias_five_part, shift_two_part, gain_one_part, gain_two_part]

    def pad_rows(a):
        return jnp.pad(a, ((0, -a.shape[0] % 8), (0, 0)))

    if fast:
        small = jnp.concatenate([jnp.zeros((dp + 2, width), F32), jnp.stack(sums), ffn_bias_part], axis=0)
        v_sum, o_sum, i_sum, d_sum, d_near, d_far, small = backward(
            d_ffn, middle_low, d_attn, hidden_act, d_pre_low, d_mix, qkv.reshape(mp, own_rows, -1),
            embed_low.reshape(v_raw.shape[:4] + (width,)), v_raw, mixed_far, mixed_heads, stats, segments, seg_col,
            pad_rows(small),
        )
        d_own = d_near.astype(F32) + d_far.astype(F32)
        qkv_grad = v_sum.reshape(2, rows, 3, -1).transpose(2, 1, 0, 3).reshape(3, rows, cols)
    else:
        embed_low = embed_low.reshape(length, width)
        mixed_heads = mixed_heads.reshape(length, cols)
        down_grad = ein("rn,yrf->ynf", d_ffn, hidden_act).astype(BF16)
        in_grad = ein("rd,yrf->ydf", middle_low, d_pre_low).astype(BF16)
        out_grad_t = ein("rn,yrk->ynk", d_attn, mixed).astype(BF16)
        d_mixed = lax.all_to_all(d_mix, "mp", 0, 0, tiled=True).reshape(length, cols)
        d_q, d_k, d_v = attend_back(qkv, d_mixed, mixed_heads, stats, segments)
        d_qkv = jnp.concatenate([d_q, d_k, d_v], axis=1).astype(BF16)
        v_grad = dg(embed_low, d_qkv, 0, 0).astype(BF16)
        d_embed = dg(d_qkv, qkv_w, 1, 1)
        time_part = bias_three_part + jnp.sum(d_embed, axis=0)
        d_embed = d_embed.astype(BF16).reshape(mp, own_rows, width)
        seq_rows = jnp.where(jnp.arange(dp)[:, None] == dp_index, time_part[None, :], 0.0)
        spread = [lax.dynamic_update_slice_in_dim(zero_row, jnp.sum(a, axis=0), column, 0) for a in (d_q, d_v)]
        small = pad_rows(jnp.concatenate([seq_rows, jnp.stack(spread + sums), ffn_bias_part], axis=0))
        v_sum = lax.psum_scatter(v_grad, "dp", scatter_dimension=0, tiled=True).astype(F32)

        def both(a):
            a = lax.psum_scatter(a, "mp", scatter_dimension=0)
            return lax.psum_scatter(a, "dp", scatter_dimension=0, tiled=True).astype(F32)

        o_sum, i_sum, d_sum = both(out_grad_t), both(in_grad), both(down_grad)
        d_own = lax.psum_scatter(d_embed, "mp", scatter_dimension=0).astype(F32).reshape(own_rows, width)
        small = lax.psum(small, ("dp", "mp"))
        qkv_grad = v_sum.reshape(rows, 3, cols).transpose(1, 0, 2)

    input_grad = (d_pre_one.reshape(d_own.shape) + d_own).reshape(own_rows, width)
    d_time = small[:dp]
    start = dp_index * rows
    features = few[:, :width]
    features = lax.dynamic_slice_in_dim(features, start, rows, axis=1)
    time_grad = lax.dot_general(
        features, d_time, (((0,), (0,)), ((), ())), precision=lax.Precision.HIGHEST
    )
    tail = small[dp:]
    bias_rows = jnp.concatenate([jnp.sum(d_time, axis=0)[None], tail[:6]], axis=0)
    bias_grad = lax.dynamic_slice_in_dim(bias_rows, start, rows, axis=1)
    gain_grad = lax.dynamic_slice_in_dim(tail[6:8], start, rows, axis=1)
    ffn_rows = ffn_bias.shape[0]
    ffn_all = tail[8:].reshape(-1)
    ffn_bias_grad = lax.dynamic_slice_in_dim(ffn_all, dp_index * ffn_rows, ffn_rows)
    return (
        layer_out,
        input_grad,
        time_grad,
        qkv_grad,
        o_sum.T,
        i_sum,
        d_sum.T,
        bias_grad,
        gain_grad,
        ffn_bias_grad,
    )


def solution(mesh):
    dp, mp = mesh.shape["dp"], mesh.shape["mp"]
    placed = (
        P(("dp", "mp"), None),
        P("dp", None),
        P("dp"),
        P("dp", None),
        P(None, "dp", "mp"),
        P("mp", "dp"),
        P("dp", "mp"),
        P("mp", "dp"),
        P(None, "dp"),
        P(None, "dp"),
        P("dp"),
        P(("dp", "mp"), None),
    )
    return jax.shard_map(
        functools.partial(on_device, dp=dp, mp=mp),
        mesh=mesh,
        in_specs=placed,
        out_specs=(
            P(("dp", "mp"), None),
            P(("dp", "mp"), None),
            P("dp", None),
            P(None, "dp", "mp"),
            P("mp", "dp"),
            P("dp", "mp"),
            P("mp", "dp"),
            P(None, "dp"),
            P(None, "dp"),
            P("dp"),
        ),
        check_vma=False,
    )
```
